32 devices in a mesh: dp: 8 (over y, x, core), tensor: 4 (over z).
Axes of the slice: x: 2, y: 2, z: 4, core: 2. Of those that a mesh axis runs over, the one named last changes fastest.
Arguments:
- x_in: bfloat16 [16384, 640], P(('dp', 'tensor')), may hold values from -6 to 6
- cotangent: bfloat16 [16384, 640], P(('dp', 'tensor')), may hold values from -6 to 6
- lengths: int32 [8, 8], P('dp'), may hold values from 0 to 1024, as said below
- bucket_ids: int32 [8], P('dp'), may hold values from 0 to 2, as said below
- bucket_weights: float32 [3], replicated, may hold values from 0.5 to 2
- ln1_gain: float32 [640], replicated, may hold values from 0.5 to 1.5
- ln1_bias: float32 [640], replicated, may hold values from -1.5 to 1.5
- w_qkv: bfloat16 [3, 640, 640], P(None, None, 'tensor'), may hold values from -0.25 to 0.25
- qv_bias: float32 [2, 640], P(None, 'tensor'), may hold values from -1.5 to 1.5
- w_out: bfloat16 [640, 640], P('tensor'), may hold values from -2.5 to 2.5
- b_out: float32 [640], replicated, may hold values from -1.5 to 1.5
- ln2_gain: float32 [640], replicated, may hold values from 0.5 to 1.5
- ln2_bias: float32 [640], replicated, may hold values from -1.5 to 1.5
- w_up: bfloat16 [640, 5120], P(None, 'tensor'), may hold values from -0.25 to 0.25
- b_up: float32 [5120], P('tensor'), may hold values from -1.5 to 1.5
- w_down: bfloat16 [5120, 640], P('tensor'), may hold values from -0.078125 to 0.078125
- b_down: float32 [640], replicated, may hold values from -1.5 to 1.5
Outputs:
- layer_out: bfloat16 [16384, 640], P(('dp', 'tensor'))
- x_grad: float32 [16384, 640], P(('dp', 'tensor'))
- ln1_gain_grad: float32 [640], replicated
- ln1_bias_grad: float32 [640], replicated
- w_qkv_grad: float32 [3, 640, 640], P(None, None, 'tensor')
- qv_bias_grad: float32 [2, 640], P(None, 'tensor')
- w_out_grad: float32 [640, 640], P('tensor')
- b_out_grad: float32 [640], replicated
- ln2_gain_grad: float32 [640], replicated
- ln2_bias_grad: float32 [640], replicated
- w_up_grad: float32 [640, 5120], P(None, 'tensor')
- b_up_grad: float32 [5120], P('tensor')
- w_down_grad: float32 [5120, 640], P('tensor')
- b_down_grad: float32 [640], replicated
The draws below stay inside these ranges and needn't reach their ends.
Inputs may be any that keep to these rules, and one draw needn't show every extreme that they name: `bucket_ids`: every bucket 0, 1 and 2 is held by some index of dp. `lengths`: with span s = 256, 512, 1024 for bucket 0, 1, 2 of index i, entries j < 2048 / s of row i lie between s / 4 and s, entry 0 equals s; later entries are 0.
All inputs are finite; a program needn't handle non-finite values.
Results may differ from the reference program's by a relative error of at most 0.02.
Values may be sent and summed in bfloat16 or wider, within the bound.
A program may use at most 192 MiB of HBM per device.

```python
import math
import jax
import jax.numpy as jnp
from jax import lax

D = 640
HEADS = 20
HD = 32
FF = 5120
BUCKET = 256
ROWS = 2048
SLOTS = 8
TOKENS = 16384
N_DP = 8


def bucket_law(key):
    order = jax.random.permutation(jax.random.fold_in(key, 11), N_DP)
    return (order % 3).astype(jnp.int32)


def draw_bucket_ids(key, part):
    return bucket_law(key)


def draw_lengths(key, part):
    bucket = bucket_law(key)
    span = jnp.where(bucket == 0, BUCKET, jnp.where(bucket == 1, 2 * BUCKET, 4 * BUCKET)).astype(jnp.int32)[:, None]
    raw = jax.random.randint(jax.random.fold_in(key, 23), (N_DP, SLOTS), 0, 1 << 20)
    least = span // 4
    length = least + raw % (span - least + 1)
    slot = jnp.arange(SLOTS, dtype=jnp.int32)[None, :]
    length = jnp.where(slot == 0, span, length)
    return jnp.where(slot < ROWS // span, length, 0).astype(jnp.int32)


def levels(own_key, shape, cuts, low, top_value):
    loudness, own = 1.0, jax.random.fold_in(own_key, 6)
    for position, parts in cuts:
        draws = jnp.exp(jax.random.uniform(jax.random.fold_in(own, position), (parts,), jnp.float32, low / len(cuts), top_value / len(cuts)))
        loudness = loudness * jnp.repeat(draws, shape[position] // parts).reshape([-1 if axis == position else 1 for axis in range(len(shape))])
    return loudness


def noise(rng, extent, width, bound, shards=(), kind=jnp.bfloat16):
    factor_of = levels(rng, extent, shards, -0.22, 0.18) if shards else 1.0
    values = jax.random.normal(rng, extent, jnp.float32) * width * factor_of
    return jnp.minimum(jnp.maximum(values, -bound), bound).astype(kind)


def setup_inputs(seed: int = 0) -> dict:
    seeds = jax.random.split(jax.random.key(seed), 18)
    x_in = noise(seeds[0], (TOKENS, D), 1.0, 6.0, ((0, 32),))
    cotangent = noise(seeds[1], (TOKENS, D), 1.0, 6.0, ((0, 32),))
    lengths = draw_lengths(jax.random.fold_in(seeds[17], 71), 0)
    bucket_ids = draw_bucket_ids(jax.random.fold_in(seeds[17], 71), 0)
    bucket_weights = jnp.clip(jnp.exp(jax.random.uniform(seeds[4], (3,), jnp.float32, math.log(0.5), math.log(2.0))), 0.5, 2.0)
    ln1_gain = jnp.clip(1.0 + 0.1 * jax.random.normal(seeds[5], (D,), jnp.float32), 0.5, 1.5)
    ln1_bias = noise(seeds[6], (D,), 0.3, 1.5, (), jnp.float32)
    w_qkv = noise(seeds[7], (3, D, D), D ** -0.5, 0.25, ((2, 4),))
    qv_bias = noise(seeds[8], (2, D), 0.3, 1.5, ((1, 4),), jnp.float32)
    w_out = noise(seeds[9], (D, D), (max(D // 128, 1)) ** -0.5, 2.5, ((0, 4),))
    b_out = noise(seeds[10], (D,), 0.3, 1.5, (), jnp.float32)
    ln2_gain = jnp.clip(1.0 + 0.1 * jax.random.normal(seeds[11], (D,), jnp.float32), 0.5, 1.5)
    ln2_bias = noise(seeds[12], (D,), 0.3, 1.5, (), jnp.float32)
    w_up = noise(seeds[13], (D, FF), D ** -0.5, 0.25, ((1, 4),))
    b_up = noise(seeds[14], (FF,), 0.3, 1.5, ((0, 4),), jnp.float32)
    w_down = noise(seeds[15], (FF, D), FF ** -0.5, 0.078125, ((0, 4),))
    b_down = noise(seeds[16], (D,), 0.3, 1.5, (), jnp.float32)
    return dict(x_in=x_in, cotangent=cotangent, lengths=lengths, bucket_ids=bucket_ids, bucket_weights=bucket_weights, ln1_gain=ln1_gain, ln1_bias=ln1_bias, w_qkv=w_qkv, qv_bias=qv_bias, w_out=w_out, b_out=b_out, ln2_gain=ln2_gain, ln2_bias=ln2_bias, w_up=w_up, b_up=b_up, w_down=w_down, b_down=b_down)


@jax.custom_vjp
def low(v):
    return lax.optimization_barrier(v.astype(jnp.bfloat16)).astype(jnp.float32)

@jax.custom_vjp
def low_back(v):
    return v

def low_keep(v):
    return (low(v), None)

def low_pass(kept, grad):
    return (grad,)

def back_keep(v):
    return (v, None)

def back_low(kept, grad):
    return (low(grad),)
low.defvjp(low_keep, low_pass)
low_back.defvjp(back_keep, back_low)
EPSILON = 1e-05
HIGH = lax.Precision.HIGHEST

def layer_norm(values, gain, shift):
    centre = values - lax.optimization_barrier(jnp.mean(values, axis=-1, keepdims=True))
    scale_inv = lax.rsqrt(lax.optimization_barrier(jnp.mean(centre * centre, axis=-1, keepdims=True)) + EPSILON)
    return centre * scale_inv * gain + shift

def matmul(left, right):
    return jnp.dot(left, right, precision=HIGH, preferred_element_type=jnp.float32)

def row_tables(lengths, bucket_ids, bucket_weights):
    row_pos = jnp.arange(TOKENS, dtype=jnp.int32)
    owner = row_pos // ROWS
    place = row_pos % ROWS
    bucket_row = bucket_ids[owner]
    span = jnp.where(bucket_row == 0, BUCKET, jnp.where(bucket_row == 1, 2 * BUCKET, 4 * BUCKET)).astype(jnp.int32)
    item_ids = (owner * SLOTS + place // span).astype(jnp.int32)
    live = place % span < lengths.reshape(-1)[item_ids]
    row_weight = jnp.where(live, bucket_weights[bucket_row], 0.0).astype(jnp.float32)
    return (item_ids, live, row_weight)

def attend(queries, key_rows, value_rows, item_ids, live):
    block = 2 * BUCKET
    window = 4 * BUCKET
    factor = HD ** (-0.5)

    def one_block(index):
        start = index * block
        wstart = start // window * window
        query_b = lax.dynamic_slice_in_dim(queries, start, block, 0)
        key_b = lax.dynamic_slice_in_dim(key_rows, wstart, window, 0)
        value_b = lax.dynamic_slice_in_dim(value_rows, wstart, window, 0)
        item_q = lax.dynamic_slice_in_dim(item_ids, start, block, 0)
        item_k = lax.dynamic_slice_in_dim(item_ids, wstart, window, 0)
        live_k = lax.dynamic_slice_in_dim(live, wstart, window, 0)
        scores = low_back(jnp.einsum('qhd,khd->hqk', query_b, key_b, precision=HIGH) * factor)
        allowed = (item_q[:, None] == item_k[None, :]) & live_k[None, :]
        masked = jnp.where(allowed[None], scores, -1e+30)
        top = lax.optimization_barrier(jnp.max(masked, axis=-1, keepdims=True))
        expo = jnp.exp(masked - top)
        probs = expo / lax.optimization_barrier(jnp.sum(expo, axis=-1, keepdims=True))
        return jnp.einsum('hqk,khd->qhd', low(probs), value_b, precision=HIGH)
    blocks = lax.map(jax.checkpoint(one_block), jnp.arange(TOKENS // block, dtype=jnp.int32))
    return blocks.reshape(TOKENS, HEADS * HD)

def reference(x_in, cotangent, lengths, bucket_ids, bucket_weights, ln1_gain, ln1_bias, w_qkv, qv_bias, w_out, b_out, ln2_gain, ln2_bias, w_up, b_up, w_down, b_down):
    item_ids, live, row_weight = row_tables(lengths, bucket_ids, bucket_weights)

    def forward(x_f, g_one, s_one, qkv_f, qvb_f, wout_f, bout_f, g_two, s_two, up_f, bup_f, down_f, bdown_f):
        normed = low(layer_norm(x_f, g_one, s_one))
        queries = low_back(low(matmul(normed, qkv_f[0]) + qvb_f[0]))
        key_rows = low_back(low(matmul(normed, qkv_f[1])))
        value_rows = low_back(low(matmul(normed, qkv_f[2]) + qvb_f[1]))
        shape = (TOKENS, HEADS, HD)
        mixed = low_back(low(attend(queries.reshape(shape), key_rows.reshape(shape), value_rows.reshape(shape), item_ids, live)))
        middle = x_f + low_back(matmul(mixed, wout_f) + bout_f)
        normed2 = low(layer_norm(middle, g_two, s_two))
        hidden = low_back(matmul(normed2, up_f) + bup_f)
        active = low(jax.nn.gelu(hidden, approximate=False))
        return middle + low_back(matmul(active, down_f) + bdown_f)
    result, pullback = jax.vjp(forward, x_in.astype(jnp.float32), ln1_gain, ln1_bias, w_qkv.astype(jnp.float32), qv_bias, w_out.astype(jnp.float32), b_out, ln2_gain, ln2_bias, w_up.astype(jnp.float32), b_up, w_down.astype(jnp.float32), b_down)
    grads = pullback(cotangent.astype(jnp.float32) * row_weight[:, None])
    return (result.astype(jnp.bfloat16), grads[0], grads[1], grads[2], grads[3], grads[4], grads[5], grads[6], grads[7], grads[8], grads[9], grads[10], grads[11], grads[12])
```

```python
import functools
import math

import jax
import jax.numpy as jnp
from jax import lax
from jax.experimental import pallas as pl
from jax.experimental.pallas import tpu as pltpu
from jax.sharding import PartitionSpec as P

HD = 32
BUCKET = 256
EPSILON = 1e-05
GROUP = 8
BLK = 256
BIG = 1e30
F32 = jnp.float32
BF16 = jnp.bfloat16
MESH = pl.DeviceIdType.MESH
RSQRT2 = 1.0 / math.sqrt(2.0)
RSQRT2PI = 1.0 / math.sqrt(2.0 * math.pi)
SLOTS_C = 2
G_LAG1 = 8
G_LAG2 = 5


def nn(a, b):
    return lax.dot_general(a, b, (((1,), (0,)), ((), ())), preferred_element_type=F32)


def nt(a, b):
    return lax.dot_general(a, b, (((1,), (1,)), ((), ())), preferred_element_type=F32)


def unit_of(values):
    centre = values - jnp.mean(values, axis=-1, keepdims=True)
    scale_inv = lax.rsqrt(jnp.mean(centre * centre, axis=-1, keepdims=True) + EPSILON)
    return centre * scale_inv, scale_inv


def norm_back(grad, unit, scale_inv, gain):
    scaled = grad * gain
    return scale_inv * (
        scaled
        - jnp.mean(scaled, axis=-1, keepdims=True)
        - unit * jnp.mean(scaled * unit, axis=-1, keepdims=True)
    )


def lanes(shape):
    return lax.broadcasted_iota(jnp.int32, shape, 1)


def kernel(
    x_ref,
    cot_ref,
    len_ref,
    bid_ref,
    bw_ref,
    g1_ref,
    s1_ref,
    wqkv_ref,
    qvb_ref,
    wout_ref,
    bout_ref,
    g2_ref,
    s2_ref,
    wup_ref,
    bup_ref,
    wdn_ref,
    bdn_ref,
    lo_ref,
    xg_ref,
    of_ref,
    oa_ref,
    osm_ref,
    ph_ref,
    fg,
    aw,
    rc_f,
    r2_f,
    r1_f,
    rz_f,
    rc_a,
    r2_a,
    r1_a,
    rz_a,
    xn,
    xp,
    qb,
    kb,
    vb,
    mx,
    dob,
    dd,
    pst,
    mid,
    acc0,
    acc1,
    uu,
    ol,
    olt,
    xnt,
    ngs,
    ngr,
    bupa,
    qvba,
    early,
    late,
    e_rx,
    e_rz,
    l_rx,
    l_rz,
    loc_sem,
    ps_sem,
    za_s,
    za_r,
    zx_sem,
    zb_s,
    zb_r,
    ga_s,
    ga_r,
    zf_s,
    zf_r,
    gf_s,
    gf_r,
    cf_s,
    cf_r,
    f2_s,
    f2_r,
    f1_s,
    f1_r,
    fz_s,
    fz_r,
    af_s,
    af_r,
    ca_s,
    ca_r,
    a2_s,
    a2_r,
    a1_s,
    a1_r,
    az_s,
    az_r,
    aa_s,
    aa_r,
    sm_s,
    sm_r,
    ng_sem,
    credit,
):
    share, width = x_ref.shape
    hw = wqkv_ref.shape[2]
    heads = hw // HD
    qkvw = 3 * hw
    parts = 4
    nblk = wup_ref.shape[1] // BLK
    piece = width // GROUP
    keys = 2 * share
    factor = HD ** (-0.5)
    q_scale = factor * math.log2(math.e)

    d = lax.axis_index("dp")
    t = lax.axis_index("tensor")
    c = d % 2
    bx = (d // 2) % 2
    by = (d // 4) % 2
    dev_c = (d + 1 - 2 * c, t)
    dx = d + 2 - 4 * bx
    dy = d + 4 - 8 * by
    tp = t + 1 - 2 * (t % 2)

    def far(k):
        return (t + k) % parts

    def route(par):
        low = bx + par * (by - bx)
        high = by + par * (bx - by)
        first = (dx + par * (dy - dx), t)
        second = (dy + par * (dx - dy), t)
        return low, high, first, second

    def rcopy(src, dst, ssem, rsem, dev):
        return pltpu.make_async_remote_copy(
            src_ref=src, dst_ref=dst, send_sem=ssem, recv_sem=rsem, device_id=dev, device_id_type=MESH
        )

    def rows(start, size):
        return pl.ds(pl.multiple_of(start, 16), size)

    def up_load(j):
        return pltpu.make_async_copy(
            wup_ref.at[:, pl.ds(j * BLK, BLK)], fg.at[t * nblk + j, 0], loc_sem.at[j]
        )

    def dn_load(j):
        return pltpu.make_async_copy(
            wdn_ref.at[pl.ds(j * BLK, BLK), :],
            uu.at[j // 2, pl.ds((j % 2) * BLK, BLK), :],
            loc_sem.at[nblk + j],
        )

    for j in range(nblk):
        up_load(j).start()
        dn_load(j).start()
    cot_load = pltpu.make_async_copy(cot_ref, ol, loc_sem.at[2 * nblk])
    cot_load.start()

    aw[t, :, 0:hw] = wqkv_ref[0]
    aw[t, :, hw : 2 * hw] = wqkv_ref[1]
    aw[t, :, 2 * hw : 3 * hw] = wqkv_ref[2]
    aw[t, :, 3 * hw : 4 * hw] = wout_ref[...].T

    barrier = pltpu.get_barrier_semaphore()
    for dev in (dev_c, (dx, t), (dy, t), (d, far(1)), (d, far(2)), (d, far(3))):
        pl.semaphore_signal(barrier, inc=1, device_id=dev, device_id_type=MESH)
    pl.semaphore_wait(barrier, 6)

    low_a, high_a, first_a, second_a = route(t % 2)
    pos_own_a = (c * 4 + high_a * 2 + low_a) * piece

    def za(k):
        view = aw.at[t, rows(pos_own_a, piece), :]
        return rcopy(view, view, za_s.at[k - 1], za_r.at[t], (d, far(parts - k)))

    def za_wait(s, par):
        low, high, _, _ = route(par)
        view = aw.at[s, rows((c * 4 + high * 2 + low) * piece, piece), :]
        rcopy(view, view, za_s.at[0], za_r.at[s], (d, t)).wait_recv()

    def zb(k, which):
        src = bup_ref if which == 0 else qvb_ref
        dst = (bupa if which == 0 else qvba).at[t]
        return rcopy(src, dst, zb_s.at[2 * (k - 1) + which], zb_r.at[which, t], (d, far(parts - k)))

    def zb_wait(s, which):
        src = bup_ref if which == 0 else qvb_ref
        dst = (bupa if which == 0 else qvba).at[s]
        rcopy(src, dst, zb_s.at[0], zb_r.at[which, s], (d, t)).wait_recv()

    x_copy = rcopy(x_ref, xp, zx_sem.at[0], zx_sem.at[1], (d, tp))

    for k in range(1, parts):
        za(k).start()
        zb(k, 1).start()
    x_copy.start()
    for k in range(1, parts):
        zb(k, 0).start()
    bupa[t] = bup_ref[...]
    qvba[t] = qvb_ref[...]

    gain1 = g1_ref[...]
    shift1 = s1_ref[...]
    unit, _ = unit_of(x_ref[...].astype(F32))
    normed = (unit * gain1 + shift1).astype(BF16)
    xn[0:share, :] = normed
    xnt[:, 0:share] = normed.T

    bucket = bid_ref[0]
    span = jnp.where(bucket == 0, BUCKET, jnp.where(bucket == 1, 2 * BUCKET, 4 * BUCKET))
    weight = jnp.where(bucket == 0, bw_ref[0], jnp.where(bucket == 1, bw_ref[1], bw_ref[2]))

    def slot_info(base, shape):
        place = base + lax.broadcasted_iota(jnp.int32, shape, 0)
        item = jnp.zeros(shape, jnp.int32)
        for j in range(1, len_ref.shape[1]):
            item = item + jnp.where(place >= j * span, 1, 0)
        length = jnp.zeros(shape, jnp.int32)
        for j in range(len_ref.shape[1]):
            length = jnp.where(item == j, len_ref[0, j], length)
        return item, (place - item * span) < length

    wide = (share, 2 * 128)
    lane = lanes(wide)
    slots = len_ref.shape[1]
    in_aux = (lane >= hw) & (lane < hw + slots)
    one_aux = jnp.where(lane >= hw, 1.0, 0.0).astype(BF16)

    own_item, own_live = slot_info(t * share, wide)
    q_aux = jnp.where(in_aux & (own_item == lane - hw), 1.0, 0.0).astype(BF16)
    k_aux0 = jnp.where(in_aux & ~((own_item == lane - hw) & own_live), -BIG, 0.0).astype(BF16)
    pair_item, pair_live = slot_info(tp * share, wide)
    k_aux1 = jnp.where(in_aux & ~((pair_item == lane - hw) & pair_live), -BIG, 0.0).astype(BF16)
    for s in range(parts):
        qb[s] = q_aux
        kb[s, 0:share] = k_aux0
        kb[s, share:keys] = k_aux1
        vb[s, 0:share] = one_aux
        vb[s, share:keys] = one_aux
    _, live1 = slot_info(t * share, (share, 128))
    row_weight = jnp.where(live1, weight, 0.0)[:, 0:1]

    def zf(k, j):
        low, high, _, _ = route((t + j) % 2)
        view = fg.at[t * nblk + j, :, rows((c * 4 + high * 2 + low) * piece, piece), :]
        return rcopy(
            view, view, zf_s.at[(k - 1) * nblk + j], zf_r.at[t * nblk + j], (d, far(parts - k))
        )

    for j in range(nblk):
        up_load(j).wait()
        dn_load(j).wait()
        fg[t * nblk + j, 1] = uu[j // 2, (j % 2) * BLK : (j % 2 + 1) * BLK, :].T
    for k in range(1, parts):
        for j in range(nblk):
            zf(k, j).start()

    def ga(stage, s):
        low, high, first, second = route(s % 2)
        if stage == 0:
            view, dev = aw.at[s, rows((c * 4 + high * 2 + low) * piece, piece), :], first
        elif stage == 1:
            view, dev = aw.at[s, rows((c * 4 + high * 2) * piece, 2 * piece), :], second
        else:
            view, dev = aw.at[s, rows(c * 4 * piece, 4 * piece), :], dev_c
        return rcopy(view, view, ga_s.at[stage, s], ga_r.at[stage, s], dev)

    def project(s, base, own):
        bias_q = qvba[s, 0:1, :]
        bias_v = qvba[s, 1:2, :]
        out = nn(xn[base : base + share, :], aw[s, :, 0:qkvw])
        if own:
            qb[s, :, 0:hw] = ((out[:, 0:hw] + bias_q) * q_scale).astype(BF16)
        kb[s, base : base + share, 0:hw] = out[:, hw : 2 * hw].astype(BF16)
        vb[s, base : base + share, 0:hw] = (out[:, 2 * hw : 3 * hw] + bias_v).astype(BF16)

    for k in range(1, parts):
        s = far(k)
        za_wait(s, s % 2)
        ga(0, s).start()
    project(t, 0, True)
    for stage in (1, 2):
        for k in range(1, parts):
            s = far(k)
            ga(stage - 1, s).wait_recv()
            ga(stage, s).start()
    for k in range(1, parts):
        s = far(k)
        zb_wait(s, 1)
        ga(2, s).wait_recv()
        project(s, 0, True)

    x_copy.wait_recv()
    unit, _ = unit_of(xp[...].astype(F32))
    normed = (unit * gain1 + shift1).astype(BF16)
    xn[share:keys, :] = normed
    xnt[:, share:keys] = normed.T

    def pair_project(k, carry):
        project(far(k), share, False)
        return carry

    lax.fori_loop(0, parts, pair_project, 0)

    n_far = (parts - 1) * nblk

    def far_block(m):
        s = (t + 1 + m // nblk) % parts
        j = m % nblk
        return s, j, s * nblk + j

    def gf(stage, m):
        s, j, b = far_block(m)
        low, high, first, second = route((s + j) % 2)
        if stage == 0:
            view, dev = fg.at[b, :, rows((c * 4 + high * 2 + low) * piece, piece), :], first
        elif stage == 1:
            view, dev = fg.at[b, :, rows((c * 4 + high * 2) * piece, 2 * piece), :], second
        else:
            view, dev = fg.at[b, :, rows(c * 4 * piece, 4 * piece), :], dev_c
        return rcopy(view, view, gf_s.at[stage, b], gf_r.at[stage, b], dev)

    def zf_wait(m):
        s, j, b = far_block(m)
        low, high, _, _ = route((s + j) % 2)
        view = fg.at[b, :, rows((c * 4 + high * 2 + low) * piece, piece), :]
        rcopy(view, view, zf_s.at[0], zf_r.at[b], (d, t)).wait_recv()

    def within(n, size):
        return (n >= 0) & (n < size)

    def gather_tick(n):
        @pl.when(within(n, n_far))
        def _():
            zf_wait(n)
            gf(0, n).start()

        @pl.when(within(n - 1, n_far))
        def _():
            gf(0, n - 1).wait_recv()
            gf(1, n - 1).start()

        @pl.when(within(n - 2, n_far))
        def _():
            gf(1, n - 2).wait_recv()
            gf(2, n - 2).start()

    def p_out(s, h, slot):
        return (
            pltpu.make_async_copy(
                pst.at[2 * slot], ph_ref.at[s * heads + h, 0], ps_sem.at[2 * slot]
            ),
            pltpu.make_async_copy(
                pst.at[2 * slot + 1], ph_ref.at[s * heads + h, 1], ps_sem.at[2 * slot + 1]
            ),
        )

    def att_forward(k, carry):
        s = far(k)
        qg = qb[s]
        kg = kb[s]
        vg = vb[s]
        lane_q = lanes((share, 2 * 128))
        out = jnp.zeros((share, 2 * 128), F32)
        for h in range(heads):
            head = (lane_q >= HD * h) & (lane_q < HD * (h + 1))
            qm = jnp.where(head | (lane_q >= hw), qg, jnp.zeros_like(qg))
            scores = nt(qm, kg)
            top = jnp.max(scores, axis=1, keepdims=True)
            probs = jnp.exp2(scores - top).astype(BF16)
            idx = k * heads + h
            slot = idx % 2

            @pl.when(idx >= 2)
            def _():
                for cp in p_out(s, h, slot):
                    cp.wait()

            pst[2 * slot] = probs[:, 0:share]
            pst[2 * slot + 1] = probs[:, share:keys]
            for cp in p_out(s, h, slot):
                cp.start()
            mixed = nn(probs, vg)
            inv_h = 1.0 / mixed[:, hw : hw + 1]
            out = jnp.where(head, mixed * inv_h, out)
            coarse = inv_h.astype(BF16).astype(F32)
            out = jnp.where(lane_q == hw + 2 * h, coarse, out)
            out = jnp.where(lane_q == hw + 2 * h + 1, inv_h - coarse, out)
        mx[s] = out.astype(BF16)
        gather_tick(2 * k)
        gather_tick(2 * k + 1)
        return carry

    lax.fori_loop(0, parts, att_forward, 0)
    for slot in range(2):
        for cp in p_out(0, 0, slot):
            cp.wait()

    branch = jnp.zeros((share, width), F32)
    for s in range(parts):
        branch = branch + nt(mx[s, :, 0:hw], aw[s, :, qkvw : 4 * hw])
    middle = x_ref[...].astype(F32) + (branch + bout_ref[...])
    mid[...] = middle
    unit, _ = unit_of(middle)
    normed = (unit * g2_ref[...] + s2_ref[...]).astype(BF16)
    n2 = uu.at[0, 0:share, :]
    n2t = uu.at[1, :, 0:share]
    n2[...] = normed
    n2t[...] = normed.T
    cot_load.wait()
    low_grad = (ol[...].astype(F32) * row_weight).astype(BF16)
    early[...] = jnp.zeros_like(early)
    late[...] = jnp.zeros_like(late)
    early[3:4, :] = jnp.sum(low_grad.astype(F32), axis=0, keepdims=True)
    ol[...] = low_grad
    olt[...] = low_grad.T
    acc0[...] = jnp.zeros_like(acc0)
    acc1[...] = jnp.zeros_like(acc1)

    for k in range(1, parts):
        zb_wait(far(k), 0)

    n_all = parts * nblk

    def block(r):
        k = r // nblk
        j = r % nblk
        s = (t + k) % parts
        home = s * nblk + j
        own = jnp.where(k == 0, 1, 0)
        return k, j, s, home, home + own * (n_all + j - home)

    def rf(stage, r):
        k, j, s, _, g = block(r)
        low, high, first, second = route((s + j) % 2)
        if stage == 0:
            return rcopy(
                fg.at[g, :, rows((1 - c) * 4 * piece, 4 * piece), :],
                rc_f.at[r % SLOTS_C],
                cf_s.at[r],
                cf_r.at[r],
                dev_c,
            )
        if stage == 1:
            return rcopy(
                fg.at[g, :, rows((c * 4 + (1 - high) * 2) * piece, 2 * piece), :],
                r2_f.at[r],
                f2_s.at[r],
                f2_r.at[r],
                second,
            )
        if stage == 2:
            return rcopy(
                fg.at[g, :, rows((c * 4 + high * 2 + 1 - low) * piece, piece), :],
                r1_f.at[r],
                f1_s.at[r],
                f1_r.at[r],
                first,
            )
        z = jnp.maximum(r - nblk, 0)
        return rcopy(
            fg.at[g, :, rows((c * 4 + high * 2 + low) * piece, piece), :],
            rz_f.at[z],
            fz_s.at[z],
            fz_r.at[z],
            (d, s),
        )

    def add_rows(ref, got):
        ref[...] = (ref[...].astype(F32) + got[...].astype(F32)).astype(BF16)

    def rf_second(r):
        k, j, s, _, g = block(r)
        rf(0, r).wait_recv()
        add_rows(fg.at[g, :, rows(c * 4 * piece, 4 * piece), :], rc_f.at[r % SLOTS_C])

        @pl.when(r < n_all - SLOTS_C)
        def _():
            pl.semaphore_signal(credit, inc=1, device_id=dev_c, device_id_type=MESH)

        rf(1, r).start()

    def rf_first(r):
        k, j, s, _, g = block(r)
        low, high, _, _ = route((s + j) % 2)
        rf(1, r).wait_recv()
        add_rows(fg.at[g, :, rows((c * 4 + high * 2) * piece, 2 * piece), :], r2_f.at[r])
        rf(2, r).start()

    def rf_far(r):
        k, j, s, _, g = block(r)
        low, high, _, _ = route((s + j) % 2)
        rf(2, r).wait_recv()
        add_rows(fg.at[g, :, rows((c * 4 + high * 2 + low) * piece, piece), :], r1_f.at[r])

        @pl.when(r >= nblk)
        def _():
            rf(3, r).start()

    def af(stage, j):
        low, high, first, second = route((t + j) % 2)
        b = t * nblk + j
        if stage == 0:
            view, dev = fg.at[b, :, rows((c * 4 + high * 2 + low) * piece, piece), :], first
        elif stage == 1:
            view, dev = fg.at[b, :, rows((c * 4 + high * 2) * piece, 2 * piece), :], second
        else:
            view, dev = fg.at[b, :, rows(c * 4 * piece, 4 * piece), :], dev_c
        return rcopy(view, view, af_s.at[stage, j], af_r.at[stage, j], dev)

    def f_final(j):
        low, high, _, _ = route((t + j) % 2)
        mine = rows((c * 4 + high * 2 + low) * piece, piece)
        total = fg[n_all + j, :, mine, :].astype(F32)
        for k in range(1, parts):
            z = (k - 1) * nblk + j
            rcopy(rz_f.at[z], rz_f.at[z], fz_s.at[z], fz_r.at[z], (d, t)).wait_recv()
            total = total + rz_f[z].astype(F32)
        fg[t * nblk + j, :, mine, :] = total.astype(BF16)
        af(0, j).start()

    def f_out(j):
        return pltpu.make_async_copy(fg.at[t * nblk + j], of_ref.at[j], loc_sem.at[j])

    def final_tick(n):
        @pl.when(within(n, nblk))
        def _():
            f_final(n)

        @pl.when(within(n - 1, nblk))
        def _():
            af(0, n - 1).wait_recv()
            af(1, n - 1).start()

        @pl.when(within(n - 2, nblk))
        def _():
            af(1, n - 2).wait_recv()
            af(2, n - 2).start()

        @pl.when(within(n - 3, nblk))
        def _():
            af(2, n - 3).wait_recv()
            f_out(n - 3).start()

    def reduce_tick(n):
        @pl.when(within(n, n_all))
        def _():
            rf_second(n)

        @pl.when(within(n - G_LAG1, n_all))
        def _():
            rf_first(n - G_LAG1)

        @pl.when(within(n - G_LAG1 - G_LAG2, n_all))
        def _():
            rf_far(n - G_LAG1 - G_LAG2)

    def drain_zf(m, carry):
        view = fg.at[0, :, 0:piece, :]
        rcopy(view, view, zf_s.at[m], zf_r.at[0], (d, t)).wait_send()
        return carry

    def ffn(r, carry):
        k, j, s, home, g = block(r)

        @pl.when(k > 0)
        def _():
            gf(2, jnp.maximum(r - nblk, 0)).wait_recv()

        wu = fg[home, 0]
        wd = fg[home, 1]
        hidden = nn(n2[...], wu) + bupa[s, :, pl.ds(pl.multiple_of(j * BLK, BLK), BLK)]
        cdf = 0.5 + 0.5 * lax.erf(hidden * RSQRT2)
        slope = cdf + hidden * (jnp.exp(-0.5 * hidden * hidden) * RSQRT2PI)
        active = (hidden * cdf).astype(BF16)
        act_grad = nn(ol[...], wd)
        hid_grad = (slope * act_grad).astype(BF16)
        acc0[...] += nt(active, wd)
        acc1[...] += nt(hid_grad, wu)
        early[pl.ds(4 + home, 1), 0:BLK] = jnp.sum(hid_grad.astype(F32), axis=0, keepdims=True)
        up_grad = nn(n2t[...], hid_grad).astype(BF16)
        dn_grad = nn(olt[...], active).astype(BF16)

        @pl.when(k > 0)
        def _():
            for stage in range(3):
                gf(stage, jnp.maximum(r - nblk, 0)).wait_send()

        fg[g, 0] = up_grad
        fg[g, 1] = dn_grad

        @pl.when(r == 2 * nblk)
        def _():
            lax.fori_loop(0, n_far, drain_zf, 0)

        @pl.when(r >= SLOTS_C)
        def _():
            pl.semaphore_wait(credit, 1)

        rf(0, r).start()
        gather_tick(2 * parts + r)
        reduce_tick(r - 1)
        return carry

    lax.fori_loop(0, n_all, ffn, 0)

    middle = mid[...]
    ngs[...] = (middle + (acc0[...] + bdn_ref[...])).astype(BF16)
    lo_copy = pltpu.make_async_copy(ngs, lo_ref, loc_sem.at[2 * nblk])
    lo_copy.start()
    unit, scale_inv = unit_of(middle)
    got = acc1[...]
    early[0:1, :] = jnp.sum(got * unit, axis=0, keepdims=True)
    early[1:2, :] = jnp.sum(got, axis=0, keepdims=True)
    middle_part = norm_back(got, unit, scale_inv, g2_ref[...])
    reload = pltpu.make_async_copy(cot_ref, ol, loc_sem.at[0])
    reload.start()
    reload.wait()
    out_grad = ol[...].astype(F32) * row_weight
    middle_grad = out_grad + middle_part
    mid[...] = middle_grad
    branch_low = middle_grad.astype(BF16)
    early[2:3, :] = jnp.sum(branch_low.astype(F32), axis=0, keepdims=True)
    branch_t = olt
    ol[...] = branch_low
    branch_t[...] = branch_low.T

    for k in range(1, parts):
        za(k).wait_send()
    for k in range(1, parts):
        for stage in range(3):
            ga(stage, far(k)).wait_send()

    def out_back(k, carry):
        s = far(k)
        mixed = mx[s]
        mixed_grad = nn(ol[...], aw[s, :, qkvw : 4 * hw]).astype(BF16).astype(F32)
        inv = mixed[:, 128:256].astype(F32)
        prod = mixed_grad * mixed[:, 0:hw].astype(F32)
        lane_h = lanes((share, hw))
        lane_q = lanes((share, 2 * 128))
        scaled = jnp.zeros((share, hw), F32)
        aux = jnp.zeros((share, 2 * 128), F32)
        for h in range(heads):
            head = (lane_h >= HD * h) & (lane_h < HD * (h + 1))
            at = hw - 128 + 2 * h
            inv_h = inv[:, at : at + 1] + inv[:, at + 1 : at + 2]
            scaled = jnp.where(head, mixed_grad * inv_h, scaled)
            delta = -jnp.sum(jnp.where(head, prod, 0.0), axis=1, keepdims=True) * inv_h
            coarse = delta.astype(BF16).astype(F32)
            aux = jnp.where(lane_q == hw + 2 * h, coarse, aux)
            aux = jnp.where(lane_q == hw + 2 * h + 1, delta - coarse, aux)
        dob[s] = aux.astype(BF16)
        dob[s, :, 0:hw] = scaled.astype(BF16)
        aw[s, :, qkvw : 4 * hw] = nn(branch_t[...], mixed[:, 0:hw]).astype(BF16)
        reduce_tick(n_all - 1 + k)
        return carry

    lax.fori_loop(0, parts, out_back, 0)

    def p_in(s, h, half):
        return pltpu.make_async_copy(ph_ref.at[s * heads + h, half], pst.at[h], ps_sem.at[h])

    def group_of(it):
        return (t + 1 + it % parts) % parts

    def fetch(it):
        for h in range(heads):
            p_in(group_of(it), h, 1 - it // parts).start()

    def att_group(it, half):
        s = group_of(it)
        base = half * share
        qg = qb[s]
        dg = dob[s]
        kg = kb[s, base : base + share]
        vg = vb[s, base : base + share]
        qt = qg[:, 0:hw].T
        dt = dg[:, 0:hw].T
        lane_q = lanes((share, 2 * 128))
        dq = jnp.zeros((share, 2 * 128), F32)
        dks = []
        dvs = []
        for h in range(heads):
            head = (lane_q >= HD * h) & (lane_q < HD * (h + 1))
            aux = (lane_q >= hw + 2 * h) & (lane_q < hw + 2 * h + 2)
            dm = jnp.where(head | aux, dg, jnp.zeros_like(dg))
            prob_grad = nt(dm, vg)
            p_in(s, h, half).wait()
            probs = pst[h]
            score_grad = (probs.astype(F32) * prob_grad).astype(BF16)
            dq = jnp.where(head, nn(score_grad, kg), dq)
            dks.append(nn(qt[HD * h : HD * (h + 1)], score_grad))
            dvs.append(nn(dt[HD * h : HD * (h + 1)], probs))
        dk = (jnp.concatenate(dks, axis=0) * math.log(2.0)).astype(BF16)
        dv = jnp.concatenate(dvs, axis=0).astype(BF16)
        return s, dq[:, 0:hw] * factor, dk.T, dv.T

    acc0[...] = jnp.zeros_like(acc0)
    acc1[...] = jnp.zeros_like(acc1)
    fetch(0)

    def pair_half(it, carry):
        s, dq, dk, dv = att_group(it, 1)
        fetch(it + 1)
        uu[s, 0:share, qkvw : 4 * hw] = dq.astype(BF16)
        uu[s, 0:share, 0:hw] = jnp.zeros((share, hw), BF16)
        uu[s, 0:share, hw : 2 * hw] = dk
        uu[s, 0:share, 2 * hw : 3 * hw] = dv
        acc0[...] += nt(uu[s, 0:share, 0:qkvw], aw[s, :, 0:qkvw])
        late[pl.ds(2 * s + 1, 1), 0:hw] = jnp.sum(dv.astype(F32), axis=0, keepdims=True)
        reduce_tick(n_all - 1 + parts + 2 * it)
        reduce_tick(n_all - 1 + parts + 2 * it + 1)
        return carry

    lax.fori_loop(0, parts, pair_half, 0)

    ng_copy = rcopy(ngs, ngr, ng_sem.at[0], ng_sem.at[1], (d, tp))
    pair_grad = acc0[...]
    lo_copy.wait()
    ngs[...] = pair_grad.astype(BF16)
    ng_copy.start()
    unit, _ = unit_of(xp[...].astype(F32))
    late[8:9, :] = jnp.sum(pair_grad * unit, axis=0, keepdims=True)
    late[9:10, :] = jnp.sum(pair_grad, axis=0, keepdims=True)

    def ra(stage, q):
        s = group_of(q)
        low, high, first, second = route(s % 2)
        if stage == 0:
            return rcopy(
                aw.at[s, rows((1 - c) * 4 * piece, 4 * piece), :],
                rc_a.at[q],
                ca_s.at[q],
                ca_r.at[q],
                dev_c,
            )
        if stage == 1:
            return rcopy(
                aw.at[s, rows((c * 4 + (1 - high) * 2) * piece, 2 * piece), :],
                r2_a.at[q],
                a2_s.at[q],
                a2_r.at[q],
                second,
            )
        if stage == 2:
            return rcopy(
                aw.at[s, rows((c * 4 + high * 2 + 1 - low) * piece, piece), :],
                r1_a.at[q],
                a1_s.at[q],
                a1_r.at[q],
                first,
            )
        return rcopy(
            aw.at[s, rows((c * 4 + high * 2 + low) * piece, piece), :],
            rz_a.at[q],
            az_s.at[q],
            az_r.at[q],
            (d, s),
        )

    def ra_step(stage, q):
        s = group_of(q)
        low, high, _, _ = route(s % 2)
        ra(stage, q).wait_recv()
        if stage == 0:
            add_rows(aw.at[s, rows(c * 4 * piece, 4 * piece), :], rc_a.at[q])
        elif stage == 1:
            add_rows(aw.at[s, rows((c * 4 + high * 2) * piece, 2 * piece), :], r2_a.at[q])
        else:
            add_rows(aw.at[s, rows((c * 4 + high * 2 + low) * piece, piece), :], r1_a.at[q])

    def own_half(it, carry):
        q = it - parts
        s, dq, dk, dv = att_group(it, 0)

        @pl.when(it + 1 < 2 * parts)
        def _():
            fetch(it + 1)

        dq = (uu[s, 0:share, qkvw : 4 * hw].astype(F32) + dq).astype(BF16)
        dd[:, 0:hw] = dq
        dd[:, hw : 2 * hw] = dk
        dd[:, 2 * hw : 3 * hw] = dv
        acc1[...] += nt(dd[:, 0:qkvw], aw[s, :, 0:qkvw])
        late[pl.ds(2 * s, 1), 0:hw] = jnp.sum(dq.astype(F32), axis=0, keepdims=True)
        late[pl.ds(2 * s + 1, 1), 0:hw] = late[pl.ds(2 * s + 1, 1), 0:hw] + jnp.sum(
            dv.astype(F32), axis=0, keepdims=True
        )
        aw[s, :, 0:qkvw] = (
            nn(xnt[:, 0:share], dd[:, 0:qkvw]) + nn(xnt[:, share:keys], uu[s, 0:share, 0:qkvw])
        ).astype(BF16)
        ra(0, q).start()
        reduce_tick(n_all - 1 + 3 * parts + q)

        @pl.when(q >= 1)
        def _():
            ra_step(0, q - 1)
            ra(1, q - 1).start()

        @pl.when(q >= 2)
        def _():
            ra_step(1, q - 2)
            ra(2, q - 2).start()

        @pl.when(q >= 3)
        def _():
            ra_step(2, q - 3)
            ra(3, q - 3).start()

        final_tick(2 * q)
        final_tick(2 * q + 1)
        return carry

    lax.fori_loop(parts, 2 * parts, own_half, 0)

    last = parts - 1
    ra_step(0, last)
    ra(1, last).start()
    ra_step(1, last - 1)
    ra(2, last - 1).start()
    ra_step(2, last - 2)
    ra(3, last - 2).start()

    own_grad = acc1[...]
    unit, scale_inv = unit_of(x_ref[...].astype(F32))
    late[8:9, :] = late[8:9, :] + jnp.sum(own_grad * unit, axis=0, keepdims=True)
    late[9:10, :] = late[9:10, :] + jnp.sum(own_grad, axis=0, keepdims=True)

    stages = (dev_c, (dx, t), (dy, t))

    def vec(which, stage):
        buf, rx = (early, e_rx) if which == 0 else (late, l_rx)
        return rcopy(buf, rx.at[stage], sm_s.at[which, stage], sm_r.at[which, stage], stages[stage])

    def vec_far(which, k):
        rz = e_rz if which == 0 else l_rz
        return rcopy(
            rz.at[t], rz.at[t], sm_s.at[which, 2 + k], sm_r.at[which, 3 + t], (d, far(k))
        )

    for stage in range(3):
        for which in range(2):
            vec(which, stage).start()
        if stage == 0:
            ra_step(1, last)
            ra(2, last).start()
            ra_step(2, last - 1)
            ra(3, last - 1).start()
        for which in range(2):
            buf, rx = (early, e_rx) if which == 0 else (late, l_rx)
            vec(which, stage).wait_recv()
            vec(which, stage).wait_send()
            buf[...] = buf[...] + rx[stage]
    for which in range(2):
        buf, rz = (early, e_rz) if which == 0 else (late, l_rz)
        rz[t] = buf[...]
        for k in range(1, parts):
            vec_far(which, k).start()

    ra_step(2, last)
    mine = rows(pos_own_a, piece)
    total = aw[t, mine, :].astype(F32)
    for q in range(parts - 1):
        rcopy(rz_a.at[q], rz_a.at[q], az_s.at[q], az_r.at[q], (d, t)).wait_recv()
        total = total + rz_a[q].astype(F32)
    done = uu.at[0]
    done[mine, :] = total.astype(BF16)

    def aa(stage):
        if stage == 0:
            view, dev = done.at[mine, :], first_a
        elif stage == 1:
            view, dev = done.at[rows((c * 4 + high_a * 2) * piece, 2 * piece), :], second_a
        else:
            view, dev = done.at[rows(c * 4 * piece, 4 * piece), :], dev_c
        return rcopy(view, view, aa_s.at[stage], aa_r.at[stage], dev)

    aa(0).start()
    for n in range(2 * parts, nblk + 3):
        final_tick(n)

    ng_copy.wait_recv()
    grad = own_grad + ngr[...].astype(F32)
    mid[...] = mid[...] + norm_back(grad, unit, scale_inv, gain1)
    xg_copy = pltpu.make_async_copy(mid, xg_ref, loc_sem.at[nblk])
    xg_copy.start()

    aa(0).wait_recv()
    aa(1).start()

    for which in range(2):
        rz = e_rz if which == 0 else l_rz
        for k in range(1, parts):
            s = far(k)
            rcopy(
                rz.at[s], rz.at[s], sm_s.at[which, 3], sm_r.at[which, 3 + s], (d, t)
            ).wait_recv()
    osm_ref[0:24, :] = ((e_rz[0] + e_rz[1]) + e_rz[2]) + e_rz[3]
    osm_ref[24:40, :] = ((l_rz[0] + l_rz[1]) + l_rz[2]) + l_rz[3]

    aa(1).wait_recv()
    aa(2).start()

    for k in range(1, parts):
        zb(k, 0).wait_send()
        zb(k, 1).wait_send()
        for which in range(2):
            vec_far(which, k).wait_send()
    x_copy.wait_send()
    ng_copy.wait_send()

    def drain_far(m, carry):
        rf(3, m + nblk).wait_send()
        return carry

    lax.fori_loop(0, n_far, drain_far, 0)

    def drain_all(r, carry):
        for stage in range(3):
            rf(stage, r).wait_send()
        return carry

    lax.fori_loop(0, n_all, drain_all, 0)

    def drain_own(j, carry):
        for stage in range(3):
            af(stage, j).wait_send()
        f_out(j).wait()
        return carry

    lax.fori_loop(0, nblk, drain_own, 0)

    for q in range(parts):
        for stage in range(3):
            ra(stage, q).wait_send()
        if q < parts - 1:
            ra(3, q).wait_send()
    aa(2).wait_recv()
    oa_copy = pltpu.make_async_copy(done, oa_ref, loc_sem.at[nblk + 1])
    oa_copy.start()
    oa_copy.wait()
    xg_copy.wait()
    for stage in range(3):
        aa(stage).wait_send()


def local(
    x_in,
    cotangent,
    lengths,
    bucket_ids,
    bucket_weights,
    ln1_gain,
    ln1_bias,
    w_qkv,
    qv_bias,
    w_out,
    b_out,
    ln2_gain,
    ln2_bias,
    w_up,
    b_up,
    w_down,
    b_down,
):
    share, width = x_in.shape
    hw = w_qkv.shape[2]
    heads = hw // HD
    parts = 4
    fw = w_up.shape[1]
    nblk = fw // BLK
    piece = width // GROUP
    keys = 2 * share
    n_all = parts * nblk
    n_far = n_all - nblk
    vm = pl.BlockSpec(memory_space=pltpu.VMEM)
    sm = pl.BlockSpec(memory_space=pltpu.SMEM)
    hbm = pl.BlockSpec(memory_space=pl.ANY)
    dma = pltpu.SemaphoreType.DMA
    scratch = [
        pltpu.VMEM((n_all + nblk, 2, width, BLK), BF16),
        pltpu.VMEM((parts, width, 4 * hw), BF16),
        pltpu.VMEM((SLOTS_C, 2, 4 * piece, BLK), BF16),
        pltpu.VMEM((n_all, 2, 2 * piece, BLK), BF16),
        pltpu.VMEM((n_all, 2, piece, BLK), BF16),
        pltpu.VMEM((n_far, 2, piece, BLK), BF16),
        pltpu.VMEM((parts, 4 * piece, 4 * hw), BF16),
        pltpu.VMEM((parts, 2 * piece, 4 * hw), BF16),
        pltpu.VMEM((parts, piece, 4 * hw), BF16),
        pltpu.VMEM((parts - 1, piece, 4 * hw), BF16),
        pltpu.VMEM((keys, width), BF16),
        pltpu.VMEM((share, width), BF16),
        pltpu.VMEM((parts, share, 256), BF16),
        pltpu.VMEM((parts, keys, 256), BF16),
        pltpu.VMEM((parts, keys, 256), BF16),
        pltpu.VMEM((parts, share, 256), BF16),
        pltpu.VMEM((parts, share, 256), BF16),
        pltpu.VMEM((share, 512), BF16),
        pltpu.VMEM((heads, share, share), BF16),
        pltpu.VMEM((share, width), F32),
        pltpu.VMEM((share, width), F32),
        pltpu.VMEM((share, width), F32),
        pltpu.VMEM((parts, width, width), BF16),
        pltpu.VMEM((share, width), BF16),
        pltpu.VMEM((width, share), BF16),
        pltpu.VMEM((width, keys), BF16),
        pltpu.VMEM((share, width), BF16),
        pltpu.VMEM((share, width), BF16),
        pltpu.VMEM((parts, 1, fw), F32),
        pltpu.VMEM((parts, 2, hw), F32),
        pltpu.VMEM((24, width), F32),
        pltpu.VMEM((16, width), F32),
        pltpu.VMEM((3, 24, width), F32),
        pltpu.VMEM((parts, 24, width), F32),
        pltpu.VMEM((3, 16, width), F32),
        pltpu.VMEM((parts, 16, width), F32),
        dma((2 * nblk + 1,)),
        dma((heads,)),
        dma((3,)),
        dma((parts,)),
        dma((2,)),
        dma((6,)),
        dma((2, parts)),
        dma((3, parts)),
        dma((3, parts)),
        dma((n_far,)),
        dma((n_all,)),
        dma((3, n_all)),
        dma((3, n_all)),
        dma((n_all,)),
        dma((n_all,)),
        dma((n_all,)),
        dma((n_all,)),
        dma((n_all,)),
        dma((n_all,)),
        dma((n_far,)),
        dma((n_far,)),
        dma((3, nblk)),
        dma((3, nblk)),
        dma((parts,)),
        dma((parts,)),
        dma((parts,)),
        dma((parts,)),
        dma((parts,)),
        dma((parts,)),
        dma((parts,)),
        dma((parts,)),
        dma((3,)),
        dma((3,)),
        dma((2, 7)),
        dma((2, 7)),
        dma((2,)),
        pltpu.SemaphoreType.REGULAR,
    ]
    layer_out, x_grad, of, oa, osm, _ = pl.pallas_call(
        kernel,
        out_shape=[
            jax.ShapeDtypeStruct((share, width), BF16),
            jax.ShapeDtypeStruct((share, width), F32),
            jax.ShapeDtypeStruct((nblk, 2, width, BLK), BF16),
            jax.ShapeDtypeStruct((width, 4 * hw), BF16),
            jax.ShapeDtypeStruct((40, width), F32),
            jax.ShapeDtypeStruct((parts * heads, 2, share, share), BF16),
        ],
        in_specs=[vm, hbm, sm, sm, sm, vm, vm, vm, vm, vm, vm, vm, vm, hbm, vm, hbm, vm],
        out_specs=[hbm, hbm, hbm, hbm, vm, hbm],
        scratch_shapes=scratch,
        compiler_params=pltpu.CompilerParams(
            collective_id=0, has_side_effects=True, vmem_limit_bytes=67043328
        ),
    )(
        x_in,
        cotangent,
        lengths,
        bucket_ids,
        bucket_weights,
        ln1_gain.reshape(1, -1),
        ln1_bias.reshape(1, -1),
        w_qkv,
        qv_bias,
        w_out,
        b_out.reshape(1, -1),
        ln2_gain.reshape(1, -1),
        ln2_bias.reshape(1, -1),
        w_up,
        b_up.reshape(1, -1),
        w_down,
        b_down.reshape(1, -1),
    )
    dp = lax.axis_size("dp")
    grads = (of, oa, osm)
    if dp > GROUP:
        groups = [[g + GROUP * i for i in range(dp // GROUP)] for g in range(GROUP)]
        grads = lax.psum(tuple(g.astype(F32) for g in grads), "dp", axis_index_groups=groups)
    of, oa, osm = grads
    t = lax.axis_index("tensor")
    of = of.astype(F32)
    oa = oa.astype(F32)
    grad_up = of[:, 0].transpose(1, 0, 2).reshape(width, fw)
    grad_down = of[:, 1].transpose(0, 2, 1).reshape(fw, width)
    grad_qkv = oa[:, : 3 * hw].reshape(width, 3, hw).transpose(1, 0, 2)
    grad_w_out = oa[:, 3 * hw :].T
    grad_up_bias = lax.dynamic_slice_in_dim(osm, 4 + t * nblk, nblk, 0)[:, :BLK].reshape(fw)
    grad_qv = lax.dynamic_slice_in_dim(osm, 24 + 2 * t, 2, 0)[:, :hw]
    return (
        layer_out,
        x_grad,
        osm[32],
        osm[33],
        grad_qkv,
        grad_qv,
        grad_w_out,
        osm[2],
        osm[0],
        osm[1],
        grad_up,
        grad_up_bias,
        grad_down,
        osm[3],
    )


def solution(mesh):
    return jax.shard_map(
        local,
        mesh=mesh,
        in_specs=(
            P(("dp", "tensor"), None),
            P(("dp", "tensor"), None),
            P("dp", None),
            P("dp"),
            P(),
            P(),
            P(),
            P(None, None, "tensor"),
            P(None, "tensor"),
            P("tensor", None),
            P(),
            P(),
            P(),
            P(None, "tensor"),
            P("tensor"),
            P("tensor", None),
            P(),
        ),
        out_specs=(
            P(("dp", "tensor"), None),
            P(("dp", "tensor"), None),
            P(),
            P(),
            P(None, None, "tensor"),
            P(None, "tensor"),
            P("tensor", None),
            P(),
            P(),
            P(),
            P(None, "tensor"),
            P("tensor"),
            P("tensor", None),
            P(),
        ),
        check_vma=False,
    )
```

```python
import functools
import math

import jax
import jax.numpy as jnp
from jax import lax
from jax.experimental import pallas as pl
from jax.experimental.pallas import tpu as pltpu
from jax.sharding import PartitionSpec as P

HD = 32
BUCKET = 256
EPSILON = 1e-05
GROUP = 8
BLK = 256
BIG = 1e30
F32 = jnp.float32
BF16 = jnp.bfloat16
MESH = pl.DeviceIdType.MESH
RSQRT2 = 1.0 / math.sqrt(2.0)
RSQRT2PI = 1.0 / math.sqrt(2.0 * math.pi)
SLOTS_C = 2
G_LAG1 = 8
G_LAG2 = 5
LAG = 2


def nn(a, b):
    return lax.dot_general(a, b, (((1,), (0,)), ((), ())), preferred_element_type=F32)


def nt(a, b):
    return lax.dot_general(a, b, (((1,), (1,)), ((), ())), preferred_element_type=F32)


def unit_of(values):
    centre = values - jnp.mean(values, axis=-1, keepdims=True)
    scale_inv = lax.rsqrt(jnp.mean(centre * centre, axis=-1, keepdims=True) + EPSILON)
    return centre * scale_inv, scale_inv


def norm_back(grad, unit, scale_inv, gain):
    scaled = grad * gain
    return scale_inv * (
        scaled
        - jnp.mean(scaled, axis=-1, keepdims=True)
        - unit * jnp.mean(scaled * unit, axis=-1, keepdims=True)
    )


def lanes(shape):
    return lax.broadcasted_iota(jnp.int32, shape, 1)


def kernel(
    x_ref,
    cot_ref,
    len_ref,
    bid_ref,
    bw_ref,
    g1_ref,
    s1_ref,
    wqkv_ref,
    qvb_ref,
    wout_ref,
    bout_ref,
    g2_ref,
    s2_ref,
    wup_ref,
    bup_ref,
    wdn_ref,
    bdn_ref,
    lo_ref,
    xg_ref,
    ou_ref,
    od_ref,
    oa_ref,
    osm_ref,
    ph_ref,
    fg,
    aw,
    rc_f,
    r2_f,
    r1_f,
    rz_f,
    rc_a,
    r2_a,
    r1_a,
    rz_a,
    xn,
    xp,
    qb,
    kb,
    vb,
    mx,
    dmx,
    stat,
    dd,
    pst,
    mid,
    acc0,
    acc1,
    uu,
    ol,
    olt,
    ngs,
    ngr,
    bupa,
    qvba,
    early,
    late,
    e_rx,
    e_rz,
    l_rx,
    l_rz,
    loc_sem,
    ps_sem,
    za_s,
    za_r,
    zx_sem,
    zb_s,
    zb_r,
    ga_s,
    ga_r,
    zf_s,
    zf_r,
    gf_s,
    gf_r,
    cf_s,
    cf_r,
    f2_s,
    f2_r,
    f1_s,
    f1_r,
    fz_s,
    fz_r,
    af_s,
    af_r,
    ca_s,
    ca_r,
    a2_s,
    a2_r,
    a1_s,
    a1_r,
    az_s,
    az_r,
    aa_s,
    aa_r,
    sm_s,
    sm_r,
    ng_sem,
    credit,
):
    share, width = x_ref.shape
    hw = wqkv_ref.shape[1]
    heads = hw // HD
    qkvw = 3 * hw
    parts = 4
    nblk = wup_ref.shape[1] // BLK
    piece = width // GROUP
    keys = 2 * share
    factor = HD ** (-0.5)
    q_scale = factor * math.log2(math.e)

    d = lax.axis_index("dp")
    t = lax.axis_index("tensor")
    c = d % 2
    bx = (d // 2) % 2
    by = (d // 4) % 2
    dev_c = (d + 1 - 2 * c, t)
    dx = d + 2 - 4 * bx
    dy = d + 4 - 8 * by
    tp = t + 1 - 2 * (t % 2)

    def far(k):
        return (t + k) % parts

    def route(par):
        low = bx + par * (by - bx)
        high = by + par * (bx - by)
        first = (dx + par * (dy - dx), t)
        second = (dy + par * (dx - dy), t)
        return low, high, first, second

    def rcopy(src, dst, ssem, rsem, dev):
        return pltpu.make_async_remote_copy(
            src_ref=src, dst_ref=dst, send_sem=ssem, recv_sem=rsem, device_id=dev, device_id_type=MESH
        )

    def rows(start, size):
        return pl.ds(pl.multiple_of(start, 16), size)

    def up_load(j):
        return pltpu.make_async_copy(
            wup_ref.at[:, pl.ds(j * BLK, BLK)], fg.at[t * nblk + j, 0], loc_sem.at[j]
        )

    def dn_load(j):
        return pltpu.make_async_copy(
            wdn_ref.at[pl.ds(j * BLK, BLK), :],
            uu.at[j // 2, pl.ds((j % 2) * BLK, BLK), :],
            loc_sem.at[nblk + j],
        )

    cot_load = pltpu.make_async_copy(cot_ref, ol, loc_sem.at[2 * nblk])

    a_loads = [
        pltpu.make_async_copy(
            wqkv_ref.at[i], aw.at[t, pl.ds(i * hw, hw), :], loc_sem.at[2 * nblk + 1 + i]
        )
        for i in range(3)
    ]
    a_loads.append(
        pltpu.make_async_copy(
            wout_ref, aw.at[t, pl.ds(qkvw, hw), :], loc_sem.at[2 * nblk + 4]
        )
    )
    for cp in a_loads:
        cp.start()
    for j in range(nblk):
        dn_load(j).start()
        up_load(j).start()
    cot_load.start()
    bupa[t] = bup_ref[...][None, :]
    qvba[t] = qvb_ref[...]

    barrier = pltpu.get_barrier_semaphore()
    for dev in (dev_c, (dx, t), (dy, t), (d, far(1)), (d, far(2)), (d, far(3))):
        pl.semaphore_signal(barrier, inc=1, device_id=dev, device_id_type=MESH)
    pl.semaphore_wait(barrier, 6)

    low_a, high_a, first_a, second_a = route(t % 2)
    pos_own_a = (c * 4 + high_a * 2 + low_a) * piece

    def za(k):
        view = aw.at[t, rows(pos_own_a, piece), :]
        return rcopy(view, view, za_s.at[k - 1], za_r.at[t], (d, far(parts - k)))

    def za_wait(s, par):
        low, high, _, _ = route(par)
        view = aw.at[s, rows((c * 4 + high * 2 + low) * piece, piece), :]
        rcopy(view, view, za_s.at[0], za_r.at[s], (d, t)).wait_recv()

    def zb(k, which):
        dst = (bupa if which == 0 else qvba).at[t]
        return rcopy(dst, dst, zb_s.at[2 * (k - 1) + which], zb_r.at[which, t], (d, far(parts - k)))

    def zb_wait(s, which):
        dst = (bupa if which == 0 else qvba).at[s]
        rcopy(dst, dst, zb_s.at[0], zb_r.at[which, s], (d, t)).wait_recv()

    x_copy = rcopy(x_ref, xp, zx_sem.at[0], zx_sem.at[1], (d, tp))

    for cp in a_loads:
        cp.wait()
    for k in range(1, parts):
        za(k).start()
        zb(k, 1).start()
    x_copy.start()
    for k in range(1, parts):
        zb(k, 0).start()

    def ga(stage, s):
        low, high, first, second = route(s % 2)
        if stage == 0:
            view, dev = aw.at[s, rows((c * 4 + high * 2 + low) * piece, piece), :], first
        elif stage == 1:
            view, dev = aw.at[s, rows((c * 4 + high * 2) * piece, 2 * piece), :], second
        else:
            view, dev = aw.at[s, rows(c * 4 * piece, 4 * piece), :], dev_c
        return rcopy(view, view, ga_s.at[stage, s], ga_r.at[stage, s], dev)

    def ga_step(stage, k):
        s = far(k)
        if stage == 0:
            za_wait(s, s % 2)
        else:
            ga(stage - 1, s).wait_recv()
        ga(stage, s).start()

    gain1 = g1_ref[...][None, :]
    shift1 = s1_ref[...][None, :]
    unit, _ = unit_of(x_ref[...].astype(F32))
    xn[0:share, :] = (unit * gain1 + shift1).astype(BF16)
    ga_step(0, 1)

    bucket = bid_ref[0]
    span = jnp.where(bucket == 0, BUCKET, jnp.where(bucket == 1, 2 * BUCKET, 4 * BUCKET))
    weight = jnp.where(bucket == 0, bw_ref[0], jnp.where(bucket == 1, bw_ref[1], bw_ref[2]))

    def slot_info(base, shape):
        place = base + lax.broadcasted_iota(jnp.int32, shape, 0)
        item = jnp.zeros(shape, jnp.int32)
        for j in range(1, len_ref.shape[1]):
            item = item + jnp.where(place >= j * span, 1, 0)
        length = jnp.zeros(shape, jnp.int32)
        for j in range(len_ref.shape[1]):
            length = jnp.where(item == j, len_ref[0, j], length)
        return item, (place - item * span) < length

    wide = (share, 2 * 128)
    lane = lanes(wide)
    slots = len_ref.shape[1]
    in_aux = (lane >= hw) & (lane < hw + slots)
    one_aux = jnp.where(lane >= hw, 1.0, 0.0).astype(BF16)

    own_item, own_live = slot_info(t * share, wide)
    q_aux = jnp.where(in_aux & (own_item == lane - hw), 1.0, 0.0).astype(BF16)
    k_aux0 = jnp.where(in_aux & ~((own_item == lane - hw) & own_live), -BIG, 0.0).astype(BF16)
    pair_item, pair_live = slot_info(tp * share, wide)
    k_aux1 = jnp.where(in_aux & ~((pair_item == lane - hw) & pair_live), -BIG, 0.0).astype(BF16)
    for s in range(parts):
        qb[s] = q_aux
        kb[s, 0:share] = k_aux0
        kb[s, share:keys] = k_aux1
        vb[s, 0:share] = one_aux
        vb[s, share:keys] = one_aux
    _, live1 = slot_info(t * share, (share, 128))
    row_weight = jnp.where(live1, weight, 0.0)[:, 0:1]

    ga_step(0, 2)

    def zf(k, j):
        low, high, _, _ = route((t + j) % 2)
        view = fg.at[t * nblk + j, :, rows((c * 4 + high * 2 + low) * piece, piece), :]
        return rcopy(
            view, view, zf_s.at[(k - 1) * nblk + j], zf_r.at[t * nblk + j], (d, far(parts - k))
        )

    for j in range(nblk):
        up_load(j).wait()
        dn_load(j).wait()
        fg[t * nblk + j, 1] = uu[j // 2, (j % 2) * BLK : (j % 2 + 1) * BLK, :].T
    for k in range(1, parts):
        for j in range(nblk):
            zf(k, j).start()

    ga_step(1, 1)
    ga_step(0, 3)

    def project(s, half, own):
        base = half * share
        first = 0 if own else hw
        out = nt(xn[base : base + share, :], aw[s, first:qkvw, :])
        if own:
            qb[s, :, 0:hw] = ((out[:, 0:hw] + qvba[s, 0:1, :]) * q_scale).astype(BF16)
        at = hw - first
        kb[s, base : base + share, 0:hw] = out[:, at : at + hw].astype(BF16)
        vb[s, base : base + share, 0:hw] = (
            out[:, at + hw : at + 2 * hw] + qvba[s, 1:2, :]
        ).astype(BF16)

    n_far = (parts - 1) * nblk

    def far_block(m):
        s = (t + 1 + m // nblk) % parts
        j = m % nblk
        return s, j, s * nblk + j

    def gf(stage, m):
        s, j, b = far_block(m)
        low, high, first, second = route((s + j) % 2)
        if stage == 0:
            view, dev = fg.at[b, :, rows((c * 4 + high * 2 + low) * piece, piece), :], first
        elif stage == 1:
            view, dev = fg.at[b, :, rows((c * 4 + high * 2) * piece, 2 * piece), :], second
        else:
            view, dev = fg.at[b, :, rows(c * 4 * piece, 4 * piece), :], dev_c
        return rcopy(view, view, gf_s.at[stage, b], gf_r.at[stage, b], dev)

    def zf_wait(m):
        s, j, b = far_block(m)
        low, high, _, _ = route((s + j) % 2)
        view = fg.at[b, :, rows((c * 4 + high * 2 + low) * piece, piece), :]
        rcopy(view, view, zf_s.at[0], zf_r.at[b], (d, t)).wait_recv()

    def within(n, size):
        return (n >= 0) & (n < size)

    def gather_tick(n):
        @pl.when(within(n, n_far))
        def _():
            zf_wait(n)
            gf(0, n).start()

        @pl.when(within(n - LAG, n_far))
        def _():
            gf(0, n - LAG).wait_recv()
            gf(1, n - LAG).start()

        @pl.when(within(n - 2 * LAG, n_far))
        def _():
            gf(1, n - 2 * LAG).wait_recv()
            gf(2, n - 2 * LAG).start()

    lane_w = lanes((share, 2 * 128))
    lane_n = lanes((share, 128))

    def head_lanes(h):
        return (lane_w >= HD * h) & (lane_w < HD * (h + 1))

    def spread(values, at):
        out = jnp.zeros((share, 2 * 128), F32)
        for h in range(heads):
            out = jnp.where(head_lanes(h), values[:, at + h : at + h + 1], out)
        return out

    def p_out(s, h, half, buf):
        return pltpu.make_async_copy(
            pst.at[buf, h], ph_ref.at[s * heads + h, half], ps_sem.at[buf, h]
        )

    def att_forward(k, half):
        s = far(k)
        base = half * share
        buf = k % 2
        if half == 1:
            for h in range(heads):
                p_out(s, h, half, buf).wait()
        else:

            @pl.when(k >= 2)
            def _():
                for h in range(heads):
                    p_out(s, h, half, buf).wait()

        qg = qb[s]
        kg = kb[s, base : base + share]
        vg = vb[s, base : base + share]
        out = jnp.zeros((share, 2 * 128), F32)
        tops = jnp.zeros((share, 128), F32)
        sums = jnp.ones((share, 128), F32)
        for h in range(heads):
            head = head_lanes(h)
            qm = jnp.where(head | (lane_w >= hw), qg, jnp.zeros_like(qg))
            scores = nt(qm, kg)
            top = jnp.max(scores, axis=1, keepdims=True)
            probs = jnp.exp2(scores - top).astype(BF16)
            pst[buf, h] = probs
            mixed = nn(probs, vg)
            out = jnp.where(head, mixed, out)
            tops = jnp.where(lane_n == h, top, tops)
            sums = jnp.where(lane_n == h, mixed[:, hw : hw + 1], sums)
        for h in range(heads):
            p_out(s, h, half, buf).start()
        log_sum = tops + jnp.log2(sums)
        if half == 0:
            mx[s] = (out * spread(1.0 / sums, 0)).astype(BF16)
            stat[s] = jnp.where(lane_n < 8, tops, pltpu.roll(log_sum, 8, 1))
        else:
            before = stat[s]
            log_before = pltpu.roll(before, 120, 1)
            upper = jnp.maximum(log_sum, log_before)
            lower = jnp.minimum(log_sum, log_before)
            log_all = upper + jnp.log2(1.0 + jnp.exp2(lower - upper))
            part0 = jnp.exp2(log_before - log_all)
            part1 = jnp.exp2(log_sum - log_all) / sums
            mx[s] = (mx[s].astype(F32) * spread(part0, 0) + out * spread(part1, 0)).astype(BF16)
            stat[s] = jnp.where(
                lane_n < 8,
                jnp.exp2(before - log_all),
                pltpu.roll(jnp.exp2(tops - log_all), 8, 1),
            )

    def own_keys(k, carry):
        s = far(k)

        @pl.when(k > 0)
        def _():
            zb_wait(s, 1)
            ga(2, s).wait_recv()

        project(s, 0, True)
        att_forward(k, 0)

        @pl.when(k == 0)
        def _():
            ga_step(2, 1)
            ga_step(1, 2)

        @pl.when(k == 1)
        def _():
            ga_step(2, 2)
            ga_step(1, 3)

        @pl.when(k == 2)
        def _():
            ga_step(2, 3)

        return carry

    lax.fori_loop(0, parts, own_keys, 0)

    x_copy.wait_recv()
    unit, _ = unit_of(xp[...].astype(F32))
    xn[share:keys, :] = (unit * gain1 + shift1).astype(BF16)

    def pair_keys(k, carry):
        project(far(k), 1, False)
        att_forward(k, 1)
        gather_tick(k)
        return carry

    lax.fori_loop(0, parts, pair_keys, 0)
    for buf in range(2):
        for h in range(heads):
            p_out(0, h, 1, buf).wait()

    branch = jnp.zeros((share, width), F32)
    for s in range(parts):
        branch = branch + nn(mx[s, :, 0:hw], aw[s, qkvw : 4 * hw, :])
    middle = x_ref[...].astype(F32) + (branch + bout_ref[...][None, :])
    mid[...] = middle
    unit, _ = unit_of(middle)
    normed = (unit * g2_ref[...][None, :] + s2_ref[...][None, :]).astype(BF16)
    n2 = uu.at[0, 0:share, :]
    n2t = uu.at[1, :, 0:share]
    n2[...] = normed
    n2t[...] = normed.T
    cot_load.wait()
    low_grad = (ol[...].astype(F32) * row_weight).astype(BF16)
    early[...] = jnp.zeros_like(early)
    late[...] = jnp.zeros_like(late)
    early[3:4, :] = jnp.sum(low_grad.astype(F32), axis=0, keepdims=True)
    ol[...] = low_grad
    olt[...] = low_grad.T
    acc0[...] = jnp.zeros_like(acc0)
    acc1[...] = jnp.zeros_like(acc1)

    for k in range(1, parts):
        zb_wait(far(k), 0)

    n_all = parts * nblk

    def block(r):
        k = r // nblk
        j = r % nblk
        s = (t + k) % parts
        home = s * nblk + j
        own = jnp.where(k == 0, 1, 0)
        return k, j, s, home, home + own * (n_all + j - home)

    def rf(stage, r):
        k, j, s, _, g = block(r)
        low, high, first, second = route((s + j) % 2)
        if stage == 0:
            return rcopy(
                fg.at[g, :, rows((1 - c) * 4 * piece, 4 * piece), :],
                rc_f.at[r % SLOTS_C],
                cf_s.at[r],
                cf_r.at[r],
                dev_c,
            )
        if stage == 1:
            return rcopy(
                fg.at[g, :, rows((c * 4 + (1 - high) * 2) * piece, 2 * piece), :],
                r2_f.at[r],
                f2_s.at[r],
                f2_r.at[r],
                second,
            )
        if stage == 2:
            return rcopy(
                fg.at[g, :, rows((c * 4 + high * 2 + 1 - low) * piece, piece), :],
                r1_f.at[r],
                f1_s.at[r],
                f1_r.at[r],
                first,
            )
        z = jnp.maximum(r - nblk, 0)
        return rcopy(
            fg.at[g, :, rows((c * 4 + high * 2 + low) * piece, piece), :],
            rz_f.at[z],
            fz_s.at[z],
            fz_r.at[z],
            (d, s),
        )

    def add_rows(ref, got):
        ref[...] = (ref[...].astype(F32) + got[...].astype(F32)).astype(BF16)

    def rf_second(r):
        k, j, s, _, g = block(r)
        rf(0, r).wait_recv()
        add_rows(fg.at[g, :, rows(c * 4 * piece, 4 * piece), :], rc_f.at[r % SLOTS_C])

        @pl.when(r < n_all - SLOTS_C)
        def _():
            pl.semaphore_signal(credit, inc=1, device_id=dev_c, device_id_type=MESH)

        rf(1, r).start()

    def rf_first(r):
        k, j, s, _, g = block(r)
        low, high, _, _ = route((s + j) % 2)
        rf(1, r).wait_recv()
        add_rows(fg.at[g, :, rows((c * 4 + high * 2) * piece, 2 * piece), :], r2_f.at[r])
        rf(2, r).start()

    def rf_far(r):
        k, j, s, _, g = block(r)
        low, high, _, _ = route((s + j) % 2)
        rf(2, r).wait_recv()
        add_rows(fg.at[g, :, rows((c * 4 + high * 2 + low) * piece, piece), :], r1_f.at[r])

        @pl.when(r >= nblk)
        def _():
            rf(3, r).start()

    def af(stage, j):
        low, high, first, second = route((t + j) % 2)
        b = t * nblk + j
        if stage == 0:
            view, dev = fg.at[b, :, rows((c * 4 + high * 2 + low) * piece, piece), :], first
        elif stage == 1:
            view, dev = fg.at[b, :, rows((c * 4 + high * 2) * piece, 2 * piece), :], second
        else:
            view, dev = fg.at[b, :, rows(c * 4 * piece, 4 * piece), :], dev_c
        return rcopy(view, view, af_s.at[stage, j], af_r.at[stage, j], dev)

    def f_final(j):
        low, high, _, _ = route((t + j) % 2)
        mine = rows((c * 4 + high * 2 + low) * piece, piece)
        total = fg[n_all + j, :, mine, :].astype(F32)
        for k in range(1, parts):
            z = (k - 1) * nblk + j
            rcopy(rz_f.at[z], rz_f.at[z], fz_s.at[z], fz_r.at[z], (d, t)).wait_recv()
            total = total + rz_f[z].astype(F32)
        fg[t * nblk + j, :, mine, :] = total.astype(BF16)
        af(0, j).start()

    def f_out(j, which):
        if which == 0:
            return pltpu.make_async_copy(
                fg.at[t * nblk + j, 0], ou_ref.at[:, pl.ds(j * BLK, BLK)], loc_sem.at[j]
            )
        return pltpu.make_async_copy(
            ol.at[pl.ds((j % 2) * BLK, BLK), :],
            od_ref.at[pl.ds(j * BLK, BLK), :],
            loc_sem.at[nblk + 2 + j % 2],
        )

    def reduce_tick(n):
        @pl.when(within(n, n_all))
        def _():
            rf_second(n)

        @pl.when(within(n - G_LAG1, n_all))
        def _():
            rf_first(n - G_LAG1)

        @pl.when(within(n - G_LAG1 - G_LAG2, n_all))
        def _():
            rf_far(n - G_LAG1 - G_LAG2)

    def drain_zf(m, carry):
        view = fg.at[0, :, 0:piece, :]
        rcopy(view, view, zf_s.at[m], zf_r.at[0], (d, t)).wait_send()
        return carry

    def ffn(r, carry):
        k, j, s, home, g = block(r)

        @pl.when(k > 0)
        def _():
            gf(2, jnp.maximum(r - nblk, 0)).wait_recv()

        wu = fg[home, 0]
        wd = fg[home, 1]
        hidden = nn(n2[...], wu) + bupa[s, :, pl.ds(pl.multiple_of(j * BLK, BLK), BLK)]
        cdf = 0.5 + 0.5 * lax.erf(hidden * RSQRT2)
        slope = cdf + hidden * (jnp.exp(-0.5 * hidden * hidden) * RSQRT2PI)
        active = (hidden * cdf).astype(BF16)
        act_grad = nn(ol[...], wd)
        hid_grad = (slope * act_grad).astype(BF16)
        acc0[...] += nt(active, wd)
        acc1[...] += nt(hid_grad, wu)
        early[pl.ds(4 + home, 1), 0:BLK] = jnp.sum(hid_grad.astype(F32), axis=0, keepdims=True)
        up_grad = nn(n2t[...], hid_grad).astype(BF16)
        dn_grad = nn(olt[...], active).astype(BF16)

        @pl.when(k > 0)
        def _():
            for stage in range(3):
                gf(stage, jnp.maximum(r - nblk, 0)).wait_send()

        fg[g, 0] = up_grad
        fg[g, 1] = dn_grad

        @pl.when(r == 2 * nblk)
        def _():
            lax.fori_loop(0, n_far, drain_zf, 0)

        @pl.when(r >= SLOTS_C)
        def _():
            pl.semaphore_wait(credit, 1)

        rf(0, r).start()
        gather_tick(parts + r)
        reduce_tick(r - 1)
        return carry

    lax.fori_loop(0, n_all, ffn, 0)

    middle = mid[...]
    ngs[...] = (middle + (acc0[...] + bdn_ref[...][None, :])).astype(BF16)
    lo_copy = pltpu.make_async_copy(ngs, lo_ref, loc_sem.at[2 * nblk])
    lo_copy.start()
    unit, scale_inv = unit_of(middle)
    got = acc1[...]
    early[0:1, :] = jnp.sum(got * unit, axis=0, keepdims=True)
    early[1:2, :] = jnp.sum(got, axis=0, keepdims=True)
    middle_part = norm_back(got, unit, scale_inv, g2_ref[...][None, :])
    reload = pltpu.make_async_copy(cot_ref, ol, loc_sem.at[0])
    reload.start()
    reload.wait()
    out_grad = ol[...].astype(F32) * row_weight
    middle_grad = out_grad + middle_part
    mid[...] = middle_grad
    branch_low = middle_grad.astype(BF16)
    early[2:3, :] = jnp.sum(branch_low.astype(F32), axis=0, keepdims=True)
    ol[...] = branch_low

    for k in range(1, parts):
        za(k).wait_send()
    for k in range(1, parts):
        for stage in range(3):
            ga(stage, far(k)).wait_send()

    def out_back(k, carry):
        s = far(k)
        mixed = mx[s, :, 0:hw]
        mixed_grad = nt(ol[...], aw[s, qkvw : 4 * hw, :]).astype(BF16)
        dmx[s, :, 0:hw] = mixed_grad
        prod = mixed_grad.astype(F32) * mixed.astype(F32)
        lane_h = lanes((share, hw))
        known = stat[s]
        for h in range(heads):
            head = (lane_h >= HD * h) & (lane_h < HD * (h + 1))
            delta = jnp.sum(jnp.where(head, prod, 0.0), axis=1, keepdims=True)
            known = jnp.where(lane_n == 16 + h, delta, known)
        stat[s] = known
        aw[s, qkvw : 4 * hw, :] = nn(mixed.T, ol[...]).astype(BF16)
        reduce_tick(n_all - 1 + k)
        return carry

    lax.fori_loop(0, parts, out_back, 0)

    def p_in(s, h, half, buf):
        return pltpu.make_async_copy(
            ph_ref.at[s * heads + h, half], pst.at[buf, h], ps_sem.at[buf, h]
        )

    def group_of(it):
        return (t + 1 + it % parts) % parts

    def fetch(it):
        for h in range(heads):
            p_in(group_of(it), h, 1 - it // parts, it % 2).start()

    def att_group(it, half):
        s = group_of(it)
        base = half * share
        buf = it % 2

        @pl.when(it + 1 < 2 * parts)
        def _():
            fetch(it + 1)

        for h in range(heads):
            p_in(s, h, half, buf).wait()
        known = stat[s]
        wanted = known if half == 0 else pltpu.roll(known, 120, 1)
        delta = -(pltpu.roll(known, 112, 1) * wanted)
        coarse = delta.astype(BF16).astype(F32)
        fine = delta - coarse
        scaled = dmx[s].astype(F32) * spread(wanted, 0)
        for h in range(heads):
            scaled = jnp.where(lane_w == hw + 2 * h, coarse[:, h : h + 1], scaled)
            scaled = jnp.where(lane_w == hw + 2 * h + 1, fine[:, h : h + 1], scaled)
        dg = jnp.where(lane_w < hw + 2 * heads, scaled, 0.0).astype(BF16)
        qg = qb[s]
        kg = kb[s, base : base + share]
        vg = vb[s, base : base + share]
        qt = qg[:, 0:hw].T
        dt = dg[:, 0:hw].T
        dq = jnp.zeros((share, 2 * 128), F32)
        dks = []
        dvs = []
        for h in range(heads):
            head = head_lanes(h)
            aux = (lane_w >= hw + 2 * h) & (lane_w < hw + 2 * h + 2)
            dm = jnp.where(head | aux, dg, jnp.zeros_like(dg))
            prob_grad = nt(dm, vg)
            probs = pst[buf, h]
            score_grad = (probs.astype(F32) * prob_grad).astype(BF16)
            dq = jnp.where(head, nn(score_grad, kg), dq)
            dks.append(nn(qt[HD * h : HD * (h + 1)], score_grad))
            dvs.append(nn(dt[HD * h : HD * (h + 1)], probs))
        dqt = (dq[:, 0:hw] * factor).T
        dkt = (jnp.concatenate(dks, axis=0) * math.log(2.0)).astype(BF16)
        dvt = jnp.concatenate(dvs, axis=0).astype(BF16)
        return s, dqt, dkt, dvt

    acc0[...] = jnp.zeros_like(acc0)
    acc1[...] = jnp.zeros_like(acc1)
    dmx_pad = jnp.zeros((share, 2 * 128 - hw), BF16)
    for s in range(parts):
        dmx[s, :, hw : 2 * 128] = dmx_pad
    fetch(0)

    def row_sums(values):
        return jnp.sum(values.astype(F32), axis=0, keepdims=True)

    def pair_half(it, carry):
        s, dqt, dkt, dvt = att_group(it, 1)
        uu[s, 0:hw, 0:share] = dqt.astype(BF16)
        uu[s, hw : 2 * hw, 0:share] = dkt
        uu[s, 2 * hw : qkvw, 0:share] = dvt
        back = uu[s, hw:qkvw, 0:share].T
        acc0[...] += nn(back, aw[s, hw:qkvw, :])
        late[pl.ds(2 * s + 1, 1), 0:hw] = row_sums(back[:, hw : 2 * hw])
        reduce_tick(n_all - 1 + parts + it)
        return carry

    lax.fori_loop(0, parts, pair_half, 0)

    ng_copy = rcopy(ngs, ngr, ng_sem.at[0], ng_sem.at[1], (d, tp))
    pair_grad = acc0[...]
    lo_copy.wait()
    ngs[...] = pair_grad.astype(BF16)
    ng_copy.start()
    unit, _ = unit_of(xp[...].astype(F32))
    late[8:9, :] = jnp.sum(pair_grad * unit, axis=0, keepdims=True)
    late[9:10, :] = jnp.sum(pair_grad, axis=0, keepdims=True)

    def ra(stage, q):
        s = group_of(q)
        low, high, first, second = route(s % 2)
        if stage == 0:
            return rcopy(
                aw.at[s, rows((1 - c) * 4 * piece, 4 * piece), :],
                rc_a.at[q],
                ca_s.at[q],
                ca_r.at[q],
                dev_c,
            )
        if stage == 1:
            return rcopy(
                aw.at[s, rows((c * 4 + (1 - high) * 2) * piece, 2 * piece), :],
                r2_a.at[q],
                a2_s.at[q],
                a2_r.at[q],
                second,
            )
        if stage == 2:
            return rcopy(
                aw.at[s, rows((c * 4 + high * 2 + 1 - low) * piece, piece), :],
                r1_a.at[q],
                a1_s.at[q],
                a1_r.at[q],
                first,
            )
        return rcopy(
            aw.at[s, rows((c * 4 + high * 2 + low) * piece, piece), :],
            rz_a.at[q],
            az_s.at[q],
            az_r.at[q],
            (d, s),
        )

    def ra_step(stage, q):
        s = group_of(q)
        low, high, _, _ = route(s % 2)
        ra(stage, q).wait_recv()
        if stage == 0:
            add_rows(aw.at[s, rows(c * 4 * piece, 4 * piece), :], rc_a.at[q])
        elif stage == 1:
            add_rows(aw.at[s, rows((c * 4 + high * 2) * piece, 2 * piece), :], r2_a.at[q])
        else:
            add_rows(aw.at[s, rows((c * 4 + high * 2 + low) * piece, piece), :], r1_a.at[q])

    stages = (dev_c, (dx, t), (dy, t))

    def vec(which, stage):
        buf, rx = (early, e_rx) if which == 0 else (late, l_rx)
        return rcopy(buf, rx.at[stage], sm_s.at[which, stage], sm_r.at[which, stage], stages[stage])

    def vec_far(which, k):
        rz = e_rz if which == 0 else l_rz
        return rcopy(
            rz.at[t], rz.at[t], sm_s.at[which, 2 + k], sm_r.at[which, 3 + t], (d, far(k))
        )

    def vec_next(which, stage):
        buf, rx = (early, e_rx) if which == 0 else (late, l_rx)
        vec(which, stage).wait_recv()
        vec(which, stage).wait_send()
        buf[...] = buf[...] + rx[stage]
        if stage < 2:
            vec(which, stage + 1).start()
        else:
            rz = e_rz if which == 0 else l_rz
            rz[t] = buf[...]
            for k in range(1, parts):
                vec_far(which, k).start()

    vec(0, 0).start()

    def own_half(it, carry):
        q = it - parts
        s, dqt, dkt, dvt = att_group(it, 0)
        dqt = (uu[s, 0:hw, 0:share].astype(F32) + dqt).astype(BF16)
        dd[0:hw, :] = dqt
        dd[hw : 2 * hw, :] = dkt
        dd[2 * hw : qkvw, :] = dvt
        back = dd[...].T
        acc1[...] += nn(back, aw[s, 0:qkvw, :])
        late[pl.ds(2 * s, 1), 0:hw] = row_sums(back[:, 0:hw])
        late[pl.ds(2 * s + 1, 1), 0:hw] = late[pl.ds(2 * s + 1, 1), 0:hw] + row_sums(
            back[:, 2 * hw : qkvw]
        )
        aw[s, 0:hw, :] = nn(dqt, xn[0:share, :]).astype(BF16)
        aw[s, hw:qkvw, :] = (
            nn(dd[hw:qkvw, :], xn[0:share, :]) + nn(uu[s, hw:qkvw, 0:share], xn[share:keys, :])
        ).astype(BF16)
        ra(0, q).start()
        reduce_tick(n_all - 1 + 2 * parts + q)

        @pl.when(q >= 1)
        def _():
            ra_step(0, q - 1)
            ra(1, q - 1).start()

        @pl.when(q >= 2)
        def _():
            ra_step(1, q - 2)
            ra(2, q - 2).start()

        @pl.when(q >= 3)
        def _():
            ra_step(2, q - 3)
            ra(3, q - 3).start()

        for stage in range(3):

            @pl.when(q == stage)
            def _():
                vec_next(0, stage)

        return carry

    lax.fori_loop(parts, 2 * parts, own_half, 0)

    last = parts - 1
    ra_step(0, last)
    ra(1, last).start()
    ra_step(1, last - 1)
    ra(2, last - 1).start()
    ra_step(2, last - 2)
    ra(3, last - 2).start()
    for n in range(n_all - 1 + 3 * parts, n_all + G_LAG1 + G_LAG2):
        reduce_tick(n)

    own_grad = acc1[...]
    unit, scale_inv = unit_of(x_ref[...].astype(F32))
    late[8:9, :] = late[8:9, :] + jnp.sum(own_grad * unit, axis=0, keepdims=True)
    late[9:10, :] = late[9:10, :] + jnp.sum(own_grad, axis=0, keepdims=True)
    vec(1, 0).start()
    f_final(0)
    vec_next(1, 0)
    f_final(1)
    ra_step(1, last)
    ra(2, last).start()
    vec_next(1, 1)
    f_final(2)
    f_final(3)
    ra_step(2, last - 1)
    ra(3, last - 1).start()
    vec_next(1, 2)
    f_final(4)

    def f_second(j):
        af(0, j).wait_recv()
        af(1, j).start()

    def f_third(j):
        af(1, j).wait_recv()
        af(2, j).start()

    for j in range(nblk):
        f_second(j)

    ra_step(2, last)
    mine = rows(pos_own_a, piece)
    total = aw[t, mine, :].astype(F32)
    for q in range(parts - 1):
        rcopy(rz_a.at[q], rz_a.at[q], az_s.at[q], az_r.at[q], (d, t)).wait_recv()
        total = total + rz_a[q].astype(F32)
    done = uu.at[0]
    done[mine, :] = total.astype(BF16)

    def aa(stage):
        if stage == 0:
            view, dev = done.at[mine, :], first_a
        elif stage == 1:
            view, dev = done.at[rows((c * 4 + high_a * 2) * piece, 2 * piece), :], second_a
        else:
            view, dev = done.at[rows(c * 4 * piece, 4 * piece), :], dev_c
        return rcopy(view, view, aa_s.at[stage], aa_r.at[stage], dev)

    aa(0).start()

    ng_copy.wait_recv()
    grad = own_grad + ngr[...].astype(F32)
    mid[...] = mid[...] + norm_back(grad, unit, scale_inv, gain1)
    xg_copy = pltpu.make_async_copy(mid, xg_ref, loc_sem.at[nblk])
    xg_copy.start()

    for j in range(nblk):
        f_third(j)
    aa(0).wait_recv()
    aa(1).start()

    for j in range(nblk):
        af(2, j).wait_recv()
        f_out(j, 0).start()
        if j >= 2:
            f_out(j - 2, 1).wait()
        ol[(j % 2) * BLK : (j % 2 + 1) * BLK, :] = fg[t * nblk + j, 1].T
        f_out(j, 1).start()

    for which in range(2):
        rz = e_rz if which == 0 else l_rz
        for k in range(1, parts):
            s = far(k)
            rcopy(
                rz.at[s], rz.at[s], sm_s.at[which, 3], sm_r.at[which, 3 + s], (d, t)
            ).wait_recv()
    early[...] = ((e_rz[0] + e_rz[1]) + e_rz[2]) + e_rz[3]
    late[...] = ((l_rz[0] + l_rz[1]) + l_rz[2]) + l_rz[3]
    osm_ref[0:4, :] = early[0:4, :]
    osm_ref[4:6, :] = late[8:10, :]
    osm_ref[8:9, :] = late[pl.ds(2 * t, 1), :]
    osm_ref[9:10, :] = late[pl.ds(2 * t + 1, 1), :]
    for j in range(nblk):
        osm_ref[16 + j : 17 + j, :] = early[pl.ds(4 + t * nblk + j, 1), :]

    aa(1).wait_recv()
    aa(2).start()

    for k in range(1, parts):
        zb(k, 0).wait_send()
        zb(k, 1).wait_send()
        for which in range(2):
            vec_far(which, k).wait_send()
    x_copy.wait_send()
    ng_copy.wait_send()

    def drain_far(m, carry):
        rf(3, m + nblk).wait_send()
        return carry

    lax.fori_loop(0, n_far, drain_far, 0)

    def drain_all(r, carry):
        for stage in range(3):
            rf(stage, r).wait_send()
        return carry

    lax.fori_loop(0, n_all, drain_all, 0)

    def drain_own(j, carry):
        for stage in range(3):
            af(stage, j).wait_send()
        return carry

    lax.fori_loop(0, nblk, drain_own, 0)
    for j in range(nblk):
        f_out(j, 0).wait()
    for j in range(nblk - 2, nblk):
        f_out(j, 1).wait()

    for q in range(parts):
        for stage in range(3):
            ra(stage, q).wait_send()
        if q < parts - 1:
            ra(3, q).wait_send()
    aa(2).wait_recv()
    oa_copy = pltpu.make_async_copy(done, oa_ref, loc_sem.at[nblk + 1])
    oa_copy.start()
    oa_copy.wait()
    xg_copy.wait()
    for stage in range(3):
        aa(stage).wait_send()


def finish(
    lo,
    xg,
    up,
    dn,
    at,
    sm,
    lo_out,
    xg_out,
    up_out,
    dn_out,
    qkv_out,
    out_out,
    g2_out,
    s2_out,
    bo_out,
    bd_out,
    g1_out,
    s1_out,
    qv_out,
    bup_out,
    lo_b,
    xg_b,
    up_b,
    dn_b,
    at_b,
    up_f,
    dn_f,
    at_f,
    in_sem,
    out_sem,
):
    hw = out_out.shape[0]
    qkvw = qkv_out.shape[0]
    ins = [
        pltpu.make_async_copy(src, dst, in_sem.at[i])
        for i, (src, dst) in enumerate(((up, up_b), (dn, dn_b), (at, at_b), (xg, xg_b), (lo, lo_b)))
    ]
    for cp in ins:
        cp.start()
    outs = []

    def send(src, dst):
        outs.append(pltpu.make_async_copy(src, dst, out_sem.at[len(outs)]))
        outs[-1].start()

    for i, ref in enumerate((g2_out, s2_out, bo_out, bd_out, g1_out, s1_out)):
        ref[...] = sm[i]
    qv_out[...] = sm[8:10, 0:hw]
    for j in range(bup_out.shape[0] // BLK):
        bup_out[j * BLK : (j + 1) * BLK] = sm[16 + j, 0:BLK]
    ins[0].wait()
    up_f[...] = up_b[...].astype(F32)
    send(up_f, up_out)
    ins[1].wait()
    dn_f[...] = dn_b[...].astype(F32)
    send(dn_f, dn_out)
    ins[2].wait()
    at_f[...] = at_b[...].astype(F32)
    send(at_f.at[pl.ds(0, qkvw), :], qkv_out)
    send(at_f.at[pl.ds(qkvw, hw), :], out_out)
    ins[3].wait()
    send(xg_b, xg_out)
    ins[4].wait()
    send(lo_b, lo_out)
    for cp in outs:
        cp.wait()


def local(
    x_in,
    cotangent,
    lengths,
    bucket_ids,
    bucket_weights,
    ln1_gain,
    ln1_bias,
    w_qkv,
    qv_bias,
    w_out,
    b_out,
    ln2_gain,
    ln2_bias,
    w_up,
    b_up,
    w_down,
    b_down,
):
    share, width = x_in.shape
    hw = w_qkv.shape[2]
    heads = hw // HD
    parts = 4
    fw = w_up.shape[1]
    nblk = fw // BLK
    piece = width // GROUP
    keys = 2 * share
    n_all = parts * nblk
    n_far = n_all - nblk
    vm = pl.BlockSpec(memory_space=pltpu.VMEM)
    sm = pl.BlockSpec(memory_space=pltpu.SMEM)
    hbm = pl.BlockSpec(memory_space=pl.ANY)
    dma = pltpu.SemaphoreType.DMA
    scratch = [
        pltpu.VMEM((n_all + nblk, 2, width, BLK), BF16),
        pltpu.VMEM((parts, width, 4 * hw), BF16),
        pltpu.VMEM((SLOTS_C, 2, 4 * piece, BLK), BF16),
        pltpu.VMEM((n_all, 2, 2 * piece, BLK), BF16),
        pltpu.VMEM((n_all, 2, piece, BLK), BF16),
        pltpu.VMEM((n_far, 2, piece, BLK), BF16),
        pltpu.VMEM((parts, 4 * piece, 4 * hw), BF16),
        pltpu.VMEM((parts, 2 * piece, 4 * hw), BF16),
        pltpu.VMEM((parts, piece, 4 * hw), BF16),
        pltpu.VMEM((parts - 1, piece, 4 * hw), BF16),
        pltpu.VMEM((keys, width), BF16),
        pltpu.VMEM((share, width), BF16),
        pltpu.VMEM((parts, share, 256), BF16),
        pltpu.VMEM((parts, keys, 256), BF16),
        pltpu.VMEM((parts, keys, 256), BF16),
        pltpu.VMEM((parts, share, 256), BF16),
        pltpu.VMEM((parts, share, 256), BF16),
        pltpu.VMEM((parts, share, 128), F32),
        pltpu.VMEM((3 * hw, share), BF16),
        pltpu.VMEM((2, heads, share, share), BF16),
        pltpu.VMEM((share, width), F32),
        pltpu.VMEM((share, width), F32),
        pltpu.VMEM((share, width), F32),
        pltpu.VMEM((parts, width, width), BF16),
        pltpu.VMEM((share, width), BF16),
        pltpu.VMEM((width, share), BF16),
        pltpu.VMEM((share, width), BF16),
        pltpu.VMEM((share, width), BF16),
        pltpu.VMEM((parts, 1, fw), F32),
        pltpu.VMEM((parts, 2, hw), F32),
        pltpu.VMEM((24, width), F32),
        pltpu.VMEM((16, width), F32),
        pltpu.VMEM((3, 24, width), F32),
        pltpu.VMEM((parts, 24, width), F32),
        pltpu.VMEM((3, 16, width), F32),
        pltpu.VMEM((parts, 16, width), F32),
        dma((2 * nblk + 5,)),
        dma((2, heads)),
        dma((3,)),
        dma((parts,)),
        dma((2,)),
        dma((6,)),
        dma((2, parts)),
        dma((3, parts)),
        dma((3, parts)),
        dma((n_far,)),
        dma((n_all,)),
        dma((3, n_all)),
        dma((3, n_all)),
        dma((n_all,)),
        dma((n_all,)),
        dma((n_all,)),
        dma((n_all,)),
        dma((n_all,)),
        dma((n_all,)),
        dma((n_far,)),
        dma((n_far,)),
        dma((3, nblk)),
        dma((3, nblk)),
        dma((parts,)),
        dma((parts,)),
        dma((parts,)),
        dma((parts,)),
        dma((parts,)),
        dma((parts,)),
        dma((parts,)),
        dma((parts,)),
        dma((3,)),
        dma((3,)),
        dma((2, 7)),
        dma((2, 7)),
        dma((2,)),
        pltpu.SemaphoreType.REGULAR,
    ]
    layer_out, x_grad, up, down, att, small, _ = pl.pallas_call(
        kernel,
        out_shape=[
            jax.ShapeDtypeStruct((share, width), BF16),
            jax.ShapeDtypeStruct((share, width), F32),
            jax.ShapeDtypeStruct((width, fw), BF16),
            jax.ShapeDtypeStruct((fw, width), BF16),
            jax.ShapeDtypeStruct((width, width), BF16),
            jax.ShapeDtypeStruct((24, width), F32),
            jax.ShapeDtypeStruct((parts * heads, 2, share, share), BF16),
        ],
        in_specs=[vm, hbm, sm, sm, sm, vm, vm, hbm, vm, hbm, vm, vm, vm, hbm, vm, hbm, vm],
        out_specs=[hbm, hbm, hbm, hbm, hbm, vm, hbm],
        scratch_shapes=scratch,
        compiler_params=pltpu.CompilerParams(
            collective_id=0, has_side_effects=True, vmem_limit_bytes=67043328
        ),
    )(
        x_in,
        cotangent,
        lengths,
        bucket_ids,
        bucket_weights,
        ln1_gain,
        ln1_bias,
        w_qkv.transpose(0, 2, 1),
        qv_bias,
        w_out,
        b_out,
        ln2_gain,
        ln2_bias,
        w_up,
        b_up,
        w_down,
        b_down,
    )
    dp = lax.axis_size("dp")
    if dp > GROUP:
        groups = [[g + GROUP * i for i in range(dp // GROUP)] for g in range(GROUP)]
        sums = lax.psum(
            tuple(g.astype(F32) for g in (up, down, att, small)), "dp", axis_index_groups=groups
        )
        up, down, att = (g.astype(BF16) for g in sums[:3])
        small = sums[3]
    flat = jax.ShapeDtypeStruct((width,), F32)
    outs = pl.pallas_call(
        finish,
        out_shape=[
            jax.ShapeDtypeStruct((share, width), BF16),
            jax.ShapeDtypeStruct((share, width), F32),
            jax.ShapeDtypeStruct((width, fw), F32),
            jax.ShapeDtypeStruct((fw, width), F32),
            jax.ShapeDtypeStruct((3 * hw, width), F32),
            jax.ShapeDtypeStruct((hw, width), F32),
            flat,
            flat,
            flat,
            flat,
            flat,
            flat,
            jax.ShapeDtypeStruct((2, hw), F32),
            jax.ShapeDtypeStruct((fw,), F32),
        ],
        in_specs=[hbm] * 5 + [vm],
        out_specs=[hbm] * 6 + [vm] * 8,
        scratch_shapes=[
            pltpu.VMEM((share, width), BF16),
            pltpu.VMEM((share, width), F32),
            pltpu.VMEM((width, fw), BF16),
            pltpu.VMEM((fw, width), BF16),
            pltpu.VMEM((width, width), BF16),
            pltpu.VMEM((width, fw), F32),
            pltpu.VMEM((fw, width), F32),
            pltpu.VMEM((width, width), F32),
            dma((5,)),
            dma((7,)),
        ],
    )(layer_out, x_grad, up, down, att, small)
    layer_out, x_grad, g_up, g_down, g_qkv, g_out, g2, s2, bo, bd, g1, s1, g_qv, g_bup = outs
    return (
        layer_out,
        x_grad,
        g1,
        s1,
        g_qkv.reshape(3, hw, width).transpose(0, 2, 1),
        g_qv,
        g_out,
        bo,
        g2,
        s2,
        g_up,
        g_bup,
        g_down,
        bd,
    )


def solution(mesh):
    return jax.shard_map(
        local,
        mesh=mesh,
        in_specs=(
            P(("dp", "tensor"), None),
            P(("dp", "tensor"), None),
            P("dp", None),
            P("dp"),
            P(),
            P(),
            P(),
            P(None, None, "tensor"),
            P(None, "tensor"),
            P("tensor", None),
            P(),
            P(),
            P(),
            P(None, "tensor"),
            P("tensor"),
            P("tensor", None),
            P(),
        ),
        out_specs=(
            P(("dp", "tensor"), None),
            P(("dp", "tensor"), None),
            P(),
            P(),
            P(None, None, "tensor"),
            P(None, "tensor"),
            P("tensor", None),
            P(),
            P(),
            P(),
            P(None, "tensor"),
            P("tensor"),
            P("tensor", None),
            P(),
        ),
        check_vma=False,
    )
```

```python
import functools
import math

import jax
import jax.numpy as jnp
from jax import lax
from jax.experimental import pallas as pl
from jax.experimental.pallas import tpu as pltpu
from jax.sharding import PartitionSpec as P

HD = 32
BUCKET = 256
EPSILON = 1e-05
GROUP = 8
BLK = 256
BIG = 1e30
F32 = jnp.float32
BF16 = jnp.bfloat16
MESH = pl.DeviceIdType.MESH
RSQRT2 = 1.0 / math.sqrt(2.0)
RSQRT2PI = 1.0 / math.sqrt(2.0 * math.pi)
SLOTS_C = 2
X_PLACE = 4
CUTS = ((0, 256), (256, 384))
PLAN = {
    "p0": (
        ("a0", (0, 1)),
        ("a1", (0, 1)),
    ),
    "p1": (
        ("a2", (0, 1)),
    ),
    "p2": (
        ("a0", (1, 3)),
    ),
    "pj": (
        ("a1", (1, 3)),
        ("a2", (1, 3)),
    ),
    "o": (
        ("g0", (0, 0, 0, 1, 2)),
    ),
    "q": (
        ("g0", (2, 8, 10, 15, 15)),
        ("g1", (0, 2, 4, 6, 10)),
        ("g2", (0, 0, 0, 1, 3)),
    ),
    "mid": (
        ("g1", (10, 11)),
        ("g2", (3, 5)),
    ),
    "r": (
        ("g1", (11, 12, 15, 15, 15, 15, 15, 15, 15, 15, 15, 15, 15, 15, 15, 15, 15, 15, 15, 15, 15)),
        ("g2", (5, 5, 6, 8, 10, 10, 13, 15, 15, 15, 15, 15, 15, 15, 15, 15, 15, 15, 15, 15, 15)),
        ("rf", (0, 0, 0, 0, 0, 0, 0, 0, 0, 0, 0, 0, 0, 2, 2, 2, 2, 2, 2, 3, 3)),
        ("r1", (0, 0, 0, 0, 0, 0, 0, 0, 0, 0, 1, 2, 2, 2, 3, 3, 4, 4, 4, 6, 10)),
        ("r2", (0, 0, 0, 0, 0, 0, 0, 1, 2, 3, 4, 4, 6, 6, 7, 8, 10, 10, 11, 11, 14)),
    ),
    "ln": (
        ("rf", (3, 5)),
    ),
    "k": (
        ("rf", (5, 5, 6, 6, 6)),
        ("r1", (10, 10, 11, 11, 11)),
        ("r2", (14, 15, 15, 17, 18)),
    ),
    "h": (
        ("rf", (6, 9, 11, 11, 13)),
        ("r1", (11, 11, 15, 15, 18)),
        ("r2", (18, 18, 19, 19, 20)),
    ),
    "w": (
        ("rf", (13, 18, 18, 19, 20)),
        ("r1", (18, 19, 20, 20, 20)),
        ("b3", (0, 0, 0, 0, 1)),
        ("b2", (0, 0, 0, 1, 3)),
        ("b1", (0, 0, 1, 3, 4)),
        ("f0", (0, 3, 3, 4, 4)),
        ("f1", (0, 0, 1, 2, 2)),
        ("f2", (0, 0, 0, 0, 2)),
    ),
}
TAIL = (
    ("v", 0, 0),
    ("b2", 3, 4),
    ("b3", 1, 3),
    ("f0", 4, 5),
    ("f1", 2, 5),
    ("b3", 3, 4),
    ("aa0", 0, 0),
    ("v", 0, 0),
    ("ng", 0, 0),
    ("v", 0, 0),
    ("f2", 2, 5),
    ("aa1", 0, 0),
    ("aa2", 0, 0),
)


def nn(a, b):
    return lax.dot_general(a, b, (((1,), (0,)), ((), ())), preferred_element_type=F32)


def nt(a, b):
    return lax.dot_general(a, b, (((1,), (1,)), ((), ())), preferred_element_type=F32)


def unit_of(values):
    centre = values - jnp.mean(values, axis=-1, keepdims=True)
    scale_inv = lax.rsqrt(jnp.mean(centre * centre, axis=-1, keepdims=True) + EPSILON)
    return centre * scale_inv, scale_inv


def norm_back(grad, unit, scale_inv, gain):
    scaled = grad * gain
    return scale_inv * (
        scaled
        - jnp.mean(scaled, axis=-1, keepdims=True)
        - unit * jnp.mean(scaled * unit, axis=-1, keepdims=True)
    )


def lanes(shape):
    return lax.broadcasted_iota(jnp.int32, shape, 1)


def kernel(
    x_ref,
    cot_ref,
    len_ref,
    bid_ref,
    bw_ref,
    g1_ref,
    s1_ref,
    wqkv_ref,
    qvb_ref,
    wout_ref,
    bout_ref,
    g2_ref,
    s2_ref,
    wup_ref,
    bup_ref,
    wdn_ref,
    bdn_ref,
    lo_ref,
    xg_ref,
    ou_ref,
    od_ref,
    oa_ref,
    osm_ref,
    ph_ref,
    fg,
    aw,
    rc_f,
    r2_f,
    r1_f,
    rz_f,
    rc_a,
    r2_a,
    r1_a,
    rz_a,
    xn,
    xp,
    qb,
    kb,
    vb,
    mx,
    dmx,
    stat,
    dd,
    pst,
    mid,
    acc0,
    acc1,
    uu,
    ol,
    olt,
    ngs,
    ngr,
    bupa,
    qvba,
    early,
    late,
    e_rx,
    e_rz,
    l_rx,
    l_rz,
    loc_sem,
    ps_sem,
    za_s,
    za_r,
    zx_sem,
    zb_s,
    zb_r,
    ga_s,
    ga_r,
    zf_s,
    zf_r,
    gf_s,
    gf_r,
    cf_s,
    cf_r,
    f2_s,
    f2_r,
    f1_s,
    f1_r,
    fz_s,
    fz_r,
    af_s,
    af_r,
    ra_s,
    ra_r,
    aa_s,
    aa_r,
    sm_s,
    sm_r,
    ng_sem,
    credit,
):
    share, width = x_ref.shape
    hw = wqkv_ref.shape[1]
    heads = hw // HD
    qkvw = 3 * hw
    parts = 4
    nblk = wup_ref.shape[1] // BLK
    piece = width // GROUP
    keys = 2 * share
    factor = HD ** (-0.5)
    q_scale = factor * math.log2(math.e)

    d = lax.axis_index("dp")
    t = lax.axis_index("tensor")
    c = d % 2
    bx = (d // 2) % 2
    by = (d // 4) % 2
    dev_c = (d + 1 - 2 * c, t)
    dx = d + 2 - 4 * bx
    dy = d + 4 - 8 * by
    tp = t + 1 - 2 * (t % 2)

    def far(k):
        low_t, high_t, low_k, high_k = t % 2, t // 2, k % 2, k // 2
        return low_t + low_k - 2 * low_t * low_k + 2 * (high_t + high_k - 2 * high_t * high_k)

    def route(par):
        low = bx + par * (by - bx)
        high = by + par * (bx - by)
        first = (dx + par * (dy - dx), t)
        second = (dy + par * (dx - dy), t)
        return low, high, first, second

    def rcopy(src, dst, ssem, rsem, dev):
        return pltpu.make_async_remote_copy(
            src_ref=src, dst_ref=dst, send_sem=ssem, recv_sem=rsem, device_id=dev, device_id_type=MESH
        )

    def rows(start, size):
        return pl.ds(pl.multiple_of(start, 16), size)

    def up_load(j):
        return pltpu.make_async_copy(
            wup_ref.at[:, pl.ds(j * BLK, BLK)], fg.at[t * nblk + j, 0], loc_sem.at[j]
        )

    def dn_load(j):
        return pltpu.make_async_copy(
            wdn_ref.at[pl.ds(j * BLK, BLK), :],
            uu.at[j // 2, pl.ds((j % 2) * BLK, BLK), :],
            loc_sem.at[nblk + j],
        )

    cot_load = pltpu.make_async_copy(cot_ref, ol, loc_sem.at[2 * nblk])

    a_loads = [
        pltpu.make_async_copy(
            wqkv_ref.at[i], aw.at[t, pl.ds(i * hw, hw), :], loc_sem.at[2 * nblk + 1 + i]
        )
        for i in range(3)
    ]
    a_loads.append(
        pltpu.make_async_copy(
            wout_ref, aw.at[t, pl.ds(qkvw, hw), :], loc_sem.at[2 * nblk + 4]
        )
    )
    for cp in a_loads:
        cp.start()
    for j in range(nblk):
        dn_load(j).start()
        up_load(j).start()
    cot_load.start()
    bupa[t] = bup_ref[...][None, :]
    qvba[t] = qvb_ref[...]

    barrier = pltpu.get_barrier_semaphore()
    for dev in (dev_c, (dx, t), (dy, t), (d, far(1)), (d, far(2)), (d, far(3))):
        pl.semaphore_signal(barrier, inc=1, device_id=dev, device_id_type=MESH)
    pl.semaphore_wait(barrier, 6)

    def a_rows(stage, s, a):
        low, high, _, _ = route((s + a) % 2)
        if stage == 0:
            return rows((c * 4 + high * 2 + low) * piece, piece)
        if stage == 1:
            return rows((c * 4 + high * 2) * piece, 2 * piece)
        return rows(c * 4 * piece, 4 * piece)

    def a_lanes(a):
        return pl.ds(CUTS[a][0], CUTS[a][1])

    def za(k, a):
        view = aw.at[t, a_rows(0, t, a), a_lanes(a)]
        return rcopy(view, view, za_s.at[a, k - 1], za_r.at[a, t], (d, far(k)))

    def za_wait(s, a):
        view = aw.at[s, a_rows(0, s, a), a_lanes(a)]
        rcopy(view, view, za_s.at[a, 0], za_r.at[a, s], (d, t)).wait_recv()

    def zb(k, which):
        dst = (bupa if which == 0 else qvba).at[t]
        return rcopy(dst, dst, zb_s.at[2 * (k - 1) + which], zb_r.at[which, t], (d, far(k)))

    def zb_wait(s, which):
        dst = (bupa if which == 0 else qvba).at[s]
        rcopy(dst, dst, zb_s.at[0], zb_r.at[which, s], (d, t)).wait_recv()

    x_copy = rcopy(x_ref, xp, zx_sem.at[0], zx_sem.at[1], (d, tp))

    for cp in a_loads:
        cp.wait()
    for k in range(1, parts):
        for a in range(2):
            za(k, a).start()
        zb(k, 1).start()
    for k in range(1, parts):
        zb(k, 0).start()

    def ga(stage, s, a):
        _, _, first, second = route((s + a) % 2)
        view = aw.at[s, a_rows(stage, s, a), a_lanes(a)]
        dev = (first, second, dev_c)[stage]
        return rcopy(view, view, ga_s.at[stage, a, s], ga_r.at[stage, a, s], dev)

    def step_a(stage, i):
        s = far(i + 1)
        for a in range(2):
            if stage == 0:
                za_wait(s, a)
            else:
                ga(stage - 1, s, a).wait_recv()
            ga(stage, s, a).start()

    n_far = (parts - 1) * nblk

    def far_block(m):
        s = far(1 + m % (parts - 1))
        j = m // (parts - 1)
        return s, j, s * nblk + j

    def gf(stage, m):
        s, j, b = far_block(m)
        low, high, first, second = route((s + j) % 2)
        if stage == 0:
            view, dev = fg.at[b, :, rows((c * 4 + high * 2 + low) * piece, piece), :], first
        elif stage == 1:
            view, dev = fg.at[b, :, rows((c * 4 + high * 2) * piece, 2 * piece), :], second
        else:
            view, dev = fg.at[b, :, rows(c * 4 * piece, 4 * piece), :], dev_c
        return rcopy(view, view, gf_s.at[stage, b], gf_r.at[stage, b], dev)

    def zf_wait(m):
        s, j, b = far_block(m)
        low, high, _, _ = route((s + j) % 2)
        view = fg.at[b, :, rows((c * 4 + high * 2 + low) * piece, piece), :]
        rcopy(view, view, zf_s.at[0], zf_r.at[b], (d, t)).wait_recv()

    def within(n, size):
        return (n >= 0) & (n < size)

    def step_g(stage, m):
        if stage == 0:
            zf_wait(m)
        else:
            gf(stage - 1, m).wait_recv()
        gf(stage, m).start()

    n_all = parts * nblk

    def block(r):
        own = jnp.where(r < nblk, 1, 0)
        m = r - nblk
        k = (1 - own) * (1 + m % (parts - 1))
        j = own * r + (1 - own) * (m // (parts - 1))
        s = far(k)
        home = s * nblk + j
        return k, j, s, home, home + own * (n_all + j - home)

    def rf(stage, r):
        k, j, s, _, g = block(r)
        low, high, first, second = route((s + j) % 2)
        if stage == 0:
            return rcopy(
                fg.at[g, :, rows((1 - c) * 4 * piece, 4 * piece), :],
                rc_f.at[r % SLOTS_C],
                cf_s.at[r],
                cf_r.at[r],
                dev_c,
            )
        if stage == 1:
            return rcopy(
                fg.at[g, :, rows((c * 4 + (1 - high) * 2) * piece, 2 * piece), :],
                r2_f.at[r],
                f2_s.at[r],
                f2_r.at[r],
                second,
            )
        if stage == 2:
            return rcopy(
                fg.at[g, :, rows((c * 4 + high * 2 + 1 - low) * piece, piece), :],
                r1_f.at[r],
                f1_s.at[r],
                f1_r.at[r],
                first,
            )
        z = jnp.maximum((k - 1) * nblk + j, 0)
        return rcopy(
            fg.at[g, :, rows((c * 4 + high * 2 + low) * piece, piece), :],
            rz_f.at[z],
            fz_s.at[z],
            fz_r.at[z],
            (d, s),
        )

    def add_rows(ref, got):
        ref[...] = (ref[...].astype(F32) + got[...].astype(F32)).astype(BF16)

    def rf_core(r):
        _, _, _, _, g = block(r)
        rf(0, r).wait_recv()
        add_rows(fg.at[g, :, rows(c * 4 * piece, 4 * piece), :], rc_f.at[r % SLOTS_C])

        @pl.when(r < n_all - SLOTS_C)
        def _():
            pl.semaphore_signal(credit, inc=1, device_id=dev_c, device_id_type=MESH)

    def turn(i):
        return (i + nblk) % n_all

    def rf_first(r):
        k, j, s, _, g = block(r)
        low, high, _, _ = route((s + j) % 2)
        rf(1, r).wait_recv()
        add_rows(fg.at[g, :, rows((c * 4 + high * 2) * piece, 2 * piece), :], r2_f.at[r])
        rf(2, r).start()

    def rf_far(r):
        k, j, s, _, g = block(r)
        low, high, _, _ = route((s + j) % 2)
        rf(2, r).wait_recv()
        add_rows(fg.at[g, :, rows((c * 4 + high * 2 + low) * piece, piece), :], r1_f.at[r])

        @pl.when(r >= nblk)
        def _():
            rf(3, r).start()

    def af(stage, j):
        low, high, first, second = route((t + j) % 2)
        b = t * nblk + j
        if stage == 0:
            view, dev = fg.at[b, :, rows((c * 4 + high * 2 + low) * piece, piece), :], first
        elif stage == 1:
            view, dev = fg.at[b, :, rows((c * 4 + high * 2) * piece, 2 * piece), :], second
        else:
            view, dev = fg.at[b, :, rows(c * 4 * piece, 4 * piece), :], dev_c
        return rcopy(view, view, af_s.at[stage, j], af_r.at[stage, j], dev)

    def f_final(j):
        low, high, _, _ = route((t + j) % 2)
        mine = rows((c * 4 + high * 2 + low) * piece, piece)
        total = fg[n_all + j, :, mine, :].astype(F32)
        for k in range(1, parts):
            z = (k - 1) * nblk + j
            rcopy(rz_f.at[z], rz_f.at[z], fz_s.at[z], fz_r.at[z], (d, t)).wait_recv()
            total = total + rz_f[z].astype(F32)
        fg[t * nblk + j, :, mine, :] = total.astype(BF16)
        af(0, j).start()

    def f_out(j, which):
        if which == 0:
            return pltpu.make_async_copy(
                fg.at[t * nblk + j, 0], ou_ref.at[:, pl.ds(j * BLK, BLK)], loc_sem.at[j]
            )
        return pltpu.make_async_copy(
            ol.at[pl.ds((j % 2) * BLK, BLK), :],
            od_ref.at[pl.ds(j * BLK, BLK), :],
            loc_sem.at[nblk + 2 + j % 2],
        )

    def f_second(j):
        af(0, j).wait_recv()
        af(1, j).start()

    def f_third(j):
        af(1, j).wait_recv()
        af(2, j).start()

    def ra_view(stage, s, a):
        low, high, first, second = route((s + a) % 2)
        if stage == 0:
            return rows((1 - c) * 4 * piece, 4 * piece), rc_a, dev_c
        if stage == 1:
            return rows((c * 4 + (1 - high) * 2) * piece, 2 * piece), r2_a, second
        if stage == 2:
            return rows((c * 4 + high * 2 + 1 - low) * piece, piece), r1_a, first
        return rows((c * 4 + high * 2 + low) * piece, piece), rz_a, (d, s)

    def ra(stage, q, a):
        s = group_of(q)
        where, buf, dev = ra_view(stage, s, a)
        if stage == 3:
            q = jnp.minimum(q, parts - 2)
        return rcopy(
            aw.at[s, where, a_lanes(a)],
            buf.at[q, :, a_lanes(a)],
            ra_s.at[stage, a, q],
            ra_r.at[stage, a, q],
            dev,
        )

    def ra_add(stage, q, a):
        s = group_of(q)
        buf = (rc_a, r2_a, r1_a)[stage]
        ra(stage, q, a).wait_recv()
        add_rows(aw.at[s, a_rows(2 - stage, s, a), a_lanes(a)], buf.at[q, :, a_lanes(a)])

    def group_of(it):
        return far((it + 1) % parts)

    def step_b(stage, q):
        for a in range(2):
            ra_add(stage - 1, q, a)
        for a in range(2):
            if stage < 3:
                ra(stage, q, a).start()
            else:

                @pl.when(q < parts - 1)
                def _():
                    ra(3, q, a).start()

    steps = {
        "a0": lambda i: step_a(0, i),
        "a1": lambda i: step_a(1, i),
        "a2": lambda i: step_a(2, i),
        "g0": lambda i: step_g(0, i),
        "g1": lambda i: step_g(1, i),
        "g2": lambda i: step_g(2, i),
        "r2": lambda i: rf(1, turn(i)).start(),
        "r1": lambda i: rf_first(turn(i)),
        "rf": lambda i: rf_far(turn(i)),
        "b1": lambda i: step_b(1, i),
        "b2": lambda i: step_b(2, i),
        "b3": lambda i: step_b(3, i),
        "f0": lambda i: f_final(i),
        "f1": lambda i: f_second(i),
        "f2": lambda i: f_third(i),
    }

    def repeat(name, low, high):
        def one(i, carry):
            steps[name](i)
            return carry

        lax.fori_loop(low, high, one, 0)

    def advance(place, idx=0):
        for name, counts in PLAN[place]:
            if len(counts) == 2:
                repeat(name, counts[0], counts[1])
                continue
            low = counts[0]
            high = counts[0]
            for i in range(1, len(counts)):
                more = counts[i] - counts[i - 1]
                if more:
                    low = low + jnp.where(idx >= i, more, 0)
                    high = high + jnp.where(idx >= i - 1, more, 0)
            repeat(name, low, high)

    gain1 = g1_ref[...][None, :]
    shift1 = s1_ref[...][None, :]
    unit, _ = unit_of(x_ref[...].astype(F32))
    xn[0:share, :] = (unit * gain1 + shift1).astype(BF16)
    advance("p0")

    def zf(k, j):
        low, high, _, _ = route((t + j) % 2)
        view = fg.at[t * nblk + j, :, rows((c * 4 + high * 2 + low) * piece, piece), :]
        return rcopy(
            view, view, zf_s.at[(k - 1) * nblk + j], zf_r.at[t * nblk + j], (d, far(k))
        )

    for j in range(nblk):
        up_load(j).wait()
        dn_load(j).wait()
        fg[t * nblk + j, 1] = uu[j // 2, (j % 2) * BLK : (j % 2 + 1) * BLK, :].T
    for m in range((parts - 1) * nblk):
        if m == X_PLACE:
            x_copy.start()
        zf(1 + m % (parts - 1), m // (parts - 1)).start()

    advance("p1")

    bucket = bid_ref[0]
    span = jnp.where(bucket == 0, BUCKET, jnp.where(bucket == 1, 2 * BUCKET, 4 * BUCKET))
    weight = jnp.where(bucket == 0, bw_ref[0], jnp.where(bucket == 1, bw_ref[1], bw_ref[2]))

    def slot_info(base, shape):
        place = base + lax.broadcasted_iota(jnp.int32, shape, 0)
        item = jnp.zeros(shape, jnp.int32)
        for j in range(1, len_ref.shape[1]):
            item = item + jnp.where(place >= j * span, 1, 0)
        length = jnp.zeros(shape, jnp.int32)
        for j in range(len_ref.shape[1]):
            length = jnp.where(item == j, len_ref[0, j], length)
        return item, (place - item * span) < length

    wide = (share, 2 * 128)
    lane = lanes(wide)
    slots = len_ref.shape[1]
    in_aux = (lane >= hw) & (lane < hw + slots)
    one_aux = jnp.where(lane >= hw, 1.0, 0.0).astype(BF16)

    own_item, own_live = slot_info(t * share, wide)
    q_aux = jnp.where(in_aux & (own_item == lane - hw), 1.0, 0.0).astype(BF16)
    k_aux0 = jnp.where(in_aux & ~((own_item == lane - hw) & own_live), -BIG, 0.0).astype(BF16)
    pair_item, pair_live = slot_info(tp * share, wide)
    k_aux1 = jnp.where(in_aux & ~((pair_item == lane - hw) & pair_live), -BIG, 0.0).astype(BF16)
    for s in range(parts):
        qb[s] = q_aux
        kb[s, 0:share] = k_aux0
        kb[s, share:keys] = k_aux1
        vb[s, 0:share] = one_aux
        vb[s, share:keys] = one_aux
    _, live1 = slot_info(t * share, (share, 128))
    row_weight = jnp.where(live1, weight, 0.0)[:, 0:1]

    advance("p2")

    def project(s, half, own):
        base = half * share
        first = 0 if own else hw
        out = nt(xn[base : base + share, :], aw[s, first:qkvw, :])
        if own:
            qb[s, :, 0:hw] = ((out[:, 0:hw] + qvba[s, 0:1, :]) * q_scale).astype(BF16)
        at = hw - first
        kb[s, base : base + share, 0:hw] = out[:, at : at + hw].astype(BF16)
        vb[s, base : base + share, 0:hw] = (
            out[:, at + hw : at + 2 * hw] + qvba[s, 1:2, :]
        ).astype(BF16)

    lane_w = lanes((share, 2 * 128))
    lane_n = lanes((share, 128))

    def head_lanes(h):
        return (lane_w >= HD * h) & (lane_w < HD * (h + 1))

    def spread(values, at):
        out = jnp.zeros((share, 2 * 128), F32)
        for h in range(heads):
            out = jnp.where(head_lanes(h), values[:, at + h : at + h + 1], out)
        return out

    def p_out(s, h, half, buf):
        return pltpu.make_async_copy(
            pst.at[buf, h], ph_ref.at[s * heads + h, half], ps_sem.at[buf, h]
        )

    at0 = hw - 128
    at1 = at0 + 32
    at2 = at0 + 64

    def att_forward(k, half):
        s = far(k)
        base = half * share
        buf = k % 2
        if half == 1:
            for h in range(heads):
                p_out(s, h, half, buf).wait()
        else:

            @pl.when(k >= 2)
            def _():
                for h in range(heads):
                    p_out(s, h, half, buf).wait()

        qg = qb[s]
        kg = kb[s, base : base + share]
        vg = vb[s, base : base + share]
        out = jnp.zeros((share, 2 * 128), F32)
        tops = jnp.zeros((share, 128), F32)
        for h in range(heads):
            head = head_lanes(h)
            qm = jnp.where(head | (lane_w >= hw), qg, jnp.zeros_like(qg))
            scores = nt(qm, kg)
            top = jnp.max(scores, axis=1, keepdims=True)
            probs = jnp.exp2(scores - top).astype(BF16)
            pst[buf, h] = probs
            mixed = nn(probs, vg)
            out = jnp.where(head | (lane_w == hw + h), mixed, out)
            tops = jnp.where(lane_n == at0 + h, top, tops)
        for h in range(heads):
            p_out(s, h, half, buf).start()
        sums = jnp.where((lane_n >= at0) & (lane_n < at0 + heads), out[:, 128:256], 1.0)
        log_sum = tops + jnp.log2(sums)
        if half == 0:
            mx[s] = (out * spread(1.0 / sums, at0)).astype(BF16)
            stat[s] = jnp.where(lane_n < at1, tops, pltpu.roll(log_sum, 32, 1))
        else:
            before = stat[s]
            log_before = pltpu.roll(before, 96, 1)
            upper = jnp.maximum(log_sum, log_before)
            lower = jnp.minimum(log_sum, log_before)
            log_all = upper + jnp.log2(1.0 + jnp.exp2(lower - upper))
            part0 = jnp.exp2(log_before - log_all)
            part1 = jnp.exp2(log_sum - log_all) / sums
            mx[s] = (
                mx[s].astype(F32) * spread(part0, at0) + out * spread(part1, at0)
            ).astype(BF16)
            stat[s] = jnp.where(
                lane_n < at1,
                jnp.exp2(before - log_all),
                pltpu.roll(jnp.exp2(tops - log_all), 32, 1),
            )

    def own_keys(k, carry):
        s = far(k)

        @pl.when(k > 0)
        def _():
            zb_wait(s, 1)
            for a in range(2):
                ga(2, s, a).wait_recv()

        project(s, 0, True)

        @pl.when(k == 0)
        def _():
            advance("pj")

        att_forward(k, 0)
        advance("o", k)
        return carry

    lax.fori_loop(0, parts, own_keys, 0)

    x_copy.wait_recv()
    unit, _ = unit_of(xp[...].astype(F32))
    xn[share:keys, :] = (unit * gain1 + shift1).astype(BF16)

    def pair_keys(k, carry):
        project(far(k), 1, False)
        att_forward(k, 1)
        advance("q", k)
        return carry

    lax.fori_loop(0, parts, pair_keys, 0)
    for buf in range(2):
        for h in range(heads):
            p_out(0, h, 1, buf).wait()

    branch = jnp.zeros((share, width), F32)
    for s in range(parts):
        branch = branch + nn(mx[s, :, 0:hw], aw[s, qkvw : 4 * hw, :])
    middle = x_ref[...].astype(F32) + (branch + bout_ref[...][None, :])
    mid[...] = middle
    unit, _ = unit_of(middle)
    normed = (unit * g2_ref[...][None, :] + s2_ref[...][None, :]).astype(BF16)
    n2 = uu.at[0, 0:share, :]
    n2t = uu.at[1, :, 0:share]
    n2[...] = normed
    n2t[...] = normed.T
    cot_load.wait()
    low_grad = (ol[...].astype(F32) * row_weight).astype(BF16)
    early[...] = jnp.zeros_like(early)
    late[...] = jnp.zeros_like(late)
    early[3:4, :] = jnp.sum(low_grad.astype(F32), axis=0, keepdims=True)
    ol[...] = low_grad
    olt[...] = low_grad.T
    acc0[...] = jnp.zeros_like(acc0)
    acc1[...] = jnp.zeros_like(acc1)

    for k in range(1, parts):
        zb_wait(far(k), 0)
    advance("mid")

    def drain_zf(m, carry):
        view = fg.at[0, :, 0:piece, :]
        rcopy(view, view, zf_s.at[m], zf_r.at[0], (d, t)).wait_send()
        return carry

    def ffn(r, carry):
        k, j, s, home, g = block(r)

        @pl.when(k > 0)
        def _():
            gf(2, jnp.maximum(r - nblk, 0)).wait_recv()

        wu = fg[home, 0]
        wd = fg[home, 1]
        hidden = nn(n2[...], wu) + bupa[s, :, pl.ds(pl.multiple_of(j * BLK, BLK), BLK)]
        cdf = 0.5 + 0.5 * lax.erf(hidden * RSQRT2)
        slope = cdf + hidden * (jnp.exp(-0.5 * hidden * hidden) * RSQRT2PI)
        active = (hidden * cdf).astype(BF16)
        act_grad = nn(ol[...], wd)
        hid_grad = (slope * act_grad).astype(BF16)
        acc0[...] += nt(active, wd)
        acc1[...] += nt(hid_grad, wu)
        early[pl.ds(4 + home, 1), 0:BLK] = jnp.sum(hid_grad.astype(F32), axis=0, keepdims=True)
        up_grad = nn(n2t[...], hid_grad).astype(BF16)
        dn_grad = nn(olt[...], active).astype(BF16)

        @pl.when(k > 0)
        def _():
            for stage in range(3):
                gf(stage, jnp.maximum(r - nblk, 0)).wait_send()

        fg[g, 0] = up_grad
        fg[g, 1] = dn_grad

        @pl.when(r == 2 * nblk)
        def _():
            lax.fori_loop(0, n_far, drain_zf, 0)

        @pl.when(r >= SLOTS_C)
        def _():
            pl.semaphore_wait(credit, 1)

        rf(0, r).start()

        @pl.when(r > 0)
        def _():
            rf_core(r - 1)

        advance("r", r)
        return carry

    lax.fori_loop(0, n_all, ffn, 0)
    rf_core(n_all - 1)

    middle = mid[...]
    ngs[...] = (middle + (acc0[...] + bdn_ref[...][None, :])).astype(BF16)
    lo_copy = pltpu.make_async_copy(ngs, lo_ref, loc_sem.at[2 * nblk])
    lo_copy.start()
    unit, scale_inv = unit_of(middle)
    got = acc1[...]
    early[0:1, :] = jnp.sum(got * unit, axis=0, keepdims=True)
    early[1:2, :] = jnp.sum(got, axis=0, keepdims=True)
    middle_part = norm_back(got, unit, scale_inv, g2_ref[...][None, :])
    reload = pltpu.make_async_copy(cot_ref, ol, loc_sem.at[0])
    reload.start()
    reload.wait()
    out_grad = ol[...].astype(F32) * row_weight
    middle_grad = out_grad + middle_part
    mid[...] = middle_grad
    branch_low = middle_grad.astype(BF16)
    early[2:3, :] = jnp.sum(branch_low.astype(F32), axis=0, keepdims=True)
    ol[...] = branch_low

    for k in range(1, parts):
        for a in range(2):
            za(k, a).wait_send()
            for stage in range(3):
                ga(stage, far(k), a).wait_send()
    advance("ln")

    head_row = lax.broadcasted_iota(jnp.int32, (hw, 128), 0)
    head_col = (lax.broadcasted_iota(jnp.int32, (hw, 128), 1) - at2) * HD
    pick = jnp.where((head_row >= head_col) & (head_row < head_col + HD), 1.0, 0.0).astype(BF16)

    def out_back(k, carry):
        s = far(k)
        mixed = mx[s, :, 0:hw]
        mixed_grad = nt(ol[...], aw[s, qkvw : 4 * hw, :]).astype(BF16)
        dmx[s, :, 0:hw] = mixed_grad
        prod = mixed_grad.astype(F32) * mixed.astype(F32)
        coarse = prod.astype(BF16)
        fine = (prod - coarse.astype(F32)).astype(BF16)
        delta = nn(coarse, pick) + nn(fine, pick)
        stat[s] = jnp.where((lane_n >= at2) & (lane_n < at2 + heads), delta, stat[s])
        aw[s, qkvw : 4 * hw, :] = nn(mixed.T, ol[...]).astype(BF16)
        advance("k", k)
        return carry

    lax.fori_loop(0, parts, out_back, 0)

    def p_in(s, h, half, buf):
        return pltpu.make_async_copy(
            ph_ref.at[s * heads + h, half], pst.at[buf, h], ps_sem.at[buf, h]
        )

    def fetch(it):
        for h in range(heads):
            p_in(group_of(it), h, 1 - it // parts, it % 2).start()

    def att_group(it, half):
        s = group_of(it)
        base = half * share
        buf = it % 2

        @pl.when(it + 1 < 2 * parts)
        def _():
            fetch(it + 1)

        for h in range(heads):
            p_in(s, h, half, buf).wait()
        known = stat[s]
        wanted = known if half == 0 else pltpu.roll(known, 96, 1)
        delta = -(pltpu.roll(known, 64, 1) * wanted)
        coarse = delta.astype(BF16).astype(F32)
        aux = jnp.where((lane_n >= at0) & (lane_n < at0 + heads), coarse, 0.0)
        aux = jnp.where(
            (lane_n >= at0 + 8) & (lane_n < at0 + 8 + heads), pltpu.roll(delta - coarse, 8, 1), aux
        )
        scaled = dmx[s].astype(F32) * spread(wanted, at0)
        dg = jnp.concatenate(
            [scaled[:, 0:128], jnp.where(lane_n < at0, scaled[:, 128:256], aux)], axis=1
        ).astype(BF16)
        qg = qb[s]
        kg = kb[s, base : base + share]
        vg = vb[s, base : base + share]
        qt = qg[:, 0:hw].T
        dt = dg[:, 0:hw].T
        dq = jnp.zeros((share, 2 * 128), F32)
        dks = []
        dvs = []
        for h in range(heads):
            head = head_lanes(h)
            aux_h = (lane_w == hw + h) | (lane_w == hw + 8 + h)
            dm = jnp.where(head | aux_h, dg, jnp.zeros_like(dg))
            prob_grad = nt(dm, vg)
            probs = pst[buf, h]
            score_grad = (probs.astype(F32) * prob_grad).astype(BF16)
            dq = jnp.where(head, nn(score_grad, kg), dq)
            dks.append(nn(qt[HD * h : HD * (h + 1)], score_grad))
            dvs.append(nn(dt[HD * h : HD * (h + 1)], probs))
        dqt = (dq[:, 0:hw] * factor).T
        dkt = (jnp.concatenate(dks, axis=0) * math.log(2.0)).astype(BF16)
        dvt = jnp.concatenate(dvs, axis=0).astype(BF16)
        return s, dqt, dkt, dvt

    acc0[...] = jnp.zeros_like(acc0)
    acc1[...] = jnp.zeros_like(acc1)
    dmx_pad = jnp.zeros((share, 2 * 128 - hw), BF16)
    for s in range(parts):
        dmx[s, :, hw : 2 * 128] = dmx_pad
    fetch(0)

    def row_sums(values):
        return jnp.sum(values.astype(F32), axis=0, keepdims=True)

    def pair_half(it, carry):
        s, dqt, dkt, dvt = att_group(it, 1)
        uu[s, 0:hw, 0:share] = dqt.astype(BF16)
        uu[s, hw : 2 * hw, 0:share] = dkt
        uu[s, 2 * hw : qkvw, 0:share] = dvt
        back = uu[s, hw:qkvw, 0:share].T
        acc0[...] += nn(back, aw[s, hw:qkvw, :])
        late[pl.ds(2 * s + 1, 1), 0:hw] = row_sums(back[:, hw : 2 * hw])
        advance("h", it)
        return carry

    lax.fori_loop(0, parts, pair_half, 0)

    ng_copy = rcopy(ngs, ngr, ng_sem.at[0], ng_sem.at[1], (d, tp))
    pair_grad = acc0[...]
    lo_copy.wait()
    ngs[...] = pair_grad.astype(BF16)
    ng_copy.start()
    unit, _ = unit_of(xp[...].astype(F32))
    late[8:9, :] = jnp.sum(pair_grad * unit, axis=0, keepdims=True)
    late[9:10, :] = jnp.sum(pair_grad, axis=0, keepdims=True)

    stages = (dev_c, (dx, t), (dy, t))

    def vec(which, stage):
        buf, rx = (early, e_rx) if which == 0 else (late, l_rx)
        return rcopy(buf, rx.at[stage], sm_s.at[which, stage], sm_r.at[which, stage], stages[stage])

    def vec_far(which, k):
        rz = e_rz if which == 0 else l_rz
        return rcopy(
            rz.at[t], rz.at[t], sm_s.at[which, 2 + k], sm_r.at[which, 3 + t], (d, far(k))
        )

    def vec_next(which, stage):
        buf, rx = (early, e_rx) if which == 0 else (late, l_rx)
        vec(which, stage).wait_recv()
        vec(which, stage).wait_send()
        buf[...] = buf[...] + rx[stage]
        if stage < 2:
            vec(which, stage + 1).start()
        else:
            rz = e_rz if which == 0 else l_rz
            rz[t] = buf[...]
            for k in range(1, parts):
                vec_far(which, k).start()

    vec(0, 0).start()

    def own_half(it, carry):
        q = it - parts
        s, dqt, dkt, dvt = att_group(it, 0)
        dqt = (uu[s, 0:hw, 0:share].astype(F32) + dqt).astype(BF16)
        dd[0:hw, :] = dqt
        dd[hw : 2 * hw, :] = dkt
        dd[2 * hw : qkvw, :] = dvt
        back = dd[...].T
        acc1[...] += nn(back, aw[s, 0:qkvw, :])
        late[pl.ds(2 * s, 1), 0:hw] = row_sums(back[:, 0:hw])
        late[pl.ds(2 * s + 1, 1), 0:hw] = late[pl.ds(2 * s + 1, 1), 0:hw] + row_sums(
            back[:, 2 * hw : qkvw]
        )
        aw[s, 0:hw, :] = nn(dqt, xn[0:share, :]).astype(BF16)
        aw[s, hw:qkvw, :] = (
            nn(dd[hw:qkvw, :], xn[0:share, :]) + nn(uu[s, hw:qkvw, 0:share], xn[share:keys, :])
        ).astype(BF16)
        for a in range(2):
            ra(0, q, a).start()
        advance("w", q)

        for stage in range(3):

            @pl.when(q == stage)
            def _():
                vec_next(0, stage)

        return carry

    lax.fori_loop(parts, 2 * parts, own_half, 0)

    own_grad = acc1[...]
    unit, scale_inv = unit_of(x_ref[...].astype(F32))
    late[8:9, :] = late[8:9, :] + jnp.sum(own_grad * unit, axis=0, keepdims=True)
    late[9:10, :] = late[9:10, :] + jnp.sum(own_grad, axis=0, keepdims=True)
    vec(1, 0).start()
    done = uu.at[0]
    xg_copy = pltpu.make_async_copy(mid, xg_ref, loc_sem.at[nblk])

    def aa(stage, a):
        _, _, first, second = route((t + a) % 2)
        view = done.at[a_rows(stage, t, a), a_lanes(a)]
        dev = (first, second, dev_c)[stage]
        return rcopy(view, view, aa_s.at[stage, a], aa_r.at[stage, a], dev)

    def att_final():
        for a in range(2):
            mine = a_rows(0, t, a)
            low = CUTS[a][0]
            high = low + CUTS[a][1]
            total = aw[t, mine, low:high].astype(F32)
            for q in range(parts - 1):
                view = rz_a.at[q, :, a_lanes(a)]
                rcopy(view, view, ra_s.at[3, a, q], ra_r.at[3, a, q], (d, t)).wait_recv()
                total = total + rz_a[q, :, low:high].astype(F32)
            done[mine, low:high] = total.astype(BF16)
            aa(0, a).start()

    def att_round(stage):
        for a in range(2):
            aa(stage - 1, a).wait_recv()
            aa(stage, a).start()

    def rows_final():
        ng_copy.wait_recv()
        grad = own_grad + ngr[...].astype(F32)
        mid[...] = mid[...] + norm_back(grad, unit, scale_inv, gain1)
        xg_copy.start()

    vec_stage = 0
    for name, low, high in TAIL:
        if name == "v":
            vec_next(1, vec_stage)
            vec_stage += 1
        elif name == "aa0":
            att_final()
        elif name == "aa1":
            att_round(1)
        elif name == "aa2":
            att_round(2)
        elif name == "ng":
            rows_final()
        else:
            repeat(name, low, high)

    for j in range(nblk):
        af(2, j).wait_recv()
        f_out(j, 0).start()
        if j >= 2:
            f_out(j - 2, 1).wait()
        ol[(j % 2) * BLK : (j % 2 + 1) * BLK, :] = fg[t * nblk + j, 1].T
        f_out(j, 1).start()

    for which in range(2):
        rz = e_rz if which == 0 else l_rz
        for k in range(1, parts):
            s = far(k)
            rcopy(
                rz.at[s], rz.at[s], sm_s.at[which, 3], sm_r.at[which, 3 + s], (d, t)
            ).wait_recv()
    early[...] = ((e_rz[0] + e_rz[1]) + e_rz[2]) + e_rz[3]
    late[...] = ((l_rz[0] + l_rz[1]) + l_rz[2]) + l_rz[3]
    osm_ref[0:4, :] = early[0:4, :]
    osm_ref[4:6, :] = late[8:10, :]
    osm_ref[8:9, :] = late[pl.ds(2 * t, 1), :]
    osm_ref[9:10, :] = late[pl.ds(2 * t + 1, 1), :]
    for j in range(nblk):
        osm_ref[16 + j : 17 + j, :] = early[pl.ds(4 + t * nblk + j, 1), :]

    for k in range(1, parts):
        zb(k, 0).wait_send()
        zb(k, 1).wait_send()
        for which in range(2):
            vec_far(which, k).wait_send()
    x_copy.wait_send()
    ng_copy.wait_send()

    def drain_far(m, carry):
        rf(3, m + nblk).wait_send()
        return carry

    lax.fori_loop(0, n_far, drain_far, 0)

    def drain_all(r, carry):
        for stage in range(3):
            rf(stage, r).wait_send()
        return carry

    lax.fori_loop(0, n_all, drain_all, 0)

    def drain_own(j, carry):
        for stage in range(3):
            af(stage, j).wait_send()
        return carry

    lax.fori_loop(0, nblk, drain_own, 0)
    for j in range(nblk):
        f_out(j, 0).wait()
    for j in range(nblk - 2, nblk):
        f_out(j, 1).wait()

    for q in range(parts):
        for a in range(2):
            for stage in range(3):
                ra(stage, q, a).wait_send()
            if q < parts - 1:
                ra(3, q, a).wait_send()
    for a in range(2):
        aa(2, a).wait_recv()
    oa_copy = pltpu.make_async_copy(done, oa_ref, loc_sem.at[nblk + 1])
    oa_copy.start()
    oa_copy.wait()
    xg_copy.wait()
    for stage in range(3):
        for a in range(2):
            aa(stage, a).wait_send()


def finish(
    lo,
    xg,
    up,
    dn,
    at,
    sm,
    lo_out,
    xg_out,
    up_out,
    dn_out,
    qkv_out,
    out_out,
    g2_out,
    s2_out,
    bo_out,
    bd_out,
    g1_out,
    s1_out,
    qv_out,
    bup_out,
    lo_b,
    xg_b,
    up_b,
    dn_b,
    at_b,
    up_f,
    dn_f,
    at_f,
    in_sem,
    out_sem,
):
    hw = out_out.shape[0]
    qkvw = qkv_out.shape[0]
    ins = [
        pltpu.make_async_copy(src, dst, in_sem.at[i])
        for i, (src, dst) in enumerate(((up, up_b), (dn, dn_b), (at, at_b), (xg, xg_b), (lo, lo_b)))
    ]
    for cp in ins:
        cp.start()
    outs = []

    def send(src, dst):
        outs.append(pltpu.make_async_copy(src, dst, out_sem.at[len(outs)]))
        outs[-1].start()

    for i, ref in enumerate((g2_out, s2_out, bo_out, bd_out, g1_out, s1_out)):
        ref[...] = sm[i]
    qv_out[...] = sm[8:10, 0:hw]
    for j in range(bup_out.shape[0] // BLK):
        bup_out[j * BLK : (j + 1) * BLK] = sm[16 + j, 0:BLK]
    ins[0].wait()
    up_f[...] = up_b[...].astype(F32)
    send(up_f, up_out)
    ins[1].wait()
    dn_f[...] = dn_b[...].astype(F32)
    send(dn_f, dn_out)
    ins[2].wait()
    at_f[...] = at_b[...].astype(F32)
    send(at_f.at[pl.ds(0, qkvw), :], qkv_out)
    send(at_f.at[pl.ds(qkvw, hw), :], out_out)
    ins[3].wait()
    send(xg_b, xg_out)
    ins[4].wait()
    send(lo_b, lo_out)
    for cp in outs:
        cp.wait()


def local(
    x_in,
    cotangent,
    lengths,
    bucket_ids,
    bucket_weights,
    ln1_gain,
    ln1_bias,
    w_qkv,
    qv_bias,
    w_out,
    b_out,
    ln2_gain,
    ln2_bias,
    w_up,
    b_up,
    w_down,
    b_down,
):
    share, width = x_in.shape
    hw = w_qkv.shape[2]
    heads = hw // HD
    parts = 4
    fw = w_up.shape[1]
    nblk = fw // BLK
    piece = width // GROUP
    keys = 2 * share
    n_all = parts * nblk
    n_far = n_all - nblk
    vm = pl.BlockSpec(memory_space=pltpu.VMEM)
    sm = pl.BlockSpec(memory_space=pltpu.SMEM)
    hbm = pl.BlockSpec(memory_space=pl.ANY)
    dma = pltpu.SemaphoreType.DMA
    scratch = [
        pltpu.VMEM((n_all + nblk, 2, width, BLK), BF16),
        pltpu.VMEM((parts, width, 4 * hw), BF16),
        pltpu.VMEM((SLOTS_C, 2, 4 * piece, BLK), BF16),
        pltpu.VMEM((n_all, 2, 2 * piece, BLK), BF16),
        pltpu.VMEM((n_all, 2, piece, BLK), BF16),
        pltpu.VMEM((n_far, 2, piece, BLK), BF16),
        pltpu.VMEM((parts, 4 * piece, 4 * hw), BF16),
        pltpu.VMEM((parts, 2 * piece, 4 * hw), BF16),
        pltpu.VMEM((parts, piece, 4 * hw), BF16),
        pltpu.VMEM((parts - 1, piece, 4 * hw), BF16),
        pltpu.VMEM((keys, width), BF16),
        pltpu.VMEM((share, width), BF16),
        pltpu.VMEM((parts, share, 256), BF16),
        pltpu.VMEM((parts, keys, 256), BF16),
        pltpu.VMEM((parts, keys, 256), BF16),
        pltpu.VMEM((parts, share, 256), BF16),
        pltpu.VMEM((parts, share, 256), BF16),
        pltpu.VMEM((parts, share, 128), F32),
        pltpu.VMEM((3 * hw, share), BF16),
        pltpu.VMEM((2, heads, share, share), BF16),
        pltpu.VMEM((share, width), F32),
        pltpu.VMEM((share, width), F32),
        pltpu.VMEM((share, width), F32),
        pltpu.VMEM((parts, width, width), BF16),
        pltpu.VMEM((share, width), BF16),
        pltpu.VMEM((width, share), BF16),
        pltpu.VMEM((share, width), BF16),
        pltpu.VMEM((share, width), BF16),
        pltpu.VMEM((parts, 1, fw), F32),
        pltpu.VMEM((parts, 2, hw), F32),
        pltpu.VMEM((24, width), F32),
        pltpu.VMEM((16, width), F32),
        pltpu.VMEM((3, 24, width), F32),
        pltpu.VMEM((parts, 24, width), F32),
        pltpu.VMEM((3, 16, width), F32),
        pltpu.VMEM((parts, 16, width), F32),
        dma((2 * nblk + 5,)),
        dma((2, heads)),
        dma((2, 3)),
        dma((2, parts)),
        dma((2,)),
        dma((6,)),
        dma((2, parts)),
        dma((3, 2, parts)),
        dma((3, 2, parts)),
        dma((n_far,)),
        dma((n_all,)),
        dma((3, n_all)),
        dma((3, n_all)),
        dma((n_all,)),
        dma((n_all,)),
        dma((n_all,)),
        dma((n_all,)),
        dma((n_all,)),
        dma((n_all,)),
        dma((n_far,)),
        dma((n_far,)),
        dma((3, nblk)),
        dma((3, nblk)),
        dma((4, 2, parts)),
        dma((4, 2, parts)),
        dma((3, 2)),
        dma((3, 2)),
        dma((2, 7)),
        dma((2, 7)),
        dma((2,)),
        pltpu.SemaphoreType.REGULAR,
    ]
    layer_out, x_grad, up, down, att, small, _ = pl.pallas_call(
        kernel,
        out_shape=[
            jax.ShapeDtypeStruct((share, width), BF16),
            jax.ShapeDtypeStruct((share, width), F32),
            jax.ShapeDtypeStruct((width, fw), BF16),
            jax.ShapeDtypeStruct((fw, width), BF16),
            jax.ShapeDtypeStruct((width, width), BF16),
            jax.ShapeDtypeStruct((24, width), F32),
            jax.ShapeDtypeStruct((parts * heads, 2, share, share), BF16),
        ],
        in_specs=[vm, hbm, sm, sm, sm, vm, vm, hbm, vm, hbm, vm, vm, vm, hbm, vm, hbm, vm],
        out_specs=[hbm, hbm, hbm, hbm, hbm, vm, hbm],
        scratch_shapes=scratch,
        compiler_params=pltpu.CompilerParams(
            collective_id=0, has_side_effects=True, vmem_limit_bytes=67043328
        ),
    )(
        x_in,
        cotangent,
        lengths,
        bucket_ids,
        bucket_weights,
        ln1_gain,
        ln1_bias,
        w_qkv.transpose(0, 2, 1),
        qv_bias,
        w_out,
        b_out,
        ln2_gain,
        ln2_bias,
        w_up,
        b_up,
        w_down,
        b_down,
    )
    dp = lax.axis_size("dp")
    if dp > GROUP:
        groups = [[g + GROUP * i for i in range(dp // GROUP)] for g in range(GROUP)]
        sums = lax.psum(
            tuple(g.astype(F32) for g in (up, down, att, small)), "dp", axis_index_groups=groups
        )
        up, down, att = (g.astype(BF16) for g in sums[:3])
        small = sums[3]
    flat = jax.ShapeDtypeStruct((width,), F32)
    outs = pl.pallas_call(
        finish,
        out_shape=[
            jax.ShapeDtypeStruct((share, width), BF16),
            jax.ShapeDtypeStruct((share, width), F32),
            jax.ShapeDtypeStruct((width, fw), F32),
            jax.ShapeDtypeStruct((fw, width), F32),
            jax.ShapeDtypeStruct((3 * hw, width), F32),
            jax.ShapeDtypeStruct((hw, width), F32),
            flat,
            flat,
            flat,
            flat,
            flat,
            flat,
            jax.ShapeDtypeStruct((2, hw), F32),
            jax.ShapeDtypeStruct((fw,), F32),
        ],
        in_specs=[hbm] * 5 + [vm],
        out_specs=[hbm] * 6 + [vm] * 8,
        scratch_shapes=[
            pltpu.VMEM((share, width), BF16),
            pltpu.VMEM((share, width), F32),
            pltpu.VMEM((width, fw), BF16),
            pltpu.VMEM((fw, width), BF16),
            pltpu.VMEM((width, width), BF16),
            pltpu.VMEM((width, fw), F32),
            pltpu.VMEM((fw, width), F32),
            pltpu.VMEM((width, width), F32),
            dma((5,)),
            dma((7,)),
        ],
    )(layer_out, x_grad, up, down, att, small)
    layer_out, x_grad, g_up, g_down, g_qkv, g_out, g2, s2, bo, bd, g1, s1, g_qv, g_bup = outs
    return (
        layer_out,
        x_grad,
        g1,
        s1,
        g_qkv.reshape(3, hw, width).transpose(0, 2, 1),
        g_qv,
        g_out,
        bo,
        g2,
        s2,
        g_up,
        g_bup,
        g_down,
        bd,
    )


def solution(mesh):
    return jax.shard_map(
        local,
        mesh=mesh,
        in_specs=(
            P(("dp", "tensor"), None),
            P(("dp", "tensor"), None),
            P("dp", None),
            P("dp"),
            P(),
            P(),
            P(),
            P(None, None, "tensor"),
            P(None, "tensor"),
            P("tensor", None),
            P(),
            P(),
            P(),
            P(None, "tensor"),
            P("tensor"),
            P("tensor", None),
            P(),
        ),
        out_specs=(
            P(("dp", "tensor"), None),
            P(("dp", "tensor"), None),
            P(),
            P(),
            P(None, None, "tensor"),
            P(None, "tensor"),
            P("tensor", None),
            P(),
            P(),
            P(),
            P(None, "tensor"),
            P("tensor"),
            P("tensor", None),
            P(),
        ),
        check_vma=False,
    )
```

```python
import functools
import math

import jax
import jax.numpy as jnp
from jax import lax
from jax.experimental import pallas as pl
from jax.experimental.pallas import tpu as pltpu
from jax.sharding import PartitionSpec as P

HD = 32
BUCKET = 256
EPSILON = 1e-05
GROUP = 8
BLK = 256
BIG = 1e30
F32 = jnp.float32
BF16 = jnp.bfloat16
MESH = pl.DeviceIdType.MESH
RSQRT2 = 1.0 / math.sqrt(2.0)
RSQRT2PI = 1.0 / math.sqrt(2.0 * math.pi)
SLOTS_C = 2
X_PLACE = 0
WIDE_FROM = 15
NG_PLACE = 2
CUTS = ((0, 256), (256, 384))
CHUNKS = 4
PLAN = {
    "p0": (
        ("a0", (0, 1)),
        ("a1", (0, 1)),
    ),
    "p1": (
        ("a0", (1, 2)),
    ),
    "p2": (
        ("a0", (2, 3)),
        ("a1", (1, 3)),
        ("a2", (0, 3)),
    ),
    "pj": (
    ),
    "o": (
    ),
    "q": (
        ("g0", (0, 4, 12, 12, 15)),
        ("g1", (0, 0, 0, 5, 8)),
    ),
    "mid": (
        ("g1", (8, 10)),
        ("g2", (0, 3)),
    ),
    "r": (
        ("g1", (10, 13, 15, 15, 15, 15, 15, 15, 15, 15, 15, 15, 15, 15, 15, 15, 15, 15, 15, 15, 15)),
        ("g2", (3, 3, 5, 5, 6, 9, 10, 13, 15, 15, 15, 15, 15, 15, 15, 15, 15, 15, 15, 15, 15)),
        ("rf", (0, 0, 0, 0, 0, 0, 0, 0, 0, 0, 0, 0, 0, 1, 1, 1, 1, 1, 2, 2, 3)),
        ("r1", (0, 0, 0, 0, 0, 0, 0, 0, 0, 0, 1, 2, 2, 2, 2, 3, 3, 5, 5, 6, 6)),
        ("r2", (0, 0, 0, 0, 0, 0, 0, 1, 2, 3, 4, 5, 6, 6, 8, 8, 9, 11, 12, 12, 12)),
    ),
    "ln": (
        ("rf", (3, 4)),
    ),
    "k": (
        ("rf", (4, 4, 4, 5, 5)),
        ("r1", (6, 10, 10, 10, 10)),
        ("r2", (12, 13, 14, 17, 17)),
    ),
    "h": (
        ("rf", (5, 5, 5, 9, 12)),
        ("r1", (10, 11, 12, 17, 18)),
        ("r2", (17, 18, 19, 19, 20)),
    ),
    "w": (
        ("rf", (12, 18, 19, 20, 20)),
        ("r1", (18, 20, 20, 20, 20)),
        ("b3", (0, 0, 0, 0, 1)),
        ("b2", (0, 0, 1, 1, 3)),
        ("b1", (0, 1, 1, 3, 4)),
        ("f0", (0, 3, 4, 5, 5)),
        ("f1", (0, 0, 2, 3, 5)),
    ),
}
TAIL = (
    ("b3", 1, 3),
    ("b2", 3, 4),
    ("v", 0, 0),
    ("v", 0, 0),
    ("b3", 3, 4),
    ("aa0", 0, 0),
    ("f2", 0, 5),
    ("v", 0, 0),
    ("aa1", 0, 0),
    ("ng", 0, 0),
    ("aa2", 0, 0),
)


def nn(a, b):
    return lax.dot_general(a, b, (((1,), (0,)), ((), ())), preferred_element_type=F32)


def nt(a, b):
    return lax.dot_general(a, b, (((1,), (1,)), ((), ())), preferred_element_type=F32)


def unit_of(values):
    centre = values - jnp.mean(values, axis=-1, keepdims=True)
    scale_inv = lax.rsqrt(jnp.mean(centre * centre, axis=-1, keepdims=True) + EPSILON)
    return centre * scale_inv, scale_inv


def norm_back(grad, unit, scale_inv, gain):
    scaled = grad * gain
    return scale_inv * (
        scaled
        - jnp.mean(scaled, axis=-1, keepdims=True)
        - unit * jnp.mean(scaled * unit, axis=-1, keepdims=True)
    )


def lanes(shape):
    return lax.broadcasted_iota(jnp.int32, shape, 1)


def kernel(
    x_ref,
    cot_ref,
    len_ref,
    bid_ref,
    bw_ref,
    g1_ref,
    s1_ref,
    wqkv_ref,
    qvb_ref,
    wout_ref,
    bout_ref,
    g2_ref,
    s2_ref,
    wup_ref,
    bup_ref,
    wdn_ref,
    bdn_ref,
    lo_ref,
    xg_ref,
    ou_ref,
    od_ref,
    oa_ref,
    osm_ref,
    ph_ref,
    fg,
    aw,
    rc_f,
    r2_f,
    r1_f,
    rz_f,
    rc_a,
    r2_a,
    r1_a,
    rz_a,
    xn,
    xp,
    qb,
    kb,
    vb,
    mx,
    dmx,
    stat,
    dd,
    pst,
    mid,
    acc0,
    acc1,
    uu,
    ol,
    olt,
    ngs,
    ngr,
    bupa,
    qvba,
    early,
    late,
    e_rx,
    e_rz,
    l_rx,
    l_rz,
    loc_sem,
    ps_sem,
    za_s,
    za_r,
    zx_sem,
    zb_s,
    zb_r,
    ga_s,
    ga_r,
    zf_s,
    zf_r,
    gf_s,
    gf_r,
    cf_s,
    cf_r,
    f2_s,
    f2_r,
    f1_s,
    f1_r,
    fz_s,
    fz_r,
    af_s,
    af_r,
    ra_s,
    ra_r,
    aa_s,
    aa_r,
    sm_s,
    sm_r,
    ng_sem,
    credit,
):
    share, width = x_ref.shape
    hw = wqkv_ref.shape[1]
    heads = hw // HD
    qkvw = 3 * hw
    parts = 4
    nblk = wup_ref.shape[1] // BLK
    piece = width // GROUP
    keys = 2 * share
    factor = HD ** (-0.5)
    q_scale = factor * math.log2(math.e)

    d = lax.axis_index("dp")
    t = lax.axis_index("tensor")
    c = d % 2
    bx = (d // 2) % 2
    by = (d // 4) % 2
    dev_c = (d + 1 - 2 * c, t)
    dx = d + 2 - 4 * bx
    dy = d + 4 - 8 * by
    t0 = t % 2
    t1 = t // 2
    tp = t + 1 - 2 * t0

    def quotient(n, step, limit):
        if isinstance(n, int):
            return n // step
        return sum(jnp.where(n >= i, 1, 0) for i in range(step, limit, step))

    def odd(n, limit):
        return n - 2 * quotient(n, 2, limit)

    def differ(a, b):
        return a + b - 2 * a * b

    def far_bits(k):
        high = quotient(k, 2, parts)
        low = differ(t0, k - 2 * high)
        return low + 2 * differ(t1, high), low

    def far(k):
        return far_bits(k)[0]

    def route(par):
        low = bx + par * (by - bx)
        high = by + par * (bx - by)
        first = (dx + par * (dy - dx), t)
        second = (dy + par * (dx - dy), t)
        return low, high, first, second

    def rcopy(src, dst, ssem, rsem, dev):
        return pltpu.make_async_remote_copy(
            src_ref=src, dst_ref=dst, send_sem=ssem, recv_sem=rsem, device_id=dev, device_id_type=MESH
        )

    def arrived(view, sem):
        rcopy(view, view, sem, sem, (d, t)).wait_recv()

    def left(view, sem):
        rcopy(view, view, sem, sem, (d, t)).wait_send()

    def rows(start, size):
        return pl.ds(pl.multiple_of(start, 16), size)

    def up_load(j):
        return pltpu.make_async_copy(
            wup_ref.at[:, pl.ds(j * BLK, BLK)], fg.at[t * nblk + j, 0], loc_sem.at[j]
        )

    def dn_load(j):
        return pltpu.make_async_copy(
            wdn_ref.at[pl.ds(j * BLK, BLK), :],
            uu.at[j // 2, pl.ds((j % 2) * BLK, BLK), :],
            loc_sem.at[nblk + j],
        )

    cot_load = pltpu.make_async_copy(cot_ref, ol, loc_sem.at[2 * nblk])

    a_loads = [
        pltpu.make_async_copy(
            wqkv_ref.at[i], aw.at[t, pl.ds(i * hw, hw), :], loc_sem.at[2 * nblk + 1 + i]
        )
        for i in range(3)
    ]
    a_loads.append(
        pltpu.make_async_copy(
            wout_ref, aw.at[t, pl.ds(qkvw, hw), :], loc_sem.at[2 * nblk + 4]
        )
    )
    for cp in a_loads:
        cp.start()
    for j in range(nblk):
        dn_load(j).start()
        up_load(j).start()
    cot_load.start()
    bupa[t] = bup_ref[...][None, :]
    qvba[t] = qvb_ref[...]

    barrier = pltpu.get_barrier_semaphore()
    for dev in (dev_c, (dx, t), (dy, t), (d, far(1)), (d, far(2)), (d, far(3))):
        pl.semaphore_signal(barrier, inc=1, device_id=dev, device_id_type=MESH)
    pl.semaphore_wait(barrier, 6)

    def a_rows(stage, parity, a):
        low, high, _, _ = route(parity if a == 0 else 1 - parity)
        if stage == 0:
            return rows((c * 4 + high * 2 + low) * piece, piece)
        if stage == 1:
            return rows((c * 4 + high * 2) * piece, 2 * piece)
        return rows(c * 4 * piece, 4 * piece)

    def a_lanes(a):
        return pl.ds(CUTS[a][0], CUTS[a][1])

    def a_any(stage, a):
        return aw.at[0, 0 : (piece, 2 * piece, 4 * piece)[stage], a_lanes(a)]

    def za(k, a):
        view = aw.at[t, a_rows(0, t0, a), a_lanes(a)]
        return rcopy(view, view, za_s.at[a, k - 1], za_r.at[a, t], (d, far(k)))

    def zb(k, which):
        dst = (bupa if which == 0 else qvba).at[t]
        return rcopy(dst, dst, zb_s.at[2 * (k - 1) + which], zb_r.at[which, t], (d, far(k)))

    def zb_wait(s, which):
        dst = (bupa if which == 0 else qvba).at[s]
        rcopy(dst, dst, zb_s.at[0], zb_r.at[which, s], (d, t)).wait_recv()

    x_copy = rcopy(x_ref, xp, zx_sem.at[0], zx_sem.at[1], (d, tp))

    for cp in a_loads:
        cp.wait()
    for k in range(1, parts):
        for a in range(2):
            za(k, a).start()
        zb(k, 1).start()
    for k in range(1, parts):
        zb(k, 0).start()

    def ga(stage, s, parity, a):
        _, _, first, second = route(parity if a == 0 else 1 - parity)
        view = aw.at[s, a_rows(stage, parity, a), a_lanes(a)]
        dev = (first, second, dev_c)[stage]
        return rcopy(view, view, ga_s.at[stage, a, s], ga_r.at[stage, a, s], dev)

    def step_a(stage, i):
        s, parity = far_bits(i + 1)
        for a in range(2):
            if stage == 0:
                arrived(a_any(0, a), za_r.at[a, s])
            else:
                arrived(a_any(stage - 1, a), ga_r.at[stage - 1, a, s])
            ga(stage, s, parity, a).start()

    n_far = (parts - 1) * nblk

    def far_block(m):
        j = quotient(m, parts - 1, n_far)
        s, parity = far_bits(1 + m - (parts - 1) * j)
        return s, j, s * nblk + j, differ(parity, odd(j, nblk))

    def own_parity(j):
        return differ(t0, odd(j, nblk))

    def gf(stage, m):
        _, _, b, par = far_block(m)
        low, high, first, second = route(par)
        if stage == 0:
            view, dev = fg.at[b, :, rows((c * 4 + high * 2 + low) * piece, piece), :], first
        elif stage == 1:
            view, dev = fg.at[b, :, rows((c * 4 + high * 2) * piece, 2 * piece), :], second
        else:
            view, dev = fg.at[b, :, rows(c * 4 * piece, 4 * piece), :], dev_c
        return rcopy(view, view, gf_s.at[stage, b], gf_r.at[stage, b], dev)

    def f_any(stage):
        return fg.at[0, :, 0 : (piece, 2 * piece, 4 * piece)[stage], :]

    def step_g(stage, m):
        b = far_block(m)[2]
        if WIDE_FROM >= n_far:
            if stage == 0:
                arrived(f_any(0), zf_r.at[b])
            else:
                arrived(f_any(stage - 1), gf_r.at[stage - 1, b])
            gf(stage, m).start()
            return
        if stage == 0:

            @pl.when(m < WIDE_FROM)
            def _():
                arrived(f_any(0), zf_r.at[b])
                gf(0, m).start()

            return
        if stage == 1:

            @pl.when(m < WIDE_FROM)
            def _():
                arrived(f_any(0), gf_r.at[0, b])

            @pl.when(m >= WIDE_FROM)
            def _():
                arrived(f_any(1), zf_r.at[b])

        else:
            arrived(f_any(1), gf_r.at[1, b])
        gf(stage, m).start()

    n_all = parts * nblk

    def block(r):
        own = jnp.where(r < nblk, 1, 0)
        m = r - nblk
        turn_j = quotient(m, parts - 1, n_far)
        k = (1 - own) * (1 + m - (parts - 1) * turn_j)
        j = own * r + (1 - own) * turn_j
        s, parity = far_bits(k)
        home = s * nblk + j
        return k, j, s, home, home + own * (n_all + j - home), differ(parity, odd(j, nblk))

    def rf(stage, r, slot=None):
        k, j, s, _, g, par = block(r)
        low, high, first, second = route(par)
        if stage == 0:
            return rcopy(
                fg.at[g, :, rows((1 - c) * 4 * piece, 4 * piece), :],
                rc_f.at[slot],
                cf_s.at[r],
                cf_r.at[r],
                dev_c,
            )
        if stage == 1:
            return rcopy(
                fg.at[g, :, rows((c * 4 + (1 - high) * 2) * piece, 2 * piece), :],
                r2_f.at[r],
                f2_s.at[r],
                f2_r.at[r],
                second,
            )
        if stage == 2:
            return rcopy(
                fg.at[g, :, rows((c * 4 + high * 2 + 1 - low) * piece, piece), :],
                r1_f.at[r],
                f1_s.at[r],
                f1_r.at[r],
                first,
            )
        z = jnp.maximum((k - 1) * nblk + j, 0)
        return rcopy(
            fg.at[g, :, rows((c * 4 + high * 2 + low) * piece, piece), :],
            rz_f.at[z],
            fz_s.at[z],
            fz_r.at[z],
            (d, s),
        )

    def add_rows(ref, got):
        ref[...] = (ref[...].astype(F32) + got[...].astype(F32)).astype(BF16)

    def rf_core(r, slot):
        g = block(r)[4]
        arrived(rc_f.at[slot], cf_r.at[r])
        add_rows(fg.at[g, :, rows(c * 4 * piece, 4 * piece), :], rc_f.at[slot])

        @pl.when(r < n_all - SLOTS_C)
        def _():
            pl.semaphore_signal(credit, inc=1, device_id=dev_c, device_id_type=MESH)

    def turn(i):
        return i + nblk - n_all * jnp.where(i >= n_all - nblk, 1, 0)

    def rf_first(r):
        _, _, _, _, g, par = block(r)
        _, high, _, _ = route(par)
        arrived(r2_f.at[r], f2_r.at[r])
        add_rows(fg.at[g, :, rows((c * 4 + high * 2) * piece, 2 * piece), :], r2_f.at[r])
        rf(2, r).start()

    def rf_far(r):
        _, _, _, _, g, par = block(r)
        low, high, _, _ = route(par)
        arrived(r1_f.at[r], f1_r.at[r])
        add_rows(fg.at[g, :, rows((c * 4 + high * 2 + low) * piece, piece), :], r1_f.at[r])

        @pl.when(r >= nblk)
        def _():
            rf(3, r).start()

    def af(stage, j):
        low, high, first, second = route(own_parity(j))
        b = t * nblk + j
        if stage == 0:
            view, dev = fg.at[b, :, rows((c * 4 + high * 2 + low) * piece, piece), :], first
        elif stage == 1:
            view, dev = fg.at[b, :, rows((c * 4 + high * 2) * piece, 2 * piece), :], second
        else:
            view, dev = fg.at[b, :, rows(c * 4 * piece, 4 * piece), :], dev_c
        return rcopy(view, view, af_s.at[stage, j], af_r.at[stage, j], dev)

    def f_final(j):
        low, high, _, _ = route(own_parity(j))
        mine = rows((c * 4 + high * 2 + low) * piece, piece)
        total = fg[n_all + j, :, mine, :].astype(F32)
        for k in range(1, parts):
            z = (k - 1) * nblk + j
            arrived(rz_f.at[z], fz_r.at[z])
            total = total + rz_f[z].astype(F32)
        fg[t * nblk + j, :, mine, :] = total.astype(BF16)
        af(0, j).start()

    def f_out(j, which):
        if which == 0:
            return pltpu.make_async_copy(
                fg.at[t * nblk + j, 0], ou_ref.at[:, pl.ds(j * BLK, BLK)], loc_sem.at[j]
            )
        return pltpu.make_async_copy(
            ol.at[pl.ds((j % 2) * BLK, BLK), :],
            od_ref.at[pl.ds(j * BLK, BLK), :],
            loc_sem.at[nblk + 2 + j % 2],
        )

    def f_second(j):
        arrived(f_any(0), af_r.at[0, j])
        af(1, j).start()

    def f_third(j):
        arrived(f_any(1), af_r.at[1, j])
        af(2, j).start()

    def group_bits(it):
        n = it + 1
        return far_bits(n - parts * quotient(n, parts, 2 * parts + 1))

    def group_of(it):
        return group_bits(it)[0]

    def ra(stage, q, a):
        s, parity = group_bits(q)
        low, high, first, second = route(parity if a == 0 else 1 - parity)
        if stage == 0:
            where, buf, dev = rows((1 - c) * 4 * piece, 4 * piece), rc_a, dev_c
        elif stage == 1:
            where, buf, dev = rows((c * 4 + (1 - high) * 2) * piece, 2 * piece), r2_a, second
        elif stage == 2:
            where, buf, dev = rows((c * 4 + high * 2 + 1 - low) * piece, piece), r1_a, first
        else:
            where, buf, dev = rows((c * 4 + high * 2 + low) * piece, piece), rz_a, (d, s)
            q = jnp.minimum(q, parts - 2)
        return rcopy(
            aw.at[s, where, a_lanes(a)],
            buf.at[q, :, a_lanes(a)],
            ra_s.at[stage, a, q],
            ra_r.at[stage, a, q],
            dev,
        )

    def step_b(stage, q):
        s, parity = group_bits(q)
        buf = (rc_a, r2_a, r1_a)[stage - 1]
        for a in range(2):
            view = buf.at[q, :, a_lanes(a)]
            arrived(view, ra_r.at[stage - 1, a, q])
            add_rows(aw.at[s, a_rows(3 - stage, parity, a), a_lanes(a)], view)
            if stage < 3:
                ra(stage, q, a).start()
            else:

                @pl.when(q < parts - 1)
                def _():
                    ra(3, q, a).start()

    steps = {
        "a0": lambda i: step_a(0, i),
        "a1": lambda i: step_a(1, i),
        "a2": lambda i: step_a(2, i),
        "g0": lambda i: step_g(0, i),
        "g1": lambda i: step_g(1, i),
        "g2": lambda i: step_g(2, i),
        "r2": lambda i: rf(1, turn(i)).start(),
        "r1": lambda i: rf_first(turn(i)),
        "rf": lambda i: rf_far(turn(i)),
        "b1": lambda i: step_b(1, i),
        "b2": lambda i: step_b(2, i),
        "b3": lambda i: step_b(3, i),
        "f0": lambda i: f_final(i),
        "f1": lambda i: f_second(i),
        "f2": lambda i: f_third(i),
    }

    def repeat(name, low, high):
        def one(i, carry):
            steps[name](i)
            return carry

        lax.fori_loop(low, high, one, 0)

    def advance(place, idx=None, reached=None):
        after = []
        for n, (name, counts) in enumerate(PLAN[place]):
            low = counts[0] if reached is None else reached[n]
            high = low
            if idx is None:
                high = counts[-1]
            else:
                for i in range(len(counts) - 1):
                    more = counts[i + 1] - counts[i]
                    if more:
                        high = high + jnp.where(idx == i, more, 0)
            repeat(name, low, high)
            after.append(high)
        return tuple(after)

    def begin(place):
        return tuple(jnp.int32(counts[0]) for _, counts in PLAN[place])

    gain1 = g1_ref[...][None, :]
    shift1 = s1_ref[...][None, :]
    unit, _ = unit_of(x_ref[...].astype(F32))
    xn[0:share, :] = (unit * gain1 + shift1).astype(BF16)
    advance("p0")

    def zf(k, j):
        low, high, _, _ = route(own_parity(j))
        where = rows((c * 4 + high * 2 + low) * piece, piece)
        if j * (parts - 1) + k - 1 >= WIDE_FROM:
            where = rows((c * 4 + high * 2) * piece, 2 * piece)
        view = fg.at[t * nblk + j, :, where, :]
        return rcopy(
            view, view, zf_s.at[(k - 1) * nblk + j], zf_r.at[t * nblk + j], (d, far(k))
        )

    for j in range(nblk):
        up_load(j).wait()
        dn_load(j).wait()
        fg[t * nblk + j, 1] = uu[j // 2, (j % 2) * BLK : (j % 2 + 1) * BLK, :].T
    for m in range((parts - 1) * nblk):
        if m == X_PLACE:
            x_copy.start()
        zf(1 + m % (parts - 1), m // (parts - 1)).start()

    advance("p1")

    bucket = bid_ref[0]
    span = jnp.where(bucket == 0, BUCKET, jnp.where(bucket == 1, 2 * BUCKET, 4 * BUCKET))
    weight = jnp.where(bucket == 0, bw_ref[0], jnp.where(bucket == 1, bw_ref[1], bw_ref[2]))

    def slot_info(base, shape):
        place = base + lax.broadcasted_iota(jnp.int32, shape, 0)
        item = jnp.zeros(shape, jnp.int32)
        for j in range(1, len_ref.shape[1]):
            item = item + jnp.where(place >= j * span, 1, 0)
        length = jnp.zeros(shape, jnp.int32)
        for j in range(len_ref.shape[1]):
            length = jnp.where(item == j, len_ref[0, j], length)
        return item, (place - item * span) < length

    wide = (share, 2 * 128)
    lane = lanes(wide)
    slots = len_ref.shape[1]
    in_aux = (lane >= hw) & (lane < hw + slots)
    one_aux = jnp.where(lane >= hw, 1.0, 0.0).astype(BF16)

    own_item, own_live = slot_info(t * share, wide)
    q_aux = jnp.where(in_aux & (own_item == lane - hw), 1.0, 0.0).astype(BF16)
    k_aux0 = jnp.where(in_aux & ~((own_item == lane - hw) & own_live), -BIG, 0.0).astype(BF16)
    pair_item, pair_live = slot_info(tp * share, wide)
    k_aux1 = jnp.where(in_aux & ~((pair_item == lane - hw) & pair_live), -BIG, 0.0).astype(BF16)
    for s in range(parts):
        qb[s] = q_aux
        kb[s, 0:share] = k_aux0
        kb[s, share:keys] = k_aux1
        vb[s, 0:share] = one_aux
        vb[s, share:keys] = one_aux
    _, live1 = slot_info(t * share, (share, 128))
    row_weight = jnp.where(live1, weight, 0.0)[:, 0:1]

    advance("p2")

    def project(s, half, own):
        base = half * share
        first = 0 if own else hw
        out = nt(xn[base : base + share, :], aw[s, first:qkvw, :])
        if own:
            qb[s, :, 0:hw] = ((out[:, 0:hw] + qvba[s, 0:1, :]) * q_scale).astype(BF16)
        at = hw - first
        kb[s, base : base + share, 0:hw] = out[:, at : at + hw].astype(BF16)
        vb[s, base : base + share, 0:hw] = (
            out[:, at + hw : at + 2 * hw] + qvba[s, 1:2, :]
        ).astype(BF16)

    lane_w = lanes((share, 2 * 128))
    lane_n = lanes((share, 128))

    def head_lanes(h):
        return (lane_w >= HD * h) & (lane_w < HD * (h + 1))

    def spread(values, at):
        out = jnp.zeros((share, 2 * 128), F32)
        for h in range(heads):
            out = jnp.where(head_lanes(h), values[:, at + h : at + h + 1], out)
        return out

    def p_out(s, h, half, buf):
        return pltpu.make_async_copy(
            pst.at[buf, h], ph_ref.at[s * heads + h, half], ps_sem.at[buf, h]
        )

    at0 = hw - 128
    at1 = at0 + 32
    at2 = at0 + 64

    def att_forward(k, half):
        s = far(k)
        base = half * share
        buf = odd(k, parts)
        if half == 1:
            for h in range(heads):
                p_out(s, h, half, buf).wait()
        else:

            @pl.when(k >= 2)
            def _():
                for h in range(heads):
                    p_out(s, h, half, buf).wait()

        qg = qb[s]
        kg = kb[s, base : base + share]
        vg = vb[s, base : base + share]
        out = jnp.zeros((share, 2 * 128), F32)
        tops = jnp.zeros((share, 128), F32)
        for h in range(heads):
            head = head_lanes(h)
            qm = jnp.where(head | (lane_w >= hw), qg, jnp.zeros_like(qg))
            scores = nt(qm, kg)
            top = jnp.max(scores, axis=1, keepdims=True)
            probs = jnp.exp2(scores - top).astype(BF16)
            pst[buf, h] = probs
            mixed = nn(probs, vg)
            out = jnp.where(head | (lane_w == hw + h), mixed, out)
            tops = jnp.where(lane_n == at0 + h, top, tops)
        for h in range(heads):
            p_out(s, h, half, buf).start()
        sums = jnp.where((lane_n >= at0) & (lane_n < at0 + heads), out[:, 128:256], 1.0)
        log_sum = tops + jnp.log2(sums)
        if half == 0:
            mx[s] = (out * spread(1.0 / sums, at0)).astype(BF16)
            stat[s] = jnp.where(lane_n < at1, tops, pltpu.roll(log_sum, 32, 1))
        else:
            before = stat[s]
            log_before = pltpu.roll(before, 96, 1)
            upper = jnp.maximum(log_sum, log_before)
            lower = jnp.minimum(log_sum, log_before)
            log_all = upper + jnp.log2(1.0 + jnp.exp2(lower - upper))
            part0 = jnp.exp2(log_before - log_all)
            part1 = jnp.exp2(log_sum - log_all) / sums
            mx[s] = (
                mx[s].astype(F32) * spread(part0, at0) + out * spread(part1, at0)
            ).astype(BF16)
            stat[s] = jnp.where(
                lane_n < at1,
                jnp.exp2(before - log_all),
                pltpu.roll(jnp.exp2(tops - log_all), 32, 1),
            )

    def own_keys(k, carry):
        s = far(k)

        @pl.when(k > 0)
        def _():
            zb_wait(s, 1)
            for a in range(2):
                arrived(a_any(2, a), ga_r.at[2, a, s])

        project(s, 0, True)

        @pl.when(k == 0)
        def _():
            advance("pj")

        att_forward(k, 0)
        return advance("o", k, carry)

    lax.fori_loop(0, parts, own_keys, begin("o"))

    x_copy.wait_recv()
    unit, _ = unit_of(xp[...].astype(F32))
    xn[share:keys, :] = (unit * gain1 + shift1).astype(BF16)

    def pair_keys(k, carry):
        project(far(k), 1, False)
        att_forward(k, 1)
        return advance("q", k, carry)

    lax.fori_loop(0, parts, pair_keys, begin("q"))
    for buf in range(2):
        for h in range(heads):
            p_out(0, h, 1, buf).wait()

    branch = jnp.zeros((share, width), F32)
    for s in range(parts):
        branch = branch + nn(mx[s, :, 0:hw], aw[s, qkvw : 4 * hw, :])
    middle = x_ref[...].astype(F32) + (branch + bout_ref[...][None, :])
    mid[...] = middle
    unit, _ = unit_of(middle)
    normed = (unit * g2_ref[...][None, :] + s2_ref[...][None, :]).astype(BF16)
    n2 = uu.at[0, 0:share, :]
    n2t = uu.at[1, :, 0:share]
    n2[...] = normed
    n2t[...] = normed.T
    cot_load.wait()
    low_grad = (ol[...].astype(F32) * row_weight).astype(BF16)
    early[...] = jnp.zeros_like(early)
    late[...] = jnp.zeros_like(late)
    early[3:4, :] = jnp.sum(low_grad.astype(F32), axis=0, keepdims=True)
    ol[...] = low_grad
    olt[...] = low_grad.T
    acc0[...] = jnp.zeros_like(acc0)
    acc1[...] = jnp.zeros_like(acc1)

    for k in range(1, parts):
        zb_wait(far(k), 0)
    advance("mid")

    def ffn(r, carry):
        k, j, s, home, g, _ = block(r)

        @pl.when(k > 0)
        def _():
            arrived(f_any(2), gf_r.at[2, home])

        wu = fg[home, 0]
        wd = fg[home, 1]
        hidden = nn(n2[...], wu) + bupa[s, :, pl.ds(pl.multiple_of(j * BLK, BLK), BLK)]
        cdf = 0.5 + 0.5 * lax.erf(hidden * RSQRT2)
        slope = cdf + hidden * (jnp.exp(-0.5 * hidden * hidden) * RSQRT2PI)
        active = (hidden * cdf).astype(BF16)
        act_grad = nn(ol[...], wd)
        hid_grad = (slope * act_grad).astype(BF16)
        acc0[...] += nt(active, wd)
        acc1[...] += nt(hid_grad, wu)
        early[pl.ds(4 + home, 1), 0:BLK] = jnp.sum(hid_grad.astype(F32), axis=0, keepdims=True)
        up_grad = nn(n2t[...], hid_grad).astype(BF16)
        dn_grad = nn(olt[...], active).astype(BF16)

        @pl.when(k > 0)
        def _():
            for stage in (1, 2):
                left(f_any(stage), gf_s.at[stage, home])

        @pl.when((k > 0) & (r - nblk < WIDE_FROM))
        def _():
            left(f_any(0), gf_s.at[0, home])

        fg[g, 0] = up_grad
        fg[g, 1] = dn_grad

        @pl.when(r == 3 * nblk - 1)
        def _():
            for m in range(n_far):
                zf(1 + m % (parts - 1), m // (parts - 1)).wait_send()

        @pl.when(r >= SLOTS_C)
        def _():
            pl.semaphore_wait(credit, 1)

        slot = odd(r, n_all)
        rf(0, r, slot).start()

        @pl.when(r > 0)
        def _():
            rf_core(r - 1, 1 - slot)

        return advance("r", r, carry)

    lax.fori_loop(0, n_all, ffn, begin("r"))
    rf_core(n_all - 1, (n_all - 1) % SLOTS_C)

    middle = mid[...]
    ngs[...] = (middle + (acc0[...] + bdn_ref[...][None, :])).astype(BF16)
    lo_copy = pltpu.make_async_copy(ngs, lo_ref, loc_sem.at[2 * nblk])
    lo_copy.start()
    unit, scale_inv = unit_of(middle)
    got = acc1[...]
    early[0:1, :] = jnp.sum(got * unit, axis=0, keepdims=True)
    early[1:2, :] = jnp.sum(got, axis=0, keepdims=True)
    middle_part = norm_back(got, unit, scale_inv, g2_ref[...][None, :])
    reload = pltpu.make_async_copy(cot_ref, ol, loc_sem.at[0])
    reload.start()
    reload.wait()
    out_grad = ol[...].astype(F32) * row_weight
    middle_grad = out_grad + middle_part
    mid[...] = middle_grad
    branch_low = middle_grad.astype(BF16)
    early[2:3, :] = jnp.sum(branch_low.astype(F32), axis=0, keepdims=True)
    ol[...] = branch_low

    for k in range(1, parts):
        for a in range(2):
            za(k, a).wait_send()
            for stage in range(3):
                left(a_any(stage, a), ga_s.at[stage, a, far(k)])
    advance("ln")

    head_row = lax.broadcasted_iota(jnp.int32, (hw, 128), 0)
    head_col = (lax.broadcasted_iota(jnp.int32, (hw, 128), 1) - at2) * HD
    pick = jnp.where((head_row >= head_col) & (head_row < head_col + HD), 1.0, 0.0).astype(BF16)

    def out_back(k, carry):
        s = far(k)
        mixed = mx[s, :, 0:hw]
        mixed_grad = nt(ol[...], aw[s, qkvw : 4 * hw, :]).astype(BF16)
        dmx[s, :, 0:hw] = mixed_grad
        prod = mixed_grad.astype(F32) * mixed.astype(F32)
        coarse = prod.astype(BF16)
        fine = (prod - coarse.astype(F32)).astype(BF16)
        delta = nn(coarse, pick) + nn(fine, pick)
        stat[s] = jnp.where((lane_n >= at2) & (lane_n < at2 + heads), delta, stat[s])
        aw[s, qkvw : 4 * hw, :] = nn(mixed.T, ol[...]).astype(BF16)
        return advance("k", k, carry)

    lax.fori_loop(0, parts, out_back, begin("k"))

    def p_in(s, h, half, buf):
        return pltpu.make_async_copy(
            ph_ref.at[s * heads + h, half], pst.at[buf, h], ps_sem.at[buf, h]
        )

    def fetch(it):
        for h in range(heads):
            p_in(group_of(it), h, 1 - quotient(it, parts, 2 * parts), odd(it, 2 * parts)).start()

    def att_group(it, half):
        s = group_of(it)
        base = half * share
        buf = odd(it, 2 * parts)

        @pl.when(it + 1 < 2 * parts)
        def _():
            fetch(it + 1)

        for h in range(heads):
            p_in(s, h, half, buf).wait()
        known = stat[s]
        wanted = known if half == 0 else pltpu.roll(known, 96, 1)
        delta = -(pltpu.roll(known, 64, 1) * wanted)
        coarse = delta.astype(BF16).astype(F32)
        aux = jnp.where((lane_n >= at0) & (lane_n < at0 + heads), coarse, 0.0)
        aux = jnp.where(
            (lane_n >= at0 + 8) & (lane_n < at0 + 8 + heads), pltpu.roll(delta - coarse, 8, 1), aux
        )
        scaled = dmx[s].astype(F32) * spread(wanted, at0)
        dg = jnp.concatenate(
            [scaled[:, 0:128], jnp.where(lane_n < at0, scaled[:, 128:256], aux)], axis=1
        ).astype(BF16)
        qg = qb[s]
        kg = kb[s, base : base + share]
        vg = vb[s, base : base + share]
        qt = qg[:, 0:hw].T
        dt = dg[:, 0:hw].T
        dq = jnp.zeros((share, 2 * 128), F32)
        dks = []
        dvs = []
        for h in range(heads):
            head = head_lanes(h)
            aux_h = (lane_w == hw + h) | (lane_w == hw + 8 + h)
            dm = jnp.where(head | aux_h, dg, jnp.zeros_like(dg))
            prob_grad = nt(dm, vg)
            probs = pst[buf, h]
            score_grad = (probs.astype(F32) * prob_grad).astype(BF16)
            dq = jnp.where(head, nn(score_grad, kg), dq)
            dks.append(nn(qt[HD * h : HD * (h + 1)], score_grad))
            dvs.append(nn(dt[HD * h : HD * (h + 1)], probs))
        dqt = (dq[:, 0:hw] * factor).T
        dkt = (jnp.concatenate(dks, axis=0) * math.log(2.0)).astype(BF16)
        dvt = jnp.concatenate(dvs, axis=0).astype(BF16)
        return s, dqt, dkt, dvt

    acc0[...] = jnp.zeros_like(acc0)
    acc1[...] = jnp.zeros_like(acc1)
    dmx_pad = jnp.zeros((share, 2 * 128 - hw), BF16)
    for s in range(parts):
        dmx[s, :, hw : 2 * 128] = dmx_pad
    fetch(0)

    def row_sums(values):
        return jnp.sum(values.astype(F32), axis=0, keepdims=True)

    def pair_half(it, carry):
        s, dqt, dkt, dvt = att_group(it, 1)
        uu[s, 0:hw, 0:share] = dqt.astype(BF16)
        uu[s, hw : 2 * hw, 0:share] = dkt
        uu[s, 2 * hw : qkvw, 0:share] = dvt
        back = uu[s, hw:qkvw, 0:share].T
        acc0[...] += nn(back, aw[s, hw:qkvw, :])
        late[pl.ds(2 * s + 1, 1), 0:hw] = row_sums(back[:, hw : 2 * hw])
        return advance("h", it, carry)

    lax.fori_loop(0, parts, pair_half, begin("h"))

    ng_copy = rcopy(ngs, ngr, ng_sem.at[0], ng_sem.at[1], (d, tp))
    pair_grad = acc0[...]
    lo_copy.wait()
    ngs[...] = pair_grad.astype(BF16)
    if NG_PLACE == 0:
        ng_copy.start()
    unit, _ = unit_of(xp[...].astype(F32))
    late[8:9, :] = jnp.sum(pair_grad * unit, axis=0, keepdims=True)
    late[9:10, :] = jnp.sum(pair_grad, axis=0, keepdims=True)

    stages = (dev_c, (dx, t), (dy, t))

    def vec(which, stage):
        buf, rx = (early, e_rx) if which == 0 else (late, l_rx)
        return rcopy(buf, rx.at[stage], sm_s.at[which, stage], sm_r.at[which, stage], stages[stage])

    def vec_far(which, k):
        rz = e_rz if which == 0 else l_rz
        return rcopy(
            rz.at[t], rz.at[t], sm_s.at[which, 2 + k], sm_r.at[which, 3 + t], (d, far(k))
        )

    def vec_next(which, stage):
        buf, rx = (early, e_rx) if which == 0 else (late, l_rx)
        vec(which, stage).wait_recv()
        vec(which, stage).wait_send()
        buf[...] = buf[...] + rx[stage]
        if stage < 2:
            vec(which, stage + 1).start()
        else:
            rz = e_rz if which == 0 else l_rz
            rz[t] = buf[...]
            for k in range(1, parts):
                vec_far(which, k).start()

    vec(0, 0).start()

    def own_half(it, carry):
        q = it - parts
        s, dqt, dkt, dvt = att_group(it, 0)
        dqt = (uu[s, 0:hw, 0:share].astype(F32) + dqt).astype(BF16)
        dd[0:hw, :] = dqt
        dd[hw : 2 * hw, :] = dkt
        dd[2 * hw : qkvw, :] = dvt
        back = dd[...].T
        acc1[...] += nn(back, aw[s, 0:qkvw, :])
        late[pl.ds(2 * s, 1), 0:hw] = row_sums(back[:, 0:hw])
        late[pl.ds(2 * s + 1, 1), 0:hw] = late[pl.ds(2 * s + 1, 1), 0:hw] + row_sums(
            back[:, 2 * hw : qkvw]
        )
        aw[s, 0:hw, :] = nn(dqt, xn[0:share, :]).astype(BF16)
        aw[s, hw:qkvw, :] = (
            nn(dd[hw:qkvw, :], xn[0:share, :]) + nn(uu[s, hw:qkvw, 0:share], xn[share:keys, :])
        ).astype(BF16)
        for a in range(2):
            ra(0, q, a).start()
        carry = advance("w", q, carry)
        if NG_PLACE > 0:

            @pl.when(q == NG_PLACE - 1)
            def _():
                ng_copy.start()

        for stage in range(3):

            @pl.when(q == stage)
            def _():
                vec_next(0, stage)

        return carry

    lax.fori_loop(parts, 2 * parts, own_half, begin("w"))

    own_grad = acc1[...]
    unit, scale_inv = unit_of(x_ref[...].astype(F32))
    late[8:9, :] = late[8:9, :] + jnp.sum(own_grad * unit, axis=0, keepdims=True)
    late[9:10, :] = late[9:10, :] + jnp.sum(own_grad, axis=0, keepdims=True)
    vec(1, 0).start()
    done = uu.at[0]
    xg_copy = pltpu.make_async_copy(mid, xg_ref, loc_sem.at[nblk])

    def aa(stage, a):
        _, _, first, second = route(t0 if a == 0 else 1 - t0)
        view = done.at[a_rows(stage, t0, a), a_lanes(a)]
        dev = (first, second, dev_c)[stage]
        return rcopy(view, view, aa_s.at[stage, a], aa_r.at[stage, a], dev)

    def att_final():
        for a in range(2):
            mine = a_rows(0, t0, a)
            low = CUTS[a][0]
            high = low + CUTS[a][1]
            total = aw[t, mine, low:high].astype(F32)
            for q in range(parts - 1):
                view = rz_a.at[q, :, a_lanes(a)]
                rcopy(view, view, ra_s.at[3, a, q], ra_r.at[3, a, q], (d, t)).wait_recv()
                total = total + rz_a[q, :, low:high].astype(F32)
            done[mine, low:high] = total.astype(BF16)
            aa(0, a).start()

    def att_round(stage):
        for a in range(2):
            aa(stage - 1, a).wait_recv()
            aa(stage, a).start()

    def rows_final():
        ng_copy.wait_recv()
        grad = own_grad + ngr[...].astype(F32)
        mid[...] = mid[...] + norm_back(grad, unit, scale_inv, gain1)
        xg_copy.start()

    vec_stage = 0
    for name, low, high in TAIL:
        if name == "v":
            vec_next(1, vec_stage)
            vec_stage += 1
        elif name == "aa0":
            att_final()
        elif name == "aa1":
            att_round(1)
        elif name == "aa2":
            att_round(2)
        elif name == "ng":
            rows_final()
        else:
            repeat(name, low, high)

    for j in range(nblk):
        af(2, j).wait_recv()
        f_out(j, 0).start()
        if j >= 2:
            f_out(j - 2, 1).wait()
        ol[(j % 2) * BLK : (j % 2 + 1) * BLK, :] = fg[t * nblk + j, 1].T
        f_out(j, 1).start()

    for which in range(2):
        rz = e_rz if which == 0 else l_rz
        for k in range(1, parts):
            s = far(k)
            rcopy(
                rz.at[s], rz.at[s], sm_s.at[which, 3], sm_r.at[which, 3 + s], (d, t)
            ).wait_recv()
    early[...] = ((e_rz[0] + e_rz[1]) + e_rz[2]) + e_rz[3]
    late[...] = ((l_rz[0] + l_rz[1]) + l_rz[2]) + l_rz[3]
    osm_ref[0:4, :] = early[0:4, :]
    osm_ref[4:6, :] = late[8:10, :]
    osm_ref[8:9, :] = late[pl.ds(2 * t, 1), :]
    osm_ref[9:10, :] = late[pl.ds(2 * t + 1, 1), :]
    for j in range(nblk):
        osm_ref[16 + j : 17 + j, :] = early[pl.ds(4 + t * nblk + j, 1), :]

    for k in range(1, parts):
        zb(k, 0).wait_send()
        zb(k, 1).wait_send()
        for which in range(2):
            vec_far(which, k).wait_send()
    x_copy.wait_send()
    ng_copy.wait_send()

    def drain_far(m, carry):
        left(f_any(0), fz_s.at[m])
        return carry

    lax.fori_loop(0, n_far, drain_far, 0)

    def drain_all(r, carry):
        left(f_any(2), cf_s.at[r])
        left(f_any(1), f2_s.at[r])
        left(f_any(0), f1_s.at[r])
        return carry

    lax.fori_loop(0, n_all, drain_all, 0)

    def drain_own(j, carry):
        for stage in range(3):
            left(f_any(stage), af_s.at[stage, j])
        return carry

    lax.fori_loop(0, nblk, drain_own, 0)
    for j in range(nblk):
        f_out(j, 0).wait()
    for j in range(nblk - 2, nblk):
        f_out(j, 1).wait()

    for q in range(parts):
        for a in range(2):
            for stage in range(3):
                left(a_any(2 - stage, a), ra_s.at[stage, a, q])
            if q < parts - 1:
                left(a_any(0, a), ra_s.at[3, a, q])
    for a in range(2):
        aa(2, a).wait_recv()
    oa_copy = pltpu.make_async_copy(done, oa_ref, loc_sem.at[nblk + 1])
    oa_copy.start()
    oa_copy.wait()
    xg_copy.wait()
    for stage in range(3):
        for a in range(2):
            aa(stage, a).wait_send()


def finish(
    lo,
    xg,
    up,
    dn,
    at,
    sm,
    lo_out,
    xg_out,
    up_out,
    dn_out,
    qkv_out,
    out_out,
    g2_out,
    s2_out,
    bo_out,
    bd_out,
    g1_out,
    s1_out,
    qv_out,
    bup_out,
    lo_b,
    xg_b,
    up_b,
    dn_b,
    at_b,
    up_f,
    dn_f,
    at_f,
    in_sem,
    out_sem,
):
    hw = out_out.shape[0]
    qkvw = qkv_out.shape[0]
    jobs = []
    for n, (src, mid_b, wide, dst) in enumerate(
        ((up, up_b, up_f, up_out), (dn, dn_b, dn_f, dn_out), (at, at_b, at_f, None))
    ):
        size = src.shape[0] // CHUNKS
        for i in range(CHUNKS):
            part = pl.ds(i * size, size)
            if dst is not None:
                to = dst.at[part, :]
            elif (i + 1) * size <= qkvw:
                to = qkv_out.at[part, :]
            else:
                to = out_out.at[pl.ds(i * size - qkvw, size), :]
            jobs.append((src.at[part, :], mid_b.at[part, :], wide.at[part, :], to))
    jobs.append((xg, xg_b, None, xg_out))
    jobs.append((lo, lo_b, None, lo_out))
    ins = [
        pltpu.make_async_copy(job[0], job[1], in_sem.at[i]) for i, job in enumerate(jobs)
    ]
    for cp in ins:
        cp.start()
    for i, ref in enumerate((g2_out, s2_out, bo_out, bd_out, g1_out, s1_out)):
        ref[...] = sm[i]
    qv_out[...] = sm[8:10, 0:hw]
    for j in range(bup_out.shape[0] // BLK):
        bup_out[j * BLK : (j + 1) * BLK] = sm[16 + j, 0:BLK]
    outs = []
    for i, (_, got, wide, dst) in enumerate(jobs):
        ins[i].wait()
        if wide is not None:
            wide[...] = got[...].astype(F32)
        outs.append(pltpu.make_async_copy(got if wide is None else wide, dst, out_sem.at[i]))
        outs[-1].start()
    for cp in outs:
        cp.wait()


def local(
    x_in,
    cotangent,
    lengths,
    bucket_ids,
    bucket_weights,
    ln1_gain,
    ln1_bias,
    w_qkv,
    qv_bias,
    w_out,
    b_out,
    ln2_gain,
    ln2_bias,
    w_up,
    b_up,
    w_down,
    b_down,
):
    share, width = x_in.shape
    hw = w_qkv.shape[2]
    heads = hw // HD
    parts = 4
    fw = w_up.shape[1]
    nblk = fw // BLK
    piece = width // GROUP
    keys = 2 * share
    n_all = parts * nblk
    n_far = n_all - nblk
    vm = pl.BlockSpec(memory_space=pltpu.VMEM)
    sm = pl.BlockSpec(memory_space=pltpu.SMEM)
    hbm = pl.BlockSpec(memory_space=pl.ANY)
    dma = pltpu.SemaphoreType.DMA
    scratch = [
        pltpu.VMEM((n_all + nblk, 2, width, BLK), BF16),
        pltpu.VMEM((parts, width, 4 * hw), BF16),
        pltpu.VMEM((SLOTS_C, 2, 4 * piece, BLK), BF16),
        pltpu.VMEM((n_all, 2, 2 * piece, BLK), BF16),
        pltpu.VMEM((n_all, 2, piece, BLK), BF16),
        pltpu.VMEM((n_far, 2, piece, BLK), BF16),
        pltpu.VMEM((parts, 4 * piece, 4 * hw), BF16),
        pltpu.VMEM((parts, 2 * piece, 4 * hw), BF16),
        pltpu.VMEM((parts, piece, 4 * hw), BF16),
        pltpu.VMEM((parts - 1, piece, 4 * hw), BF16),
        pltpu.VMEM((keys, width), BF16),
        pltpu.VMEM((share, width), BF16),
        pltpu.VMEM((parts, share, 256), BF16),
        pltpu.VMEM((parts, keys, 256), BF16),
        pltpu.VMEM((parts, keys, 256), BF16),
        pltpu.VMEM((parts, share, 256), BF16),
        pltpu.VMEM((parts, share, 256), BF16),
        pltpu.VMEM((parts, share, 128), F32),
        pltpu.VMEM((3 * hw, share), BF16),
        pltpu.VMEM((2, heads, share, share), BF16),
        pltpu.VMEM((share, width), F32),
        pltpu.VMEM((share, width), F32),
        pltpu.VMEM((share, width), F32),
        pltpu.VMEM((parts, width, width), BF16),
        pltpu.VMEM((share, width), BF16),
        pltpu.VMEM((width, share), BF16),
        pltpu.VMEM((share, width), BF16),
        pltpu.VMEM((share, width), BF16),
        pltpu.VMEM((parts, 1, fw), F32),
        pltpu.VMEM((parts, 2, hw), F32),
        pltpu.VMEM((24, width), F32),
        pltpu.VMEM((16, width), F32),
        pltpu.VMEM((3, 24, width), F32),
        pltpu.VMEM((parts, 24, width), F32),
        pltpu.VMEM((3, 16, width), F32),
        pltpu.VMEM((parts, 16, width), F32),
        dma((2 * nblk + 5,)),
        dma((2, heads)),
        dma((2, 3)),
        dma((2, parts)),
        dma((2,)),
        dma((6,)),
        dma((2, parts)),
        dma((3, 2, parts)),
        dma((3, 2, parts)),
        dma((n_far,)),
        dma((n_all,)),
        dma((3, n_all)),
        dma((3, n_all)),
        dma((n_all,)),
        dma((n_all,)),
        dma((n_all,)),
        dma((n_all,)),
        dma((n_all,)),
        dma((n_all,)),
        dma((n_far,)),
        dma((n_far,)),
        dma((3, nblk)),
        dma((3, nblk)),
        dma((4, 2, parts)),
        dma((4, 2, parts)),
        dma((3, 2)),
        dma((3, 2)),
        dma((2, 7)),
        dma((2, 7)),
        dma((2,)),
        pltpu.SemaphoreType.REGULAR,
    ]
    layer_out, x_grad, up, down, att, small, _ = pl.pallas_call(
        kernel,
        out_shape=[
            jax.ShapeDtypeStruct((share, width), BF16),
            jax.ShapeDtypeStruct((share, width), F32),
            jax.ShapeDtypeStruct((width, fw), BF16),
            jax.ShapeDtypeStruct((fw, width), BF16),
            jax.ShapeDtypeStruct((width, width), BF16),
            jax.ShapeDtypeStruct((24, width), F32),
            jax.ShapeDtypeStruct((parts * heads, 2, share, share), BF16),
        ],
        in_specs=[vm, hbm, sm, sm, sm, vm, vm, hbm, vm, hbm, vm, vm, vm, hbm, vm, hbm, vm],
        out_specs=[hbm, hbm, hbm, hbm, hbm, vm, hbm],
        scratch_shapes=scratch,
        compiler_params=pltpu.CompilerParams(
            collective_id=0, has_side_effects=True, vmem_limit_bytes=67043328
        ),
    )(
        x_in,
        cotangent,
        lengths,
        bucket_ids,
        bucket_weights,
        ln1_gain,
        ln1_bias,
        w_qkv.transpose(0, 2, 1),
        qv_bias,
        w_out,
        b_out,
        ln2_gain,
        ln2_bias,
        w_up,
        b_up,
        w_down,
        b_down,
    )
    dp = lax.axis_size("dp")
    if dp > GROUP:
        groups = [[g + GROUP * i for i in range(dp // GROUP)] for g in range(GROUP)]
        sums = lax.psum(
            tuple(g.astype(F32) for g in (up, down, att, small)), "dp", axis_index_groups=groups
        )
        up, down, att = (g.astype(BF16) for g in sums[:3])
        small = sums[3]
    flat = jax.ShapeDtypeStruct((width,), F32)
    outs = pl.pallas_call(
        finish,
        out_shape=[
            jax.ShapeDtypeStruct((share, width), BF16),
            jax.ShapeDtypeStruct((share, width), F32),
            jax.ShapeDtypeStruct((width, fw), F32),
            jax.ShapeDtypeStruct((fw, width), F32),
            jax.ShapeDtypeStruct((3 * hw, width), F32),
            jax.ShapeDtypeStruct((hw, width), F32),
            flat,
            flat,
            flat,
            flat,
            flat,
            flat,
            jax.ShapeDtypeStruct((2, hw), F32),
            jax.ShapeDtypeStruct((fw,), F32),
        ],
        in_specs=[hbm] * 5 + [vm],
        out_specs=[hbm] * 6 + [vm] * 8,
        scratch_shapes=[
            pltpu.VMEM((share, width), BF16),
            pltpu.VMEM((share, width), F32),
            pltpu.VMEM((width, fw), BF16),
            pltpu.VMEM((fw, width), BF16),
            pltpu.VMEM((width, width), BF16),
            pltpu.VMEM((width, fw), F32),
            pltpu.VMEM((fw, width), F32),
            pltpu.VMEM((width, width), F32),
            dma((3 * CHUNKS + 2,)),
            dma((3 * CHUNKS + 2,)),
        ],
    )(layer_out, x_grad, up, down, att, small)
    layer_out, x_grad, g_up, g_down, g_qkv, g_out, g2, s2, bo, bd, g1, s1, g_qv, g_bup = outs
    return (
        layer_out,
        x_grad,
        g1,
        s1,
        g_qkv.reshape(3, hw, width).transpose(0, 2, 1),
        g_qv,
        g_out,
        bo,
        g2,
        s2,
        g_up,
        g_bup,
        g_down,
        bd,
    )


def solution(mesh):
    return jax.shard_map(
        local,
        mesh=mesh,
        in_specs=(
            P(("dp", "tensor"), None),
            P(("dp", "tensor"), None),
            P("dp", None),
            P("dp"),
            P(),
            P(),
            P(),
            P(None, None, "tensor"),
            P(None, "tensor"),
            P("tensor", None),
            P(),
            P(),
            P(),
            P(None, "tensor"),
            P("tensor"),
            P("tensor", None),
            P(),
        ),
        out_specs=(
            P(("dp", "tensor"), None),
            P(("dp", "tensor"), None),
            P(),
            P(),
            P(None, None, "tensor"),
            P(None, "tensor"),
            P("tensor", None),
            P(),
            P(),
            P(),
            P(None, "tensor"),
            P("tensor"),
            P("tensor", None),
            P(),
        ),
        check_vma=False,
    )
```

```python
import functools
import math

import jax
import jax.numpy as jnp
from jax import lax
from jax.experimental import pallas as pl
from jax.experimental.pallas import tpu as pltpu
from jax.sharding import PartitionSpec as P

HD = 32
BUCKET = 256
EPSILON = 1e-05
GROUP = 8
BLK = 256
BIG = 1e30
F32 = jnp.float32
BF16 = jnp.bfloat16
MESH = pl.DeviceIdType.MESH
RSQRT2 = 1.0 / math.sqrt(2.0)
RSQRT2PI = 1.0 / math.sqrt(2.0 * math.pi)
SLOTS_C = 2
X_PLACE = 0
WIDE_FROM = 15
NG_PLACE = 1
EARLY_FAR = 3
CUTS = ((0, 256), (256, 384))
CHUNKS = 4
PLAN = {
    "p0": (
        ("a0", (0, 1)),
        ("a1", (0, 1)),
    ),
    "p1": (
        ("a0", (1, 3)),
        ("a2", (0, 1)),
    ),
    "p2": (
        ("a1", (1, 3)),
        ("a2", (1, 3)),
    ),
    "pj": (
    ),
    "o": (
    ),
    "q": (
        ("g0", (0, 0, 11, 14, 15)),
        ("g1", (0, 0, 0, 0, 8)),
    ),
    "mid": (
        ("g1", (8, 10)),
    ),
    "r": (
        ("g1", (10, 11, 15, 15, 15, 15, 15, 15, 15, 15, 15, 15, 15, 15, 15, 15, 15, 15, 15, 15, 15)),
        ("g2", (0, 0, 3, 3, 5, 8, 9, 9, 9, 11, 13, 15, 15, 15, 15, 15, 15, 15, 15, 15, 15)),
        ("rf", (0, 0, 0, 0, 0, 0, 0, 0, 0, 0, 0, 0, 0, 0, 0, 2, 2, 4, 4, 5, 5)),
        ("r1", (0, 0, 0, 0, 0, 0, 0, 0, 0, 0, 0, 0, 0, 2, 3, 3, 4, 4, 5, 5, 7)),
        ("r2", (0, 0, 0, 0, 0, 0, 0, 1, 2, 3, 4, 4, 4, 6, 8, 8, 10, 11, 12, 13, 14)),
    ),
    "ln": (
        ("rf", (5, 7)),
        ("r2", (14, 16)),
    ),
    "k": (
        ("rf", (7, 7, 8, 8, 9)),
        ("r1", (7, 9, 9, 9, 9)),
        ("r2", (16, 16, 16, 20, 20)),
    ),
    "h": (
        ("rf", (9, 9, 9, 11, 17)),
        ("r1", (9, 14, 16, 17, 17)),
        ("f0", (0, 0, 0, 0, 2)),
    ),
    "w": (
        ("rf", (17, 17, 19, 19, 20)),
        ("r1", (17, 20, 20, 20, 20)),
        ("b3", (0, 0, 0, 0, 2)),
        ("b2", (0, 0, 0, 2, 3)),
        ("b1", (0, 0, 2, 3, 4)),
        ("f0", (2, 2, 3, 3, 5)),
        ("f1", (0, 1, 1, 3, 3)),
        ("f2", (0, 0, 0, 0, 3)),
    ),
}
TAIL = (
    ("b2", 3, 4),
    ("v", 0, 0),
    ("f1", 3, 5),
    ("b3", 2, 4),
    ("v", 0, 0),
    ("aa0", 0, 0),
    ("v", 0, 0),
    ("aa1", 0, 0),
    ("f2", 3, 5),
    ("ng", 0, 0),
    ("aa2", 0, 0),
)


def nn(a, b):
    return lax.dot_general(a, b, (((1,), (0,)), ((), ())), preferred_element_type=F32)


def nt(a, b):
    return lax.dot_general(a, b, (((1,), (1,)), ((), ())), preferred_element_type=F32)


def unit_of(values):
    centre = values - jnp.mean(values, axis=-1, keepdims=True)
    scale_inv = lax.rsqrt(jnp.mean(centre * centre, axis=-1, keepdims=True) + EPSILON)
    return centre * scale_inv, scale_inv


def norm_back(grad, unit, scale_inv, gain):
    scaled = grad * gain
    return scale_inv * (
        scaled
        - jnp.mean(scaled, axis=-1, keepdims=True)
        - unit * jnp.mean(scaled * unit, axis=-1, keepdims=True)
    )


def lanes(shape):
    return lax.broadcasted_iota(jnp.int32, shape, 1)


def kernel(
    x_ref,
    cot_ref,
    len_ref,
    bid_ref,
    bw_ref,
    g1_ref,
    s1_ref,
    wqkv_ref,
    qvb_ref,
    wout_ref,
    bout_ref,
    g2_ref,
    s2_ref,
    wup_ref,
    bup_ref,
    wdn_ref,
    bdn_ref,
    lo_ref,
    xg_ref,
    ou_ref,
    od_ref,
    oa_ref,
    osm_ref,
    ph_ref,
    fg,
    aw,
    rc_f,
    r2_f,
    r1_f,
    rz_f,
    rc_a,
    r2_a,
    r1_a,
    rz_a,
    xn,
    xp,
    qb,
    kb,
    vb,
    mx,
    dmx,
    stat,
    dd,
    pst,
    mid,
    acc0,
    acc1,
    uu,
    ol,
    olt,
    ngs,
    ngr,
    bupa,
    qvba,
    early,
    late,
    e_rx,
    e_rz,
    l_rx,
    l_rz,
    loc_sem,
    ps_sem,
    za_s,
    za_r,
    zx_sem,
    zb_s,
    zb_r,
    ga_s,
    ga_r,
    zf_s,
    zf_r,
    gf_s,
    gf_r,
    cf_s,
    cf_r,
    f2_s,
    f2_r,
    f1_s,
    f1_r,
    fz_s,
    fz_r,
    af_s,
    af_r,
    ra_s,
    ra_r,
    aa_s,
    aa_r,
    sm_s,
    sm_r,
    ng_sem,
    credit,
):
    share, width = x_ref.shape
    hw = wqkv_ref.shape[1]
    heads = hw // HD
    qkvw = 3 * hw
    parts = 4
    nblk = wup_ref.shape[1] // BLK
    piece = width // GROUP
    keys = 2 * share
    factor = HD ** (-0.5)
    q_scale = factor * math.log2(math.e)

    d = lax.axis_index("dp")
    t = lax.axis_index("tensor")
    c = d % 2
    bx = (d // 2) % 2
    by = (d // 4) % 2
    dev_c = (d + 1 - 2 * c, t)
    dx = d + 2 - 4 * bx
    dy = d + 4 - 8 * by
    t0 = t % 2
    t1 = t // 2
    tp = t + 1 - 2 * t0

    def quotient(n, step, limit):
        if isinstance(n, int):
            return n // step
        return sum(jnp.where(n >= i, 1, 0) for i in range(step, limit, step))

    def odd(n, limit):
        return n - 2 * quotient(n, 2, limit)

    def differ(a, b):
        return a + b - 2 * a * b

    def far_bits(k):
        high = quotient(k, 2, parts)
        low = differ(t0, k - 2 * high)
        return low + 2 * differ(t1, high), low

    def far(k):
        return far_bits(k)[0]

    def route(par):
        low = bx + par * (by - bx)
        high = by + par * (bx - by)
        first = (dx + par * (dy - dx), t)
        second = (dy + par * (dx - dy), t)
        return low, high, first, second

    def rcopy(src, dst, ssem, rsem, dev):
        return pltpu.make_async_remote_copy(
            src_ref=src, dst_ref=dst, send_sem=ssem, recv_sem=rsem, device_id=dev, device_id_type=MESH
        )

    def arrived(view, sem):
        rcopy(view, view, sem, sem, (d, t)).wait_recv()

    def left(view, sem):
        rcopy(view, view, sem, sem, (d, t)).wait_send()

    def rows(start, size):
        return pl.ds(pl.multiple_of(start, 16), size)

    def up_load(j):
        return pltpu.make_async_copy(
            wup_ref.at[:, pl.ds(j * BLK, BLK)], fg.at[t * nblk + j, 0], loc_sem.at[j]
        )

    def dn_load(j):
        return pltpu.make_async_copy(
            wdn_ref.at[pl.ds(j * BLK, BLK), :],
            uu.at[j // 2, pl.ds((j % 2) * BLK, BLK), :],
            loc_sem.at[nblk + j],
        )

    cot_load = pltpu.make_async_copy(cot_ref, ol, loc_sem.at[2 * nblk])

    a_loads = [
        pltpu.make_async_copy(
            wqkv_ref.at[i], aw.at[t, pl.ds(i * hw, hw), :], loc_sem.at[2 * nblk + 1 + i]
        )
        for i in range(3)
    ]
    a_loads.append(
        pltpu.make_async_copy(
            wout_ref, aw.at[t, pl.ds(qkvw, hw), :], loc_sem.at[2 * nblk + 4]
        )
    )
    for cp in a_loads:
        cp.start()
    for j in range(nblk):
        dn_load(j).start()
        up_load(j).start()
    cot_load.start()
    bupa[t] = bup_ref[...][None, :]
    qvba[t] = qvb_ref[...]

    barrier = pltpu.get_barrier_semaphore()
    for dev in (dev_c, (dx, t), (dy, t), (d, far(1)), (d, far(2)), (d, far(3))):
        pl.semaphore_signal(barrier, inc=1, device_id=dev, device_id_type=MESH)
    pl.semaphore_wait(barrier, 6)

    def a_rows(stage, parity, a):
        low, high, _, _ = route(parity if a == 0 else 1 - parity)
        if stage == 0:
            return rows((c * 4 + high * 2 + low) * piece, piece)
        if stage == 1:
            return rows((c * 4 + high * 2) * piece, 2 * piece)
        return rows(c * 4 * piece, 4 * piece)

    def a_lanes(a):
        return pl.ds(CUTS[a][0], CUTS[a][1])

    def a_any(stage, a):
        return aw.at[0, 0 : (piece, 2 * piece, 4 * piece)[stage], a_lanes(a)]

    def za(k, a):
        view = aw.at[t, a_rows(0, t0, a), a_lanes(a)]
        return rcopy(view, view, za_s.at[a, k - 1], za_r.at[a, t], (d, far(k)))

    def zb(k, which):
        dst = (bupa if which == 0 else qvba).at[t]
        return rcopy(dst, dst, zb_s.at[2 * (k - 1) + which], zb_r.at[which, t], (d, far(k)))

    def zb_wait(s, which):
        dst = (bupa if which == 0 else qvba).at[s]
        rcopy(dst, dst, zb_s.at[0], zb_r.at[which, s], (d, t)).wait_recv()

    x_copy = rcopy(x_ref, xp, zx_sem.at[0], zx_sem.at[1], (d, tp))

    for cp in a_loads:
        cp.wait()
    for k in range(1, parts):
        for a in range(2):
            za(k, a).start()
        zb(k, 1).start()
    for k in range(1, parts):
        zb(k, 0).start()

    def ga(stage, s, parity, a):
        _, _, first, second = route(parity if a == 0 else 1 - parity)
        view = aw.at[s, a_rows(stage, parity, a), a_lanes(a)]
        dev = (first, second, dev_c)[stage]
        return rcopy(view, view, ga_s.at[stage, a, s], ga_r.at[stage, a, s], dev)

    def step_a(stage, i):
        s, parity = far_bits(i + 1)
        for a in range(2):
            if stage == 0:
                arrived(a_any(0, a), za_r.at[a, s])
            else:
                arrived(a_any(stage - 1, a), ga_r.at[stage - 1, a, s])
            ga(stage, s, parity, a).start()

    n_far = (parts - 1) * nblk

    def far_block(m):
        j = quotient(m, parts - 1, n_far)
        s, parity = far_bits(1 + m - (parts - 1) * j)
        return s, j, s * nblk + j, differ(parity, odd(j, nblk))

    def own_parity(j):
        return differ(t0, odd(j, nblk))

    def gf(stage, m):
        _, _, b, par = far_block(m)
        low, high, first, second = route(par)
        if stage == 0:
            view, dev = fg.at[b, :, rows((c * 4 + high * 2 + low) * piece, piece), :], first
        elif stage == 1:
            view, dev = fg.at[b, :, rows((c * 4 + high * 2) * piece, 2 * piece), :], second
        else:
            view, dev = fg.at[b, :, rows(c * 4 * piece, 4 * piece), :], dev_c
        return rcopy(view, view, gf_s.at[stage, b], gf_r.at[stage, b], dev)

    def f_any(stage):
        return fg.at[0, :, 0 : (piece, 2 * piece, 4 * piece)[stage], :]

    def step_g(stage, m):
        b = far_block(m)[2]
        if WIDE_FROM >= n_far:
            if stage == 0:
                arrived(f_any(0), zf_r.at[b])
            else:
                arrived(f_any(stage - 1), gf_r.at[stage - 1, b])
            gf(stage, m).start()
            return
        if stage == 0:

            @pl.when(m < WIDE_FROM)
            def _():
                arrived(f_any(0), zf_r.at[b])
                gf(0, m).start()

            return
        if stage == 1:

            @pl.when(m < WIDE_FROM)
            def _():
                arrived(f_any(0), gf_r.at[0, b])

            @pl.when(m >= WIDE_FROM)
            def _():
                arrived(f_any(1), zf_r.at[b])

        else:
            arrived(f_any(1), gf_r.at[1, b])
        gf(stage, m).start()

    n_all = parts * nblk

    def block(r):
        own = jnp.where(r < nblk, 1, 0)
        m = r - nblk
        turn_j = quotient(m, parts - 1, n_far)
        k = (1 - own) * (1 + m - (parts - 1) * turn_j)
        j = own * r + (1 - own) * turn_j
        s, parity = far_bits(k)
        home = s * nblk + j
        return k, j, s, home, home + own * (n_all + j - home), differ(parity, odd(j, nblk))

    def rf(stage, r, slot=None):
        k, j, s, _, g, par = block(r)
        low, high, first, second = route(par)
        if stage == 0:
            return rcopy(
                fg.at[g, :, rows((1 - c) * 4 * piece, 4 * piece), :],
                rc_f.at[slot],
                cf_s.at[r],
                cf_r.at[r],
                dev_c,
            )
        if stage == 1:
            return rcopy(
                fg.at[g, :, rows((c * 4 + (1 - high) * 2) * piece, 2 * piece), :],
                r2_f.at[r],
                f2_s.at[r],
                f2_r.at[r],
                second,
            )
        if stage == 2:
            return rcopy(
                fg.at[g, :, rows((c * 4 + high * 2 + 1 - low) * piece, piece), :],
                r1_f.at[r],
                f1_s.at[r],
                f1_r.at[r],
                first,
            )
        z = jnp.maximum((k - 1) * nblk + j, 0)
        if stage == 4:
            return rcopy(
                fg.at[g, :, rows((c * 4 + high * 2) * piece, 2 * piece), :],
                rz_f.at[z],
                fz_s.at[z],
                fz_r.at[z],
                (d, s),
            )
        return rcopy(
            fg.at[g, :, rows((c * 4 + high * 2 + low) * piece, piece), :],
            rz_f.at[z, :, 0:piece, :],
            fz_s.at[z],
            fz_r.at[z],
            (d, s),
        )

    def add_rows(ref, got):
        ref[...] = (ref[...].astype(F32) + got[...].astype(F32)).astype(BF16)

    def rf_core(r, slot):
        g = block(r)[4]
        arrived(rc_f.at[slot], cf_r.at[r])
        add_rows(fg.at[g, :, rows(c * 4 * piece, 4 * piece), :], rc_f.at[slot])

        @pl.when(r < n_all - SLOTS_C)
        def _():
            pl.semaphore_signal(credit, inc=1, device_id=dev_c, device_id_type=MESH)

    def turn(i):
        return i + nblk - n_all * jnp.where(i >= n_all - nblk, 1, 0)

    def rf_first(r):
        _, j, _, _, g, par = block(r)
        _, high, _, _ = route(par)
        both = fg.at[g, :, rows((c * 4 + high * 2) * piece, 2 * piece), :]
        arrived(r2_f.at[r], f2_r.at[r])
        add_rows(both, r2_f.at[r])

        @pl.when((j < EARLY_FAR) & (r >= nblk))
        def _():
            rf(4, r).start()

        @pl.when((j < EARLY_FAR) & (r < nblk))
        def _():
            total = both[...].astype(F32)
            for k in range(1, parts):
                z = (k - 1) * nblk + j
                arrived(rz_f.at[z], fz_r.at[z])
                total = total + rz_f[z].astype(F32)
            both[...] = total.astype(BF16)

        @pl.when((j >= EARLY_FAR) | (r < nblk))
        def _():
            rf(2, r).start()

    def rf_far(r):
        _, j, _, _, g, par = block(r)
        low, high, _, _ = route(par)

        @pl.when((j >= EARLY_FAR) | (r < nblk))
        def _():
            arrived(r1_f.at[r], f1_r.at[r])
            add_rows(fg.at[g, :, rows((c * 4 + high * 2 + low) * piece, piece), :], r1_f.at[r])

        @pl.when((j >= EARLY_FAR) & (r >= nblk))
        def _():
            rf(3, r).start()

    def af(stage, j):
        low, high, first, second = route(own_parity(j))
        b = t * nblk + j
        if stage == 0:
            view, dev = fg.at[b, :, rows((c * 4 + high * 2 + low) * piece, piece), :], first
        elif stage == 1:
            view, dev = fg.at[b, :, rows((c * 4 + high * 2) * piece, 2 * piece), :], second
        else:
            view, dev = fg.at[b, :, rows(c * 4 * piece, 4 * piece), :], dev_c
        return rcopy(view, view, af_s.at[stage, j], af_r.at[stage, j], dev)

    def f_final(j):
        low, high, _, _ = route(own_parity(j))
        mine = rows((c * 4 + high * 2 + low) * piece, piece)

        @pl.when(j < EARLY_FAR)
        def _():
            fg[t * nblk + j, :, mine, :] = fg[n_all + j, :, mine, :]

        @pl.when(j >= EARLY_FAR)
        def _():
            total = fg[n_all + j, :, mine, :].astype(F32)
            for k in range(1, parts):
                z = (k - 1) * nblk + j
                arrived(rz_f.at[z, :, 0:piece, :], fz_r.at[z])
                total = total + rz_f[z, :, 0:piece, :].astype(F32)
            fg[t * nblk + j, :, mine, :] = total.astype(BF16)

        af(0, j).start()

    def f_out(j, which):
        if which == 0:
            return pltpu.make_async_copy(
                fg.at[t * nblk + j, 0], ou_ref.at[:, pl.ds(j * BLK, BLK)], loc_sem.at[j]
            )
        return pltpu.make_async_copy(
            ol.at[pl.ds((j % 2) * BLK, BLK), :],
            od_ref.at[pl.ds(j * BLK, BLK), :],
            loc_sem.at[nblk + 2 + j % 2],
        )

    def f_second(j):
        arrived(f_any(0), af_r.at[0, j])
        af(1, j).start()

    def f_third(j):
        arrived(f_any(1), af_r.at[1, j])
        af(2, j).start()

    def group_bits(it):
        n = it + 1
        return far_bits(n - parts * quotient(n, parts, 2 * parts + 1))

    def group_of(it):
        return group_bits(it)[0]

    def ra(stage, q, a):
        s, parity = group_bits(q)
        low, high, first, second = route(parity if a == 0 else 1 - parity)
        if stage == 0:
            where, buf, dev = rows((1 - c) * 4 * piece, 4 * piece), rc_a, dev_c
        elif stage == 1:
            where, buf, dev = rows((c * 4 + (1 - high) * 2) * piece, 2 * piece), r2_a, second
        elif stage == 2:
            where, buf, dev = rows((c * 4 + high * 2 + 1 - low) * piece, piece), r1_a, first
        else:
            where, buf, dev = rows((c * 4 + high * 2 + low) * piece, piece), rz_a, (d, s)
            q = jnp.minimum(q, parts - 2)
        return rcopy(
            aw.at[s, where, a_lanes(a)],
            buf.at[q, :, a_lanes(a)],
            ra_s.at[stage, a, q],
            ra_r.at[stage, a, q],
            dev,
        )

    def step_b(stage, q):
        s, parity = group_bits(q)
        buf = (rc_a, r2_a, r1_a)[stage - 1]
        for a in range(2):
            view = buf.at[q, :, a_lanes(a)]
            arrived(view, ra_r.at[stage - 1, a, q])
            add_rows(aw.at[s, a_rows(3 - stage, parity, a), a_lanes(a)], view)
            if stage < 3:
                ra(stage, q, a).start()
            else:

                @pl.when(q < parts - 1)
                def _():
                    ra(3, q, a).start()

    steps = {
        "a0": lambda i: step_a(0, i),
        "a1": lambda i: step_a(1, i),
        "a2": lambda i: step_a(2, i),
        "g0": lambda i: step_g(0, i),
        "g1": lambda i: step_g(1, i),
        "g2": lambda i: step_g(2, i),
        "r2": lambda i: rf(1, turn(i)).start(),
        "r1": lambda i: rf_first(turn(i)),
        "rf": lambda i: rf_far(turn(i)),
        "b1": lambda i: step_b(1, i),
        "b2": lambda i: step_b(2, i),
        "b3": lambda i: step_b(3, i),
        "f0": lambda i: f_final(i),
        "f1": lambda i: f_second(i),
        "f2": lambda i: f_third(i),
    }

    def repeat(name, low, high):
        def one(i, carry):
            steps[name](i)
            return carry

        lax.fori_loop(low, high, one, 0)

    def advance(place, idx=None, reached=None):
        after = []
        for n, (name, counts) in enumerate(PLAN[place]):
            low = counts[0] if reached is None else reached[n]
            high = low
            if idx is None:
                high = counts[-1]
            else:
                for i in range(len(counts) - 1):
                    more = counts[i + 1] - counts[i]
                    if more:
                        high = high + jnp.where(idx == i, more, 0)
            repeat(name, low, high)
            after.append(high)
        return tuple(after)

    def begin(place):
        return tuple(jnp.int32(counts[0]) for _, counts in PLAN[place])

    gain1 = g1_ref[...][None, :]
    shift1 = s1_ref[...][None, :]
    unit, _ = unit_of(x_ref[...].astype(F32))
    xn[0:share, :] = (unit * gain1 + shift1).astype(BF16)
    advance("p0")

    def zf(k, j):
        low, high, _, _ = route(own_parity(j))
        where = rows((c * 4 + high * 2 + low) * piece, piece)
        if j * (parts - 1) + k - 1 >= WIDE_FROM:
            where = rows((c * 4 + high * 2) * piece, 2 * piece)
        view = fg.at[t * nblk + j, :, where, :]
        return rcopy(
            view, view, zf_s.at[(k - 1) * nblk + j], zf_r.at[t * nblk + j], (d, far(k))
        )

    for j in range(nblk):
        up_load(j).wait()
        dn_load(j).wait()
        fg[t * nblk + j, 1] = uu[j // 2, (j % 2) * BLK : (j % 2 + 1) * BLK, :].T
    for m in range((parts - 1) * nblk):
        if m == X_PLACE:
            x_copy.start()
        zf(1 + m % (parts - 1), m // (parts - 1)).start()

    advance("p1")

    bucket = bid_ref[0]
    span = jnp.where(bucket == 0, BUCKET, jnp.where(bucket == 1, 2 * BUCKET, 4 * BUCKET))
    weight = jnp.where(bucket == 0, bw_ref[0], jnp.where(bucket == 1, bw_ref[1], bw_ref[2]))

    def slot_info(base, shape):
        place = base + lax.broadcasted_iota(jnp.int32, shape, 0)
        item = jnp.zeros(shape, jnp.int32)
        for j in range(1, len_ref.shape[1]):
            item = item + jnp.where(place >= j * span, 1, 0)
        length = jnp.zeros(shape, jnp.int32)
        for j in range(len_ref.shape[1]):
            length = jnp.where(item == j, len_ref[0, j], length)
        return item, (place - item * span) < length

    wide = (share, 2 * 128)
    lane = lanes(wide)
    slots = len_ref.shape[1]
    in_aux = (lane >= hw) & (lane < hw + slots)
    one_aux = jnp.where(lane >= hw, 1.0, 0.0).astype(BF16)

    own_item, own_live = slot_info(t * share, wide)
    q_aux = jnp.where(in_aux & (own_item == lane - hw), 1.0, 0.0).astype(BF16)
    k_aux0 = jnp.where(in_aux & ~((own_item == lane - hw) & own_live), -BIG, 0.0).astype(BF16)
    pair_item, pair_live = slot_info(tp * share, wide)
    k_aux1 = jnp.where(in_aux & ~((pair_item == lane - hw) & pair_live), -BIG, 0.0).astype(BF16)
    for s in range(parts):
        qb[s] = q_aux
        kb[s, 0:share] = k_aux0
        kb[s, share:keys] = k_aux1
        vb[s, 0:share] = one_aux
        vb[s, share:keys] = one_aux
    _, live1 = slot_info(t * share, (share, 128))
    row_weight = jnp.where(live1, weight, 0.0)[:, 0:1]

    advance("p2")

    def project(s, half, own):
        base = half * share
        first = 0 if own else hw
        out = nt(xn[base : base + share, :], aw[s, first:qkvw, :])
        if own:
            qb[s, :, 0:hw] = ((out[:, 0:hw] + qvba[s, 0:1, :]) * q_scale).astype(BF16)
        at = hw - first
        kb[s, base : base + share, 0:hw] = out[:, at : at + hw].astype(BF16)
        vb[s, base : base + share, 0:hw] = (
            out[:, at + hw : at + 2 * hw] + qvba[s, 1:2, :]
        ).astype(BF16)

    lane_w = lanes((share, 2 * 128))
    lane_n = lanes((share, 128))

    def head_lanes(h):
        return (lane_w >= HD * h) & (lane_w < HD * (h + 1))

    def spread(values, at):
        out = jnp.zeros((share, 2 * 128), F32)
        for h in range(heads):
            out = jnp.where(head_lanes(h), values[:, at + h : at + h + 1], out)
        return out

    def p_out(s, h, half, buf):
        return pltpu.make_async_copy(
            pst.at[buf, h], ph_ref.at[s * heads + h, half], ps_sem.at[buf, h]
        )

    at0 = hw - 128
    at1 = at0 + 32
    at2 = at0 + 64

    def att_forward(k, half):
        s = far(k)
        base = half * share
        buf = odd(k, parts)
        if half == 1:
            for h in range(heads):
                p_out(s, h, half, buf).wait()
        else:

            @pl.when(k >= 2)
            def _():
                for h in range(heads):
                    p_out(s, h, half, buf).wait()

        qg = qb[s]
        kg = kb[s, base : base + share]
        vg = vb[s, base : base + share]
        out = jnp.zeros((share, 2 * 128), F32)
        tops = jnp.zeros((share, 128), F32)
        for h in range(heads):
            head = head_lanes(h)
            qm = jnp.where(head | (lane_w >= hw), qg, jnp.zeros_like(qg))
            scores = nt(qm, kg)
            top = jnp.max(scores, axis=1, keepdims=True)
            probs = jnp.exp2(scores - top).astype(BF16)
            pst[buf, h] = probs
            mixed = nn(probs, vg)
            out = jnp.where(head | (lane_w == hw + h), mixed, out)
            tops = jnp.where(lane_n == at0 + h, top, tops)
        for h in range(heads):
            p_out(s, h, half, buf).start()
        sums = jnp.where((lane_n >= at0) & (lane_n < at0 + heads), out[:, 128:256], 1.0)
        log_sum = tops + jnp.log2(sums)
        if half == 0:
            mx[s] = (out * spread(1.0 / sums, at0)).astype(BF16)
            stat[s] = jnp.where(lane_n < at1, tops, pltpu.roll(log_sum, 32, 1))
        else:
            before = stat[s]
            log_before = pltpu.roll(before, 96, 1)
            upper = jnp.maximum(log_sum, log_before)
            lower = jnp.minimum(log_sum, log_before)
            log_all = upper + jnp.log2(1.0 + jnp.exp2(lower - upper))
            part0 = jnp.exp2(log_before - log_all)
            part1 = jnp.exp2(log_sum - log_all) / sums
            mx[s] = (
                mx[s].astype(F32) * spread(part0, at0) + out * spread(part1, at0)
            ).astype(BF16)
            stat[s] = jnp.where(
                lane_n < at1,
                jnp.exp2(before - log_all),
                pltpu.roll(jnp.exp2(tops - log_all), 32, 1),
            )

    def own_keys(k, carry):
        s = far(k)

        @pl.when(k > 0)
        def _():
            zb_wait(s, 1)
            for a in range(2):
                arrived(a_any(2, a), ga_r.at[2, a, s])

        project(s, 0, True)

        @pl.when(k == 0)
        def _():
            advance("pj")

        att_forward(k, 0)
        return advance("o", k, carry)

    lax.fori_loop(0, parts, own_keys, begin("o"))

    x_copy.wait_recv()
    unit, _ = unit_of(xp[...].astype(F32))
    xn[share:keys, :] = (unit * gain1 + shift1).astype(BF16)

    def pair_keys(k, carry):
        project(far(k), 1, False)
        att_forward(k, 1)
        return advance("q", k, carry)

    lax.fori_loop(0, parts, pair_keys, begin("q"))
    for buf in range(2):
        for h in range(heads):
            p_out(0, h, 1, buf).wait()

    branch = jnp.zeros((share, width), F32)
    for s in range(parts):
        branch = branch + nn(mx[s, :, 0:hw], aw[s, qkvw : 4 * hw, :])
    middle = x_ref[...].astype(F32) + (branch + bout_ref[...][None, :])
    mid[...] = middle
    unit, _ = unit_of(middle)
    normed = (unit * g2_ref[...][None, :] + s2_ref[...][None, :]).astype(BF16)
    n2 = uu.at[0, 0:share, :]
    n2t = uu.at[1, :, 0:share]
    n2[...] = normed
    n2t[...] = normed.T
    cot_load.wait()
    low_grad = (ol[...].astype(F32) * row_weight).astype(BF16)
    early[...] = jnp.zeros_like(early)
    late[...] = jnp.zeros_like(late)
    early[3:4, :] = jnp.sum(low_grad.astype(F32), axis=0, keepdims=True)
    ol[...] = low_grad
    olt[...] = low_grad.T
    acc0[...] = jnp.zeros_like(acc0)
    acc1[...] = jnp.zeros_like(acc1)

    for k in range(1, parts):
        zb_wait(far(k), 0)
    advance("mid")

    def ffn(r, carry):
        k, j, s, home, g, _ = block(r)

        @pl.when(k > 0)
        def _():
            arrived(f_any(2), gf_r.at[2, home])

        wu = fg[home, 0]
        wd = fg[home, 1]
        hidden = nn(n2[...], wu) + bupa[s, :, pl.ds(pl.multiple_of(j * BLK, BLK), BLK)]
        cdf = 0.5 + 0.5 * lax.erf(hidden * RSQRT2)
        slope = cdf + hidden * (jnp.exp(-0.5 * hidden * hidden) * RSQRT2PI)
        active = (hidden * cdf).astype(BF16)
        act_grad = nn(ol[...], wd)
        hid_grad = (slope * act_grad).astype(BF16)
        acc0[...] += nt(active, wd)
        acc1[...] += nt(hid_grad, wu)
        early[pl.ds(4 + home, 1), 0:BLK] = jnp.sum(hid_grad.astype(F32), axis=0, keepdims=True)
        up_grad = nn(n2t[...], hid_grad).astype(BF16)
        dn_grad = nn(olt[...], active).astype(BF16)

        @pl.when(k > 0)
        def _():
            for stage in (1, 2):
                left(f_any(stage), gf_s.at[stage, home])

        @pl.when((k > 0) & (r - nblk < WIDE_FROM))
        def _():
            left(f_any(0), gf_s.at[0, home])

        fg[g, 0] = up_grad
        fg[g, 1] = dn_grad

        @pl.when(r == 3 * nblk - 1)
        def _():
            for m in range(n_far):
                zf(1 + m % (parts - 1), m // (parts - 1)).wait_send()

        @pl.when(r >= SLOTS_C)
        def _():
            pl.semaphore_wait(credit, 1)

        slot = odd(r, n_all)
        rf(0, r, slot).start()

        @pl.when(r > 0)
        def _():
            rf_core(r - 1, 1 - slot)

        return advance("r", r, carry)

    lax.fori_loop(0, n_all, ffn, begin("r"))
    rf_core(n_all - 1, (n_all - 1) % SLOTS_C)

    middle = mid[...]
    ngs[...] = (middle + (acc0[...] + bdn_ref[...][None, :])).astype(BF16)
    lo_copy = pltpu.make_async_copy(ngs, lo_ref, loc_sem.at[2 * nblk])
    lo_copy.start()
    unit, scale_inv = unit_of(middle)
    got = acc1[...]
    early[0:1, :] = jnp.sum(got * unit, axis=0, keepdims=True)
    early[1:2, :] = jnp.sum(got, axis=0, keepdims=True)
    middle_part = norm_back(got, unit, scale_inv, g2_ref[...][None, :])
    reload = pltpu.make_async_copy(cot_ref, ol, loc_sem.at[0])
    reload.start()
    reload.wait()
    out_grad = ol[...].astype(F32) * row_weight
    middle_grad = out_grad + middle_part
    mid[...] = middle_grad
    branch_low = middle_grad.astype(BF16)
    early[2:3, :] = jnp.sum(branch_low.astype(F32), axis=0, keepdims=True)
    ol[...] = branch_low

    for k in range(1, parts):
        for a in range(2):
            za(k, a).wait_send()
            for stage in range(3):
                left(a_any(stage, a), ga_s.at[stage, a, far(k)])
    advance("ln")

    head_row = lax.broadcasted_iota(jnp.int32, (hw, 128), 0)
    head_col = (lax.broadcasted_iota(jnp.int32, (hw, 128), 1) - at2) * HD
    pick = jnp.where((head_row >= head_col) & (head_row < head_col + HD), 1.0, 0.0).astype(BF16)

    def out_back(k, carry):
        s = far(k)
        mixed = mx[s, :, 0:hw]
        mixed_grad = nt(ol[...], aw[s, qkvw : 4 * hw, :]).astype(BF16)
        dmx[s, :, 0:hw] = mixed_grad
        prod = mixed_grad.astype(F32) * mixed.astype(F32)
        coarse = prod.astype(BF16)
        fine = (prod - coarse.astype(F32)).astype(BF16)
        delta = nn(coarse, pick) + nn(fine, pick)
        stat[s] = jnp.where((lane_n >= at2) & (lane_n < at2 + heads), delta, stat[s])
        aw[s, qkvw : 4 * hw, :] = nn(mixed.T, ol[...]).astype(BF16)
        return advance("k", k, carry)

    lax.fori_loop(0, parts, out_back, begin("k"))

    def p_in(s, h, half, buf):
        return pltpu.make_async_copy(
            ph_ref.at[s * heads + h, half], pst.at[buf, h], ps_sem.at[buf, h]
        )

    def fetch(it):
        for h in range(heads):
            p_in(group_of(it), h, 1 - quotient(it, parts, 2 * parts), odd(it, 2 * parts)).start()

    def att_group(it, half):
        s = group_of(it)
        base = half * share
        buf = odd(it, 2 * parts)

        @pl.when(it + 1 < 2 * parts)
        def _():
            fetch(it + 1)

        for h in range(heads):
            p_in(s, h, half, buf).wait()
        known = stat[s]
        wanted = known if half == 0 else pltpu.roll(known, 96, 1)
        delta = -(pltpu.roll(known, 64, 1) * wanted)
        coarse = delta.astype(BF16).astype(F32)
        aux = jnp.where((lane_n >= at0) & (lane_n < at0 + heads), coarse, 0.0)
        aux = jnp.where(
            (lane_n >= at0 + 8) & (lane_n < at0 + 8 + heads), pltpu.roll(delta - coarse, 8, 1), aux
        )
        scaled = dmx[s].astype(F32) * spread(wanted, at0)
        dg = jnp.concatenate(
            [scaled[:, 0:128], jnp.where(lane_n < at0, scaled[:, 128:256], aux)], axis=1
        ).astype(BF16)
        qg = qb[s]
        kg = kb[s, base : base + share]
        vg = vb[s, base : base + share]
        qt = qg[:, 0:hw].T
        dt = dg[:, 0:hw].T
        dq = jnp.zeros((share, 2 * 128), F32)
        dks = []
        dvs = []
        for h in range(heads):
            head = head_lanes(h)
            aux_h = (lane_w == hw + h) | (lane_w == hw + 8 + h)
            dm = jnp.where(head | aux_h, dg, jnp.zeros_like(dg))
            prob_grad = nt(dm, vg)
            probs = pst[buf, h]
            score_grad = (probs.astype(F32) * prob_grad).astype(BF16)
            dq = jnp.where(head, nn(score_grad, kg), dq)
            dks.append(nn(qt[HD * h : HD * (h + 1)], score_grad))
            dvs.append(nn(dt[HD * h : HD * (h + 1)], probs))
        dqt = (dq[:, 0:hw] * factor).T
        dkt = (jnp.concatenate(dks, axis=0) * math.log(2.0)).astype(BF16)
        dvt = jnp.concatenate(dvs, axis=0).astype(BF16)
        return s, dqt, dkt, dvt

    acc0[...] = jnp.zeros_like(acc0)
    acc1[...] = jnp.zeros_like(acc1)
    dmx_pad = jnp.zeros((share, 2 * 128 - hw), BF16)
    for s in range(parts):
        dmx[s, :, hw : 2 * 128] = dmx_pad
    fetch(0)

    def row_sums(values):
        return jnp.sum(values.astype(F32), axis=0, keepdims=True)

    def pair_half(it, carry):
        s, dqt, dkt, dvt = att_group(it, 1)
        uu[s, 0:hw, 0:share] = dqt.astype(BF16)
        uu[s, hw : 2 * hw, 0:share] = dkt
        uu[s, 2 * hw : qkvw, 0:share] = dvt
        back = uu[s, hw:qkvw, 0:share].T
        acc0[...] += nn(back, aw[s, hw:qkvw, :])
        late[pl.ds(2 * s + 1, 1), 0:hw] = row_sums(back[:, hw : 2 * hw])
        return advance("h", it, carry)

    lax.fori_loop(0, parts, pair_half, begin("h"))

    ng_copy = rcopy(ngs, ngr, ng_sem.at[0], ng_sem.at[1], (d, tp))
    pair_grad = acc0[...]
    lo_copy.wait()
    ngs[...] = pair_grad.astype(BF16)
    if NG_PLACE == 0:
        ng_copy.start()
    unit, _ = unit_of(xp[...].astype(F32))
    late[8:9, :] = jnp.sum(pair_grad * unit, axis=0, keepdims=True)
    late[9:10, :] = jnp.sum(pair_grad, axis=0, keepdims=True)

    stages = (dev_c, (dx, t), (dy, t))

    def vec(which, stage):
        buf, rx = (early, e_rx) if which == 0 else (late, l_rx)
        return rcopy(buf, rx.at[stage], sm_s.at[which, stage], sm_r.at[which, stage], stages[stage])

    def vec_far(which, k):
        rz = e_rz if which == 0 else l_rz
        return rcopy(
            rz.at[t], rz.at[t], sm_s.at[which, 2 + k], sm_r.at[which, 3 + t], (d, far(k))
        )

    def vec_next(which, stage):
        buf, rx = (early, e_rx) if which == 0 else (late, l_rx)
        vec(which, stage).wait_recv()
        vec(which, stage).wait_send()
        buf[...] = buf[...] + rx[stage]
        if stage < 2:
            vec(which, stage + 1).start()
        else:
            rz = e_rz if which == 0 else l_rz
            rz[t] = buf[...]
            for k in range(1, parts):
                vec_far(which, k).start()

    vec(0, 0).start()

    def own_half(it, carry):
        q = it - parts
        s, dqt, dkt, dvt = att_group(it, 0)
        dqt = (uu[s, 0:hw, 0:share].astype(F32) + dqt).astype(BF16)
        dd[0:hw, :] = dqt
        dd[hw : 2 * hw, :] = dkt
        dd[2 * hw : qkvw, :] = dvt
        back = dd[...].T
        acc1[...] += nn(back, aw[s, 0:qkvw, :])
        late[pl.ds(2 * s, 1), 0:hw] = row_sums(back[:, 0:hw])
        late[pl.ds(2 * s + 1, 1), 0:hw] = late[pl.ds(2 * s + 1, 1), 0:hw] + row_sums(
            back[:, 2 * hw : qkvw]
        )
        aw[s, 0:hw, :] = nn(dqt, xn[0:share, :]).astype(BF16)
        aw[s, hw:qkvw, :] = (
            nn(dd[hw:qkvw, :], xn[0:share, :]) + nn(uu[s, hw:qkvw, 0:share], xn[share:keys, :])
        ).astype(BF16)
        for a in range(2):
            ra(0, q, a).start()
        carry = advance("w", q, carry)
        if NG_PLACE > 0:

            @pl.when(q == NG_PLACE - 1)
            def _():
                ng_copy.start()

        for stage in range(3):

            @pl.when(q == stage)
            def _():
                vec_next(0, stage)

        return carry

    lax.fori_loop(parts, 2 * parts, own_half, begin("w"))

    own_grad = acc1[...]
    unit, scale_inv = unit_of(x_ref[...].astype(F32))
    late[8:9, :] = late[8:9, :] + jnp.sum(own_grad * unit, axis=0, keepdims=True)
    late[9:10, :] = late[9:10, :] + jnp.sum(own_grad, axis=0, keepdims=True)
    vec(1, 0).start()
    done = uu.at[0]
    xg_copy = pltpu.make_async_copy(mid, xg_ref, loc_sem.at[nblk])

    def aa(stage, a):
        _, _, first, second = route(t0 if a == 0 else 1 - t0)
        view = done.at[a_rows(stage, t0, a), a_lanes(a)]
        dev = (first, second, dev_c)[stage]
        return rcopy(view, view, aa_s.at[stage, a], aa_r.at[stage, a], dev)

    def att_final():
        for a in range(2):
            mine = a_rows(0, t0, a)
            low = CUTS[a][0]
            high = low + CUTS[a][1]
            total = aw[t, mine, low:high].astype(F32)
            for q in range(parts - 1):
                view = rz_a.at[q, :, a_lanes(a)]
                rcopy(view, view, ra_s.at[3, a, q], ra_r.at[3, a, q], (d, t)).wait_recv()
                total = total + rz_a[q, :, low:high].astype(F32)
            done[mine, low:high] = total.astype(BF16)
            aa(0, a).start()

    def att_round(stage):
        for a in range(2):
            aa(stage - 1, a).wait_recv()
            aa(stage, a).start()

    def rows_final():
        ng_copy.wait_recv()
        grad = own_grad + ngr[...].astype(F32)
        mid[...] = mid[...] + norm_back(grad, unit, scale_inv, gain1)
        xg_copy.start()

    vec_stage = 0
    for name, low, high in TAIL:
        if name == "v":
            vec_next(1, vec_stage)
            vec_stage += 1
        elif name == "aa0":
            att_final()
        elif name == "aa1":
            att_round(1)
        elif name == "aa2":
            att_round(2)
        elif name == "ng":
            rows_final()
        else:
            repeat(name, low, high)

    for j in range(nblk):
        af(2, j).wait_recv()
        f_out(j, 0).start()
        if j >= 2:
            f_out(j - 2, 1).wait()
        ol[(j % 2) * BLK : (j % 2 + 1) * BLK, :] = fg[t * nblk + j, 1].T
        f_out(j, 1).start()

    for which in range(2):
        rz = e_rz if which == 0 else l_rz
        for k in range(1, parts):
            s = far(k)
            rcopy(
                rz.at[s], rz.at[s], sm_s.at[which, 3], sm_r.at[which, 3 + s], (d, t)
            ).wait_recv()
    early[...] = ((e_rz[0] + e_rz[1]) + e_rz[2]) + e_rz[3]
    late[...] = ((l_rz[0] + l_rz[1]) + l_rz[2]) + l_rz[3]
    osm_ref[0:4, :] = early[0:4, :]
    osm_ref[4:6, :] = late[8:10, :]
    osm_ref[8:9, :] = late[pl.ds(2 * t, 1), :]
    osm_ref[9:10, :] = late[pl.ds(2 * t + 1, 1), :]
    for j in range(nblk):
        osm_ref[16 + j : 17 + j, :] = early[pl.ds(4 + t * nblk + j, 1), :]

    for k in range(1, parts):
        zb(k, 0).wait_send()
        zb(k, 1).wait_send()
        for which in range(2):
            vec_far(which, k).wait_send()
    x_copy.wait_send()
    ng_copy.wait_send()

    for j in range(nblk):
        for k in range(1, parts):
            left(f_any(1 if j < EARLY_FAR else 0), fz_s.at[(k - 1) * nblk + j])
    for r in range(n_all):
        if r < nblk or (r - nblk) // (parts - 1) >= EARLY_FAR:
            left(f_any(0), f1_s.at[r])

    def drain_all(r, carry):
        left(f_any(2), cf_s.at[r])
        left(f_any(1), f2_s.at[r])
        return carry

    lax.fori_loop(0, n_all, drain_all, 0)

    def drain_own(j, carry):
        for stage in range(3):
            left(f_any(stage), af_s.at[stage, j])
        return carry

    lax.fori_loop(0, nblk, drain_own, 0)
    for j in range(nblk):
        f_out(j, 0).wait()
    for j in range(nblk - 2, nblk):
        f_out(j, 1).wait()

    for q in range(parts):
        for a in range(2):
            for stage in range(3):
                left(a_any(2 - stage, a), ra_s.at[stage, a, q])
            if q < parts - 1:
                left(a_any(0, a), ra_s.at[3, a, q])
    for a in range(2):
        aa(2, a).wait_recv()
    oa_copy = pltpu.make_async_copy(done, oa_ref, loc_sem.at[nblk + 1])
    oa_copy.start()
    oa_copy.wait()
    xg_copy.wait()
    for stage in range(3):
        for a in range(2):
            aa(stage, a).wait_send()


def finish(
    lo,
    xg,
    up,
    dn,
    at,
    sm,
    lo_out,
    xg_out,
    up_out,
    dn_out,
    qkv_out,
    out_out,
    g2_out,
    s2_out,
    bo_out,
    bd_out,
    g1_out,
    s1_out,
    qv_out,
    bup_out,
    lo_b,
    xg_b,
    up_b,
    dn_b,
    at_b,
    up_f,
    dn_f,
    at_f,
    in_sem,
    out_sem,
):
    hw = out_out.shape[0]
    qkvw = qkv_out.shape[0]
    jobs = []
    for n, (src, mid_b, wide, dst) in enumerate(
        ((up, up_b, up_f, up_out), (dn, dn_b, dn_f, dn_out), (at, at_b, at_f, None))
    ):
        size = src.shape[0] // CHUNKS
        for i in range(CHUNKS):
            part = pl.ds(i * size, size)
            if dst is not None:
                to = dst.at[part, :]
            elif (i + 1) * size <= qkvw:
                to = qkv_out.at[part, :]
            else:
                to = out_out.at[pl.ds(i * size - qkvw, size), :]
            jobs.append((src.at[part, :], mid_b.at[part, :], wide.at[part, :], to))
    jobs.append((xg, xg_b, None, xg_out))
    jobs.append((lo, lo_b, None, lo_out))
    ins = [
        pltpu.make_async_copy(job[0], job[1], in_sem.at[i]) for i, job in enumerate(jobs)
    ]
    for cp in ins:
        cp.start()
    for i, ref in enumerate((g2_out, s2_out, bo_out, bd_out, g1_out, s1_out)):
        ref[...] = sm[i]
    qv_out[...] = sm[8:10, 0:hw]
    for j in range(bup_out.shape[0] // BLK):
        bup_out[j * BLK : (j + 1) * BLK] = sm[16 + j, 0:BLK]
    outs = []
    for i, (_, got, wide, dst) in enumerate(jobs):
        ins[i].wait()
        if wide is not None:
            wide[...] = got[...].astype(F32)
        outs.append(pltpu.make_async_copy(got if wide is None else wide, dst, out_sem.at[i]))
        outs[-1].start()
    for cp in outs:
        cp.wait()


def local(
    x_in,
    cotangent,
    lengths,
    bucket_ids,
    bucket_weights,
    ln1_gain,
    ln1_bias,
    w_qkv,
    qv_bias,
    w_out,
    b_out,
    ln2_gain,
    ln2_bias,
    w_up,
    b_up,
    w_down,
    b_down,
):
    share, width = x_in.shape
    hw = w_qkv.shape[2]
    heads = hw // HD
    parts = 4
    fw = w_up.shape[1]
    nblk = fw // BLK
    piece = width // GROUP
    keys = 2 * share
    n_all = parts * nblk
    n_far = n_all - nblk
    vm = pl.BlockSpec(memory_space=pltpu.VMEM)
    sm = pl.BlockSpec(memory_space=pltpu.SMEM)
    hbm = pl.BlockSpec(memory_space=pl.ANY)
    dma = pltpu.SemaphoreType.DMA
    scratch = [
        pltpu.VMEM((n_all + nblk, 2, width, BLK), BF16),
        pltpu.VMEM((parts, width, 4 * hw), BF16),
        pltpu.VMEM((SLOTS_C, 2, 4 * piece, BLK), BF16),
        pltpu.VMEM((n_all, 2, 2 * piece, BLK), BF16),
        pltpu.VMEM((n_all, 2, piece, BLK), BF16),
        pltpu.VMEM((n_far, 2, 2 * piece, BLK), BF16),
        pltpu.VMEM((parts, 4 * piece, 4 * hw), BF16),
        pltpu.VMEM((parts, 2 * piece, 4 * hw), BF16),
        pltpu.VMEM((parts, piece, 4 * hw), BF16),
        pltpu.VMEM((parts - 1, piece, 4 * hw), BF16),
        pltpu.VMEM((keys, width), BF16),
        pltpu.VMEM((share, width), BF16),
        pltpu.VMEM((parts, share, 256), BF16),
        pltpu.VMEM((parts, keys, 256), BF16),
        pltpu.VMEM((parts, keys, 256), BF16),
        pltpu.VMEM((parts, share, 256), BF16),
        pltpu.VMEM((parts, share, 256), BF16),
        pltpu.VMEM((parts, share, 128), F32),
        pltpu.VMEM((3 * hw, share), BF16),
        pltpu.VMEM((2, heads, share, share), BF16),
        pltpu.VMEM((share, width), F32),
        pltpu.VMEM((share, width), F32),
        pltpu.VMEM((share, width), F32),
        pltpu.VMEM((parts, width, width), BF16),
        pltpu.VMEM((share, width), BF16),
        pltpu.VMEM((width, share), BF16),
        pltpu.VMEM((share, width), BF16),
        pltpu.VMEM((share, width), BF16),
        pltpu.VMEM((parts, 1, fw), F32),
        pltpu.VMEM((parts, 2, hw), F32),
        pltpu.VMEM((24, width), F32),
        pltpu.VMEM((16, width), F32),
        pltpu.VMEM((3, 24, width), F32),
        pltpu.VMEM((parts, 24, width), F32),
        pltpu.VMEM((3, 16, width), F32),
        pltpu.VMEM((parts, 16, width), F32),
        dma((2 * nblk + 5,)),
        dma((2, heads)),
        dma((2, 3)),
        dma((2, parts)),
        dma((2,)),
        dma((6,)),
        dma((2, parts)),
        dma((3, 2, parts)),
        dma((3, 2, parts)),
        dma((n_far,)),
        dma((n_all,)),
        dma((3, n_all)),
        dma((3, n_all)),
        dma((n_all,)),
        dma((n_all,)),
        dma((n_all,)),
        dma((n_all,)),
        dma((n_all,)),
        dma((n_all,)),
        dma((n_far,)),
        dma((n_far,)),
        dma((3, nblk)),
        dma((3, nblk)),
        dma((4, 2, parts)),
        dma((4, 2, parts)),
        dma((3, 2)),
        dma((3, 2)),
        dma((2, 7)),
        dma((2, 7)),
        dma((2,)),
        pltpu.SemaphoreType.REGULAR,
    ]
    layer_out, x_grad, up, down, att, small, _ = pl.pallas_call(
        kernel,
        out_shape=[
            jax.ShapeDtypeStruct((share, width), BF16),
            jax.ShapeDtypeStruct((share, width), F32),
            jax.ShapeDtypeStruct((width, fw), BF16),
            jax.ShapeDtypeStruct((fw, width), BF16),
            jax.ShapeDtypeStruct((width, width), BF16),
            jax.ShapeDtypeStruct((24, width), F32),
            jax.ShapeDtypeStruct((parts * heads, 2, share, share), BF16),
        ],
        in_specs=[vm, hbm, sm, sm, sm, vm, vm, hbm, vm, hbm, vm, vm, vm, hbm, vm, hbm, vm],
        out_specs=[hbm, hbm, hbm, hbm, hbm, vm, hbm],
        scratch_shapes=scratch,
        compiler_params=pltpu.CompilerParams(
            collective_id=0, has_side_effects=True, vmem_limit_bytes=67043328
        ),
    )(
        x_in,
        cotangent,
        lengths,
        bucket_ids,
        bucket_weights,
        ln1_gain,
        ln1_bias,
        w_qkv.transpose(0, 2, 1),
        qv_bias,
        w_out,
        b_out,
        ln2_gain,
        ln2_bias,
        w_up,
        b_up,
        w_down,
        b_down,
    )
    dp = lax.axis_size("dp")
    if dp > GROUP:
        groups = [[g + GROUP * i for i in range(dp // GROUP)] for g in range(GROUP)]
        sums = lax.psum(
            tuple(g.astype(F32) for g in (up, down, att, small)), "dp", axis_index_groups=groups
        )
        up, down, att = (g.astype(BF16) for g in sums[:3])
        small = sums[3]
    flat = jax.ShapeDtypeStruct((width,), F32)
    outs = pl.pallas_call(
        finish,
        out_shape=[
            jax.ShapeDtypeStruct((share, width), BF16),
            jax.ShapeDtypeStruct((share, width), F32),
            jax.ShapeDtypeStruct((width, fw), F32),
            jax.ShapeDtypeStruct((fw, width), F32),
            jax.ShapeDtypeStruct((3 * hw, width), F32),
            jax.ShapeDtypeStruct((hw, width), F32),
            flat,
            flat,
            flat,
            flat,
            flat,
            flat,
            jax.ShapeDtypeStruct((2, hw), F32),
            jax.ShapeDtypeStruct((fw,), F32),
        ],
        in_specs=[hbm] * 5 + [vm],
        out_specs=[hbm] * 6 + [vm] * 8,
        scratch_shapes=[
            pltpu.VMEM((share, width), BF16),
            pltpu.VMEM((share, width), F32),
            pltpu.VMEM((width, fw), BF16),
            pltpu.VMEM((fw, width), BF16),
            pltpu.VMEM((width, width), BF16),
            pltpu.VMEM((width, fw), F32),
            pltpu.VMEM((fw, width), F32),
            pltpu.VMEM((width, width), F32),
            dma((3 * CHUNKS + 2,)),
            dma((3 * CHUNKS + 2,)),
        ],
    )(layer_out, x_grad, up, down, att, small)
    layer_out, x_grad, g_up, g_down, g_qkv, g_out, g2, s2, bo, bd, g1, s1, g_qv, g_bup = outs
    return (
        layer_out,
        x_grad,
        g1,
        s1,
        g_qkv.reshape(3, hw, width).transpose(0, 2, 1),
        g_qv,
        g_out,
        bo,
        g2,
        s2,
        g_up,
        g_bup,
        g_down,
        bd,
    )


def solution(mesh):
    return jax.shard_map(
        local,
        mesh=mesh,
        in_specs=(
            P(("dp", "tensor"), None),
            P(("dp", "tensor"), None),
            P("dp", None),
            P("dp"),
            P(),
            P(),
            P(),
            P(None, None, "tensor"),
            P(None, "tensor"),
            P("tensor", None),
            P(),
            P(),
            P(),
            P(None, "tensor"),
            P("tensor"),
            P("tensor", None),
            P(),
        ),
        out_specs=(
            P(("dp", "tensor"), None),
            P(("dp", "tensor"), None),
            P(),
            P(),
            P(None, None, "tensor"),
            P(None, "tensor"),
            P("tensor", None),
            P(),
            P(),
            P(),
            P(None, "tensor"),
            P("tensor"),
            P("tensor", None),
            P(),
        ),
        check_vma=False,
    )
```

```python
import functools
import math

import jax
import jax.numpy as jnp
from jax import lax
from jax.experimental import pallas as pl
from jax.experimental.pallas import tpu as pltpu
from jax.sharding import PartitionSpec as P

HD = 32
BUCKET = 256
EPSILON = 1e-05
GROUP = 8
BLK = 256
BIG = 1e30
F32 = jnp.float32
BF16 = jnp.bfloat16
MESH = pl.DeviceIdType.MESH
RSQRT2 = 1.0 / math.sqrt(2.0)
RSQRT2PI = 1.0 / math.sqrt(2.0 * math.pi)
SLOTS_C = 2
X_PLACE = 0
WIDE_FROM = 15
NG_PLACE = 1
EARLY_FAR = 3
CUTS = ((0, 256), (256, 384))
CHUNKS = 4
PLAN = {
    "p0": (
        ("a0", (0, 1)),
        ("a1", (0, 1)),
    ),
    "p1": (
        ("a0", (1, 3)),
        ("a2", (0, 1)),
    ),
    "p2": (
        ("a1", (1, 3)),
        ("a2", (1, 3)),
    ),
    "pj": (
    ),
    "o": (
    ),
    "q": (
        ("g0", (0, 0, 11, 14, 15)),
        ("g1", (0, 0, 0, 0, 8)),
    ),
    "mid": (
        ("g1", (8, 10)),
    ),
    "r": (
        ("g1", (10, 11, 15, 15, 15, 15, 15, 15, 15, 15, 15, 15, 15, 15, 15, 15, 15, 15, 15, 15, 15)),
        ("g2", (0, 0, 3, 3, 5, 8, 8, 9, 9, 11, 13, 15, 15, 15, 15, 15, 15, 15, 15, 15, 15)),
        ("rf", (0, 0, 0, 0, 0, 0, 0, 0, 0, 0, 0, 0, 0, 0, 0, 0, 0, 4, 4, 5, 5)),
        ("r1", (0, 0, 0, 0, 0, 0, 0, 0, 0, 0, 0, 0, 0, 2, 2, 3, 4, 4, 5, 5, 7)),
        ("r2", (0, 0, 0, 0, 0, 0, 0, 1, 2, 3, 4, 5, 6, 7, 8, 8, 10, 11, 12, 13, 14)),
    ),
    "ln": (
        ("rf", (5, 7)),
        ("r2", (14, 16)),
    ),
    "k": (
        ("rf", (7, 7, 8, 8, 9)),
        ("r1", (7, 9, 9, 9, 9)),
        ("r2", (16, 16, 16, 20, 20)),
    ),
    "h": (
        ("rf", (9, 9, 9, 11, 17)),
        ("r1", (9, 14, 16, 17, 17)),
        ("f0", (0, 0, 0, 0, 2)),
    ),
    "w": (
        ("rf", (17, 17, 19, 19, 20)),
        ("r1", (17, 20, 20, 20, 20)),
        ("b3", (0, 0, 0, 0, 2)),
        ("b2", (0, 0, 0, 2, 3)),
        ("b1", (0, 0, 2, 3, 4)),
        ("f0", (2, 2, 3, 3, 5)),
        ("f1", (0, 1, 1, 3, 3)),
        ("f2", (0, 0, 0, 0, 3)),
    ),
}
TAIL = (
    ("b2", 3, 4),
    ("v", 0, 0),
    ("f1", 3, 5),
    ("b3", 2, 4),
    ("v", 0, 0),
    ("aa0", 0, 0),
    ("v", 0, 0),
    ("aa1", 0, 0),
    ("f2", 3, 5),
    ("ng", 0, 0),
    ("aa2", 0, 0),
)


def nn(a, b):
    return lax.dot_general(a, b, (((1,), (0,)), ((), ())), preferred_element_type=F32)


def nt(a, b):
    return lax.dot_general(a, b, (((1,), (1,)), ((), ())), preferred_element_type=F32)


def unit_of(values):
    centre = values - jnp.mean(values, axis=-1, keepdims=True)
    scale_inv = lax.rsqrt(jnp.mean(centre * centre, axis=-1, keepdims=True) + EPSILON)
    return centre * scale_inv, scale_inv


def norm_back(grad, unit, scale_inv, gain):
    scaled = grad * gain
    return scale_inv * (
        scaled
        - jnp.mean(scaled, axis=-1, keepdims=True)
        - unit * jnp.mean(scaled * unit, axis=-1, keepdims=True)
    )


def lanes(shape):
    return lax.broadcasted_iota(jnp.int32, shape, 1)


def kernel(
    x_ref,
    cot_ref,
    len_ref,
    bid_ref,
    bw_ref,
    g1_ref,
    s1_ref,
    wqkv_ref,
    qvb_ref,
    wout_ref,
    bout_ref,
    g2_ref,
    s2_ref,
    wup_ref,
    bup_ref,
    wdn_ref,
    bdn_ref,
    lo_ref,
    xg_ref,
    ou_ref,
    od_ref,
    oa_ref,
    osm_ref,
    ph_ref,
    fg,
    aw,
    rc_f,
    r2_f,
    r1_f,
    rz_f,
    rc_a,
    r2_a,
    r1_a,
    rz_a,
    xn,
    xp,
    qb,
    kb,
    vb,
    mx,
    dmx,
    stat,
    dd,
    pst,
    mid,
    acc0,
    acc1,
    uu,
    ol,
    olt,
    ngs,
    ngr,
    bupa,
    qvba,
    early,
    late,
    e_rx,
    e_rz,
    l_rx,
    l_rz,
    loc_sem,
    ps_sem,
    za_s,
    za_r,
    zx_sem,
    zb_s,
    zb_r,
    ga_s,
    ga_r,
    zf_s,
    zf_r,
    gf_s,
    gf_r,
    cf_s,
    cf_r,
    f2_s,
    f2_r,
    f1_s,
    f1_r,
    fz_s,
    fz_r,
    af_s,
    af_r,
    ra_s,
    ra_r,
    aa_s,
    aa_r,
    sm_s,
    sm_r,
    ng_sem,
    credit,
):
    share, width = x_ref.shape
    hw = wqkv_ref.shape[1]
    heads = hw // HD
    qkvw = 3 * hw
    parts = 4
    nblk = wup_ref.shape[1] // BLK
    piece = width // GROUP
    keys = 2 * share
    factor = HD ** (-0.5)
    q_scale = factor * math.log2(math.e)

    d = lax.axis_index("dp")
    t = lax.axis_index("tensor")
    c = d % 2
    bx = (d // 2) % 2
    by = (d // 4) % 2
    dev_c = (d + 1 - 2 * c, t)
    dx = d + 2 - 4 * bx
    dy = d + 4 - 8 * by
    t0 = t % 2
    t1 = t // 2
    tp = t + 1 - 2 * t0

    def quotient(n, step, limit):
        if isinstance(n, int):
            return n // step
        return sum(jnp.where(n >= i, 1, 0) for i in range(step, limit, step))

    def odd(n, limit):
        return n - 2 * quotient(n, 2, limit)

    def differ(a, b):
        return a + b - 2 * a * b

    def far_bits(k):
        high = quotient(k, 2, parts)
        low = differ(t0, k - 2 * high)
        return low + 2 * differ(t1, high), low

    def far(k):
        return far_bits(k)[0]

    def route(par):
        low = bx + par * (by - bx)
        high = by + par * (bx - by)
        first = (dx + par * (dy - dx), t)
        second = (dy + par * (dx - dy), t)
        return low, high, first, second

    def rcopy(src, dst, ssem, rsem, dev):
        return pltpu.make_async_remote_copy(
            src_ref=src, dst_ref=dst, send_sem=ssem, recv_sem=rsem, device_id=dev, device_id_type=MESH
        )

    def arrived(view, sem):
        rcopy(view, view, sem, sem, (d, t)).wait_recv()

    def left(view, sem):
        rcopy(view, view, sem, sem, (d, t)).wait_send()

    def rows(start, size):
        return pl.ds(pl.multiple_of(start, 16), size)

    barrier = pltpu.get_barrier_semaphore()
    for dev in (dev_c, (dx, t), (dy, t), (d, far(1)), (d, far(2)), (d, far(3))):
        pl.semaphore_signal(barrier, inc=1, device_id=dev, device_id_type=MESH)

    def up_load(j):
        return pltpu.make_async_copy(
            wup_ref.at[:, pl.ds(j * BLK, BLK)], fg.at[t * nblk + j, 0], loc_sem.at[j]
        )

    def dn_load(j):
        return pltpu.make_async_copy(
            wdn_ref.at[pl.ds(j * BLK, BLK), :],
            uu.at[j // 2, pl.ds((j % 2) * BLK, BLK), :],
            loc_sem.at[nblk + j],
        )

    cot_load = pltpu.make_async_copy(cot_ref, ol, loc_sem.at[2 * nblk])

    a_loads = [
        pltpu.make_async_copy(
            wqkv_ref.at[i], aw.at[t, pl.ds(i * hw, hw), :], loc_sem.at[2 * nblk + 1 + i]
        )
        for i in range(3)
    ]
    a_loads.append(
        pltpu.make_async_copy(
            wout_ref, aw.at[t, pl.ds(qkvw, hw), :], loc_sem.at[2 * nblk + 4]
        )
    )
    for cp in a_loads:
        cp.start()
    for j in range(nblk):
        dn_load(j).start()
        up_load(j).start()
    cot_load.start()
    bupa[t] = bup_ref[...][None, :]
    qvba[t] = qvb_ref[...]

    pl.semaphore_wait(barrier, 6)

    def a_rows(stage, parity, a):
        low, high, _, _ = route(parity if a == 0 else 1 - parity)
        if stage == 0:
            return rows((c * 4 + high * 2 + low) * piece, piece)
        if stage == 1:
            return rows((c * 4 + high * 2) * piece, 2 * piece)
        return rows(c * 4 * piece, 4 * piece)

    def a_lanes(a):
        return pl.ds(CUTS[a][0], CUTS[a][1])

    def a_any(stage, a):
        return aw.at[0, 0 : (piece, 2 * piece, 4 * piece)[stage], a_lanes(a)]

    def za(k, a):
        view = aw.at[t, a_rows(0, t0, a), a_lanes(a)]
        return rcopy(view, view, za_s.at[a, k - 1], za_r.at[a, t], (d, far(k)))

    def zb(k, which):
        dst = (bupa if which == 0 else qvba).at[t]
        return rcopy(dst, dst, zb_s.at[2 * (k - 1) + which], zb_r.at[which, t], (d, far(k)))

    def zb_wait(s, which):
        dst = (bupa if which == 0 else qvba).at[s]
        rcopy(dst, dst, zb_s.at[0], zb_r.at[which, s], (d, t)).wait_recv()

    x_copy = rcopy(x_ref, xp, zx_sem.at[0], zx_sem.at[1], (d, tp))

    for cp in a_loads:
        cp.wait()
    for k in range(1, parts):
        for a in range(2):
            za(k, a).start()
        zb(k, 1).start()
    for k in range(1, parts):
        zb(k, 0).start()

    def ga(stage, s, parity, a):
        _, _, first, second = route(parity if a == 0 else 1 - parity)
        view = aw.at[s, a_rows(stage, parity, a), a_lanes(a)]
        dev = (first, second, dev_c)[stage]
        return rcopy(view, view, ga_s.at[stage, a, s], ga_r.at[stage, a, s], dev)

    def step_a(stage, i):
        s, parity = far_bits(i + 1)
        for a in range(2):
            if stage == 0:
                arrived(a_any(0, a), za_r.at[a, s])
            else:
                arrived(a_any(stage - 1, a), ga_r.at[stage - 1, a, s])
            ga(stage, s, parity, a).start()

    n_far = (parts - 1) * nblk

    def far_block(m):
        j = quotient(m, parts - 1, n_far)
        s, parity = far_bits(1 + m - (parts - 1) * j)
        return s, j, s * nblk + j, differ(parity, odd(j, nblk))

    def own_parity(j):
        return differ(t0, odd(j, nblk))

    def gf(stage, m):
        _, _, b, par = far_block(m)
        low, high, first, second = route(par)
        if stage == 0:
            view, dev = fg.at[b, :, rows((c * 4 + high * 2 + low) * piece, piece), :], first
        elif stage == 1:
            view, dev = fg.at[b, :, rows((c * 4 + high * 2) * piece, 2 * piece), :], second
        else:
            view, dev = fg.at[b, :, rows(c * 4 * piece, 4 * piece), :], dev_c
        return rcopy(view, view, gf_s.at[stage, b], gf_r.at[stage, b], dev)

    def f_any(stage):
        return fg.at[0, :, 0 : (piece, 2 * piece, 4 * piece)[stage], :]

    def step_g(stage, m):
        b = far_block(m)[2]
        if WIDE_FROM >= n_far:
            if stage == 0:
                arrived(f_any(0), zf_r.at[b])
            else:
                arrived(f_any(stage - 1), gf_r.at[stage - 1, b])
            gf(stage, m).start()
            return
        if stage == 0:

            @pl.when(m < WIDE_FROM)
            def _():
                arrived(f_any(0), zf_r.at[b])
                gf(0, m).start()

            return
        if stage == 1:

            @pl.when(m < WIDE_FROM)
            def _():
                arrived(f_any(0), gf_r.at[0, b])

            @pl.when(m >= WIDE_FROM)
            def _():
                arrived(f_any(1), zf_r.at[b])

        else:
            arrived(f_any(1), gf_r.at[1, b])
        gf(stage, m).start()

    n_all = parts * nblk

    def block(r):
        own = jnp.where(r < nblk, 1, 0)
        m = r - nblk
        turn_j = quotient(m, parts - 1, n_far)
        k = (1 - own) * (1 + m - (parts - 1) * turn_j)
        j = own * r + (1 - own) * turn_j
        s, parity = far_bits(k)
        home = s * nblk + j
        return k, j, s, home, home + own * (n_all + j - home), differ(parity, odd(j, nblk))

    def rf(stage, r, slot=None):
        k, j, s, _, g, par = block(r)
        low, high, first, second = route(par)
        if stage == 0:
            return rcopy(
                fg.at[g, :, rows((1 - c) * 4 * piece, 4 * piece), :],
                rc_f.at[slot],
                cf_s.at[r],
                cf_r.at[r],
                dev_c,
            )
        if stage == 1:
            return rcopy(
                fg.at[g, :, rows((c * 4 + (1 - high) * 2) * piece, 2 * piece), :],
                r2_f.at[r],
                f2_s.at[r],
                f2_r.at[r],
                second,
            )
        if stage == 2:
            return rcopy(
                fg.at[g, :, rows((c * 4 + high * 2 + 1 - low) * piece, piece), :],
                r1_f.at[r],
                f1_s.at[r],
                f1_r.at[r],
                first,
            )
        z = jnp.maximum((k - 1) * nblk + j, 0)
        if stage == 4:
            return rcopy(
                fg.at[g, :, rows((c * 4 + high * 2) * piece, 2 * piece), :],
                rz_f.at[z],
                fz_s.at[z],
                fz_r.at[z],
                (d, s),
            )
        return rcopy(
            fg.at[g, :, rows((c * 4 + high * 2 + low) * piece, piece), :],
            rz_f.at[z, :, 0:piece, :],
            fz_s.at[z],
            fz_r.at[z],
            (d, s),
        )

    def add_rows(ref, got):
        ref[...] = (ref[...].astype(F32) + got[...].astype(F32)).astype(BF16)

    def rf_core(r, slot):
        g = block(r)[4]
        arrived(rc_f.at[slot], cf_r.at[r])
        add_rows(fg.at[g, :, rows(c * 4 * piece, 4 * piece), :], rc_f.at[slot])

        @pl.when(r < n_all - SLOTS_C)
        def _():
            pl.semaphore_signal(credit, inc=1, device_id=dev_c, device_id_type=MESH)

    def turn(i):
        return i + nblk - n_all * jnp.where(i >= n_all - nblk, 1, 0)

    def rf_first(r):
        _, j, _, _, g, par = block(r)
        _, high, _, _ = route(par)
        both = fg.at[g, :, rows((c * 4 + high * 2) * piece, 2 * piece), :]
        arrived(r2_f.at[r], f2_r.at[r])
        add_rows(both, r2_f.at[r])

        @pl.when((j < EARLY_FAR) & (r >= nblk))
        def _():
            rf(4, r).start()

        @pl.when((j < EARLY_FAR) & (r < nblk))
        def _():
            total = both[...].astype(F32)
            for k in range(1, parts):
                z = (k - 1) * nblk + j
                arrived(rz_f.at[z], fz_r.at[z])
                total = total + rz_f[z].astype(F32)
            both[...] = total.astype(BF16)

        @pl.when((j >= EARLY_FAR) | (r < nblk))
        def _():
            rf(2, r).start()

    def rf_far(r):
        _, j, _, _, g, par = block(r)
        low, high, _, _ = route(par)

        @pl.when((j >= EARLY_FAR) | (r < nblk))
        def _():
            arrived(r1_f.at[r], f1_r.at[r])
            add_rows(fg.at[g, :, rows((c * 4 + high * 2 + low) * piece, piece), :], r1_f.at[r])

        @pl.when((j >= EARLY_FAR) & (r >= nblk))
        def _():
            rf(3, r).start()

    def af(stage, j):
        low, high, first, second = route(own_parity(j))
        b = t * nblk + j
        if stage == 0:
            view, dev = fg.at[b, :, rows((c * 4 + high * 2 + low) * piece, piece), :], first
        elif stage == 1:
            view, dev = fg.at[b, :, rows((c * 4 + high * 2) * piece, 2 * piece), :], second
        else:
            view, dev = fg.at[b, :, rows(c * 4 * piece, 4 * piece), :], dev_c
        return rcopy(view, view, af_s.at[stage, j], af_r.at[stage, j], dev)

    def f_final(j):
        low, high, _, _ = route(own_parity(j))
        mine = rows((c * 4 + high * 2 + low) * piece, piece)

        @pl.when(j < EARLY_FAR)
        def _():
            fg[t * nblk + j, :, mine, :] = fg[n_all + j, :, mine, :]

        @pl.when(j >= EARLY_FAR)
        def _():
            total = fg[n_all + j, :, mine, :].astype(F32)
            for k in range(1, parts):
                z = (k - 1) * nblk + j
                arrived(rz_f.at[z, :, 0:piece, :], fz_r.at[z])
                total = total + rz_f[z, :, 0:piece, :].astype(F32)
            fg[t * nblk + j, :, mine, :] = total.astype(BF16)

        af(0, j).start()

    def f_out(j, which):
        if which == 0:
            return pltpu.make_async_copy(
                fg.at[t * nblk + j, 0], ou_ref.at[:, pl.ds(j * BLK, BLK)], loc_sem.at[j]
            )
        return pltpu.make_async_copy(
            ol.at[pl.ds((j % 2) * BLK, BLK), :],
            od_ref.at[pl.ds(j * BLK, BLK), :],
            loc_sem.at[nblk + 2 + j % 2],
        )

    def f_second(j):
        arrived(f_any(0), af_r.at[0, j])
        af(1, j).start()

    def f_third(j):
        arrived(f_any(1), af_r.at[1, j])
        af(2, j).start()

    def group_bits(it):
        n = it + 1
        return far_bits(n - parts * quotient(n, parts, 2 * parts + 1))

    def group_of(it):
        return group_bits(it)[0]

    def ra(stage, q, a):
        s, parity = group_bits(q)
        low, high, first, second = route(parity if a == 0 else 1 - parity)
        if stage == 0:
            where, buf, dev = rows((1 - c) * 4 * piece, 4 * piece), rc_a, dev_c
        elif stage == 1:
            where, buf, dev = rows((c * 4 + (1 - high) * 2) * piece, 2 * piece), r2_a, second
        elif stage == 2:
            where, buf, dev = rows((c * 4 + high * 2 + 1 - low) * piece, piece), r1_a, first
        else:
            where, buf, dev = rows((c * 4 + high * 2 + low) * piece, piece), rz_a, (d, s)
            q = jnp.minimum(q, parts - 2)
        return rcopy(
            aw.at[s, where, a_lanes(a)],
            buf.at[q, :, a_lanes(a)],
            ra_s.at[stage, a, q],
            ra_r.at[stage, a, q],
            dev,
        )

    def step_b(stage, q):
        s, parity = group_bits(q)
        buf = (rc_a, r2_a, r1_a)[stage - 1]
        for a in range(2):
            view = buf.at[q, :, a_lanes(a)]
            arrived(view, ra_r.at[stage - 1, a, q])
            add_rows(aw.at[s, a_rows(3 - stage, parity, a), a_lanes(a)], view)
            if stage < 3:
                ra(stage, q, a).start()
            else:

                @pl.when(q < parts - 1)
                def _():
                    ra(3, q, a).start()

    steps = {
        "a0": lambda i: step_a(0, i),
        "a1": lambda i: step_a(1, i),
        "a2": lambda i: step_a(2, i),
        "g0": lambda i: step_g(0, i),
        "g1": lambda i: step_g(1, i),
        "g2": lambda i: step_g(2, i),
        "r2": lambda i: rf(1, turn(i)).start(),
        "r1": lambda i: rf_first(turn(i)),
        "rf": lambda i: rf_far(turn(i)),
        "b1": lambda i: step_b(1, i),
        "b2": lambda i: step_b(2, i),
        "b3": lambda i: step_b(3, i),
        "f0": lambda i: f_final(i),
        "f1": lambda i: f_second(i),
        "f2": lambda i: f_third(i),
    }

    def repeat(name, low, high):
        def one(i, carry):
            steps[name](i)
            return carry

        lax.fori_loop(low, high, one, 0)

    def advance(place, idx=None, reached=None):
        after = []
        for n, (name, counts) in enumerate(PLAN[place]):
            low = counts[0] if reached is None else reached[n]
            high = low
            if idx is None:
                high = counts[-1]
            else:
                for i in range(len(counts) - 1):
                    more = counts[i + 1] - counts[i]
                    if more:
                        high = high + jnp.where(idx == i, more, 0)
            repeat(name, low, high)
            after.append(high)
        return tuple(after)

    def begin(place):
        return tuple(jnp.int32(counts[0]) for _, counts in PLAN[place])

    gain1 = g1_ref[...][None, :]
    shift1 = s1_ref[...][None, :]
    unit, _ = unit_of(x_ref[...].astype(F32))
    xn[0:share, :] = (unit * gain1 + shift1).astype(BF16)
    advance("p0")

    def zf(k, j):
        low, high, _, _ = route(own_parity(j))
        where = rows((c * 4 + high * 2 + low) * piece, piece)
        if j * (parts - 1) + k - 1 >= WIDE_FROM:
            where = rows((c * 4 + high * 2) * piece, 2 * piece)
        view = fg.at[t * nblk + j, :, where, :]
        return rcopy(
            view, view, zf_s.at[(k - 1) * nblk + j], zf_r.at[t * nblk + j], (d, far(k))
        )

    for j in range(nblk):
        up_load(j).wait()
        dn_load(j).wait()
        fg[t * nblk + j, 1] = uu[j // 2, (j % 2) * BLK : (j % 2 + 1) * BLK, :].T
    for m in range((parts - 1) * nblk):
        if m == X_PLACE:
            x_copy.start()
        zf(1 + m % (parts - 1), m // (parts - 1)).start()

    advance("p1")

    bucket = bid_ref[0]
    span = jnp.where(bucket == 0, BUCKET, jnp.where(bucket == 1, 2 * BUCKET, 4 * BUCKET))
    weight = jnp.where(bucket == 0, bw_ref[0], jnp.where(bucket == 1, bw_ref[1], bw_ref[2]))

    def slot_info(base, shape):
        place = base + lax.broadcasted_iota(jnp.int32, shape, 0)
        item = jnp.zeros(shape, jnp.int32)
        for j in range(1, len_ref.shape[1]):
            item = item + jnp.where(place >= j * span, 1, 0)
        length = jnp.zeros(shape, jnp.int32)
        for j in range(len_ref.shape[1]):
            length = jnp.where(item == j, len_ref[0, j], length)
        return item, (place - item * span) < length

    wide = (share, 2 * 128)
    lane = lanes(wide)
    slots = len_ref.shape[1]
    in_aux = (lane >= hw) & (lane < hw + slots)
    one_aux = jnp.where(lane >= hw, 1.0, 0.0).astype(BF16)

    own_item, own_live = slot_info(t * share, wide)
    q_aux = jnp.where(in_aux & (own_item == lane - hw), 1.0, 0.0).astype(BF16)
    k_aux0 = jnp.where(in_aux & ~((own_item == lane - hw) & own_live), -BIG, 0.0).astype(BF16)
    pair_item, pair_live = slot_info(tp * share, wide)
    k_aux1 = jnp.where(in_aux & ~((pair_item == lane - hw) & pair_live), -BIG, 0.0).astype(BF16)
    for s in range(parts):
        qb[s] = q_aux
        kb[s, 0:share] = k_aux0
        kb[s, share:keys] = k_aux1
        vb[s, 0:share] = one_aux
        vb[s, share:keys] = one_aux
    _, live1 = slot_info(t * share, (share, 128))
    row_weight = jnp.where(live1, weight, 0.0)[:, 0:1]

    advance("p2")

    def project(s, half, own):
        base = half * share
        first = 0 if own else hw
        out = nt(xn[base : base + share, :], aw[s, first:qkvw, :])
        if own:
            qb[s, :, 0:hw] = ((out[:, 0:hw] + qvba[s, 0:1, :]) * q_scale).astype(BF16)
        at = hw - first
        kb[s, base : base + share, 0:hw] = out[:, at : at + hw].astype(BF16)
        vb[s, base : base + share, 0:hw] = (
            out[:, at + hw : at + 2 * hw] + qvba[s, 1:2, :]
        ).astype(BF16)

    lane_w = lanes((share, 2 * 128))
    lane_n = lanes((share, 128))

    def head_lanes(h):
        return (lane_w >= HD * h) & (lane_w < HD * (h + 1))

    def spread(values, at):
        out = jnp.zeros((share, 2 * 128), F32)
        for h in range(heads):
            out = jnp.where(head_lanes(h), values[:, at + h : at + h + 1], out)
        return out

    def p_out(s, h, half, buf):
        return pltpu.make_async_copy(
            pst.at[buf, h], ph_ref.at[s * heads + h, half], ps_sem.at[buf, h]
        )

    at0 = hw - 128
    at1 = at0 + 32
    at2 = at0 + 64

    def att_forward(k, half):
        s = far(k)
        base = half * share
        buf = odd(k, parts)
        if half == 1:
            for h in range(heads):
                p_out(s, h, half, buf).wait()
        else:

            @pl.when(k >= 2)
            def _():
                for h in range(heads):
                    p_out(s, h, half, buf).wait()

        qg = qb[s]
        kg = kb[s, base : base + share]
        vg = vb[s, base : base + share]
        out = jnp.zeros((share, 2 * 128), F32)
        tops = jnp.zeros((share, 128), F32)
        for h in range(heads):
            head = head_lanes(h)
            qm = jnp.where(head | (lane_w >= hw), qg, jnp.zeros_like(qg))
            scores = nt(qm, kg)
            top = jnp.max(scores, axis=1, keepdims=True)
            probs = jnp.exp2(scores - top).astype(BF16)
            pst[buf, h] = probs
            mixed = nn(probs, vg)
            out = jnp.where(head | (lane_w == hw + h), mixed, out)
            tops = jnp.where(lane_n == at0 + h, top, tops)
        for h in range(heads):
            p_out(s, h, half, buf).start()
        sums = jnp.where((lane_n >= at0) & (lane_n < at0 + heads), out[:, 128:256], 1.0)
        log_sum = tops + jnp.log2(sums)
        if half == 0:
            mx[s] = (out * spread(1.0 / sums, at0)).astype(BF16)
            stat[s] = jnp.where(lane_n < at1, tops, pltpu.roll(log_sum, 32, 1))
        else:
            before = stat[s]
            log_before = pltpu.roll(before, 96, 1)
            upper = jnp.maximum(log_sum, log_before)
            lower = jnp.minimum(log_sum, log_before)
            log_all = upper + jnp.log2(1.0 + jnp.exp2(lower - upper))
            part0 = jnp.exp2(log_before - log_all)
            part1 = jnp.exp2(log_sum - log_all) / sums
            mx[s] = (
                mx[s].astype(F32) * spread(part0, at0) + out * spread(part1, at0)
            ).astype(BF16)
            stat[s] = jnp.where(
                lane_n < at1,
                jnp.exp2(before - log_all),
                pltpu.roll(jnp.exp2(tops - log_all), 32, 1),
            )

    def own_keys(k, carry):
        s = far(k)

        @pl.when(k > 0)
        def _():
            zb_wait(s, 1)
            for a in range(2):
                arrived(a_any(2, a), ga_r.at[2, a, s])

        project(s, 0, True)

        @pl.when(k == 0)
        def _():
            advance("pj")

        att_forward(k, 0)
        return advance("o", k, carry)

    lax.fori_loop(0, parts, own_keys, begin("o"))

    x_copy.wait_recv()
    unit, _ = unit_of(xp[...].astype(F32))
    xn[share:keys, :] = (unit * gain1 + shift1).astype(BF16)

    def pair_keys(k, carry):
        project(far(k), 1, False)
        att_forward(k, 1)
        return advance("q", k, carry)

    lax.fori_loop(0, parts, pair_keys, begin("q"))
    for buf in range(2):
        for h in range(heads):
            p_out(0, h, 1, buf).wait()

    branch = jnp.zeros((share, width), F32)
    for s in range(parts):
        branch = branch + nn(mx[s, :, 0:hw], aw[s, qkvw : 4 * hw, :])
    middle = x_ref[...].astype(F32) + (branch + bout_ref[...][None, :])
    mid[...] = middle
    unit, _ = unit_of(middle)
    normed = (unit * g2_ref[...][None, :] + s2_ref[...][None, :]).astype(BF16)
    n2 = uu.at[0, 0:share, :]
    n2t = uu.at[1, :, 0:share]
    n2[...] = normed
    n2t[...] = normed.T
    cot_load.wait()
    low_grad = (ol[...].astype(F32) * row_weight).astype(BF16)
    early[...] = jnp.zeros_like(early)
    late[...] = jnp.zeros_like(late)
    early[3:4, :] = jnp.sum(low_grad.astype(F32), axis=0, keepdims=True)
    ol[...] = low_grad
    olt[...] = low_grad.T
    acc0[...] = jnp.zeros_like(acc0)
    acc1[...] = jnp.zeros_like(acc1)

    for k in range(1, parts):
        zb_wait(far(k), 0)
    advance("mid")

    def ffn(r, carry):
        k, j, s, home, g, _ = block(r)

        @pl.when(k > 0)
        def _():
            arrived(f_any(2), gf_r.at[2, home])

        wu = fg[home, 0]
        wd = fg[home, 1]
        hidden = nn(n2[...], wu) + bupa[s, :, pl.ds(pl.multiple_of(j * BLK, BLK), BLK)]
        cdf = 0.5 + 0.5 * lax.erf(hidden * RSQRT2)
        slope = cdf + hidden * (jnp.exp(-0.5 * hidden * hidden) * RSQRT2PI)
        active = (hidden * cdf).astype(BF16)
        act_grad = nn(ol[...], wd)
        hid_grad = (slope * act_grad).astype(BF16)
        acc0[...] += nt(active, wd)
        acc1[...] += nt(hid_grad, wu)
        early[pl.ds(4 + home, 1), 0:BLK] = jnp.sum(hid_grad.astype(F32), axis=0, keepdims=True)
        up_grad = nn(n2t[...], hid_grad).astype(BF16)
        dn_grad = nn(olt[...], active).astype(BF16)

        @pl.when(k > 0)
        def _():
            for stage in (1, 2):
                left(f_any(stage), gf_s.at[stage, home])

        @pl.when((k > 0) & (r - nblk < WIDE_FROM))
        def _():
            left(f_any(0), gf_s.at[0, home])

        fg[g, 0] = up_grad
        fg[g, 1] = dn_grad

        @pl.when(r == 3 * nblk - 1)
        def _():
            for m in range(n_far):
                zf(1 + m % (parts - 1), m // (parts - 1)).wait_send()

        @pl.when(r >= SLOTS_C)
        def _():
            pl.semaphore_wait(credit, 1)

        slot = odd(r, n_all)
        rf(0, r, slot).start()

        @pl.when(r > 0)
        def _():
            rf_core(r - 1, 1 - slot)

        return advance("r", r, carry)

    lax.fori_loop(0, n_all, ffn, begin("r"))
    rf_core(n_all - 1, (n_all - 1) % SLOTS_C)

    middle = mid[...]
    ngs[...] = (middle + (acc0[...] + bdn_ref[...][None, :])).astype(BF16)
    lo_copy = pltpu.make_async_copy(ngs, lo_ref, loc_sem.at[2 * nblk])
    lo_copy.start()
    unit, scale_inv = unit_of(middle)
    got = acc1[...]
    early[0:1, :] = jnp.sum(got * unit, axis=0, keepdims=True)
    early[1:2, :] = jnp.sum(got, axis=0, keepdims=True)
    middle_part = norm_back(got, unit, scale_inv, g2_ref[...][None, :])
    reload = pltpu.make_async_copy(cot_ref, ol, loc_sem.at[0])
    reload.start()
    reload.wait()
    out_grad = ol[...].astype(F32) * row_weight
    middle_grad = out_grad + middle_part
    mid[...] = middle_grad
    branch_low = middle_grad.astype(BF16)
    early[2:3, :] = jnp.sum(branch_low.astype(F32), axis=0, keepdims=True)
    ol[...] = branch_low

    for k in range(1, parts):
        for a in range(2):
            za(k, a).wait_send()
            for stage in range(3):
                left(a_any(stage, a), ga_s.at[stage, a, far(k)])
    advance("ln")

    head_row = lax.broadcasted_iota(jnp.int32, (hw, 128), 0)
    head_col = (lax.broadcasted_iota(jnp.int32, (hw, 128), 1) - at2) * HD
    pick = jnp.where((head_row >= head_col) & (head_row < head_col + HD), 1.0, 0.0).astype(BF16)

    def out_back(k, carry):
        s = far(k)
        mixed = mx[s, :, 0:hw]
        mixed_grad = nt(ol[...], aw[s, qkvw : 4 * hw, :]).astype(BF16)
        dmx[s, :, 0:hw] = mixed_grad
        prod = mixed_grad.astype(F32) * mixed.astype(F32)
        coarse = prod.astype(BF16)
        fine = (prod - coarse.astype(F32)).astype(BF16)
        delta = nn(coarse, pick) + nn(fine, pick)
        stat[s] = jnp.where((lane_n >= at2) & (lane_n < at2 + heads), delta, stat[s])
        aw[s, qkvw : 4 * hw, :] = nn(mixed.T, ol[...]).astype(BF16)
        return advance("k", k, carry)

    lax.fori_loop(0, parts, out_back, begin("k"))

    def p_in(s, h, half, buf):
        return pltpu.make_async_copy(
            ph_ref.at[s * heads + h, half], pst.at[buf, h], ps_sem.at[buf, h]
        )

    def fetch(it):
        for h in range(heads):
            p_in(group_of(it), h, 1 - quotient(it, parts, 2 * parts), odd(it, 2 * parts)).start()

    def att_group(it, half):
        s = group_of(it)
        base = half * share
        buf = odd(it, 2 * parts)

        @pl.when(it + 1 < 2 * parts)
        def _():
            fetch(it + 1)

        for h in range(heads):
            p_in(s, h, half, buf).wait()
        known = stat[s]
        wanted = known if half == 0 else pltpu.roll(known, 96, 1)
        delta = -(pltpu.roll(known, 64, 1) * wanted)
        coarse = delta.astype(BF16).astype(F32)
        aux = jnp.where((lane_n >= at0) & (lane_n < at0 + heads), coarse, 0.0)
        aux = jnp.where(
            (lane_n >= at0 + 8) & (lane_n < at0 + 8 + heads), pltpu.roll(delta - coarse, 8, 1), aux
        )
        scaled = dmx[s].astype(F32) * spread(wanted, at0)
        dg = jnp.concatenate(
            [scaled[:, 0:128], jnp.where(lane_n < at0, scaled[:, 128:256], aux)], axis=1
        ).astype(BF16)
        qg = qb[s]
        kg = kb[s, base : base + share]
        vg = vb[s, base : base + share]
        qt = qg[:, 0:hw].T
        dt = dg[:, 0:hw].T
        dq = jnp.zeros((share, 2 * 128), F32)
        dks = []
        dvs = []
        for h in range(heads):
            head = head_lanes(h)
            aux_h = (lane_w == hw + h) | (lane_w == hw + 8 + h)
            dm = jnp.where(head | aux_h, dg, jnp.zeros_like(dg))
            prob_grad = nt(dm, vg)
            probs = pst[buf, h]
            score_grad = (probs.astype(F32) * prob_grad).astype(BF16)
            dq = jnp.where(head, nn(score_grad, kg), dq)
            dks.append(nn(qt[HD * h : HD * (h + 1)], score_grad))
            dvs.append(nn(dt[HD * h : HD * (h + 1)], probs))
        dqt = (dq[:, 0:hw] * factor).T
        dkt = (jnp.concatenate(dks, axis=0) * math.log(2.0)).astype(BF16)
        dvt = jnp.concatenate(dvs, axis=0).astype(BF16)
        return s, dqt, dkt, dvt

    acc0[...] = jnp.zeros_like(acc0)
    acc1[...] = jnp.zeros_like(acc1)
    dmx_pad = jnp.zeros((share, 2 * 128 - hw), BF16)
    for s in range(parts):
        dmx[s, :, hw : 2 * 128] = dmx_pad
    fetch(0)

    def row_sums(values):
        return jnp.sum(values.astype(F32), axis=0, keepdims=True)

    def pair_half(it, carry):
        s, dqt, dkt, dvt = att_group(it, 1)
        uu[s, 0:hw, 0:share] = dqt.astype(BF16)
        uu[s, hw : 2 * hw, 0:share] = dkt
        uu[s, 2 * hw : qkvw, 0:share] = dvt
        back = uu[s, hw:qkvw, 0:share].T
        acc0[...] += nn(back, aw[s, hw:qkvw, :])
        late[pl.ds(2 * s + 1, 1), 0:hw] = row_sums(back[:, hw : 2 * hw])
        return advance("h", it, carry)

    lax.fori_loop(0, parts, pair_half, begin("h"))

    ng_copy = rcopy(ngs, ngr, ng_sem.at[0], ng_sem.at[1], (d, tp))
    pair_grad = acc0[...]
    lo_copy.wait()
    ngs[...] = pair_grad.astype(BF16)
    if NG_PLACE == 0:
        ng_copy.start()
    unit, _ = unit_of(xp[...].astype(F32))
    late[8:9, :] = jnp.sum(pair_grad * unit, axis=0, keepdims=True)
    late[9:10, :] = jnp.sum(pair_grad, axis=0, keepdims=True)

    stages = (dev_c, (dx, t), (dy, t))

    def vec(which, stage):
        buf, rx = (early, e_rx) if which == 0 else (late, l_rx)
        return rcopy(buf, rx.at[stage], sm_s.at[which, stage], sm_r.at[which, stage], stages[stage])

    def vec_far(which, k):
        rz = e_rz if which == 0 else l_rz
        return rcopy(
            rz.at[t], rz.at[t], sm_s.at[which, 2 + k], sm_r.at[which, 3 + t], (d, far(k))
        )

    def vec_next(which, stage):
        buf, rx = (early, e_rx) if which == 0 else (late, l_rx)
        vec(which, stage).wait_recv()
        vec(which, stage).wait_send()
        buf[...] = buf[...] + rx[stage]
        if stage < 2:
            vec(which, stage + 1).start()
        else:
            rz = e_rz if which == 0 else l_rz
            rz[t] = buf[...]
            for k in range(1, parts):
                vec_far(which, k).start()

    vec(0, 0).start()

    def own_half(it, carry):
        q = it - parts
        s, dqt, dkt, dvt = att_group(it, 0)
        dqt = (uu[s, 0:hw, 0:share].astype(F32) + dqt).astype(BF16)
        dd[0:hw, :] = dqt
        dd[hw : 2 * hw, :] = dkt
        dd[2 * hw : qkvw, :] = dvt
        back = dd[...].T
        acc1[...] += nn(back, aw[s, 0:qkvw, :])
        late[pl.ds(2 * s, 1), 0:hw] = row_sums(back[:, 0:hw])
        late[pl.ds(2 * s + 1, 1), 0:hw] = late[pl.ds(2 * s + 1, 1), 0:hw] + row_sums(
            back[:, 2 * hw : qkvw]
        )
        aw[s, 0:hw, :] = nn(dqt, xn[0:share, :]).astype(BF16)
        aw[s, hw:qkvw, :] = (
            nn(dd[hw:qkvw, :], xn[0:share, :]) + nn(uu[s, hw:qkvw, 0:share], xn[share:keys, :])
        ).astype(BF16)
        for a in range(2):
            ra(0, q, a).start()
        carry = advance("w", q, carry)
        if NG_PLACE > 0:

            @pl.when(q == NG_PLACE - 1)
            def _():
                ng_copy.start()

        for stage in range(3):

            @pl.when(q == stage)
            def _():
                vec_next(0, stage)

        return carry

    lax.fori_loop(parts, 2 * parts, own_half, begin("w"))

    own_grad = acc1[...]
    unit, scale_inv = unit_of(x_ref[...].astype(F32))
    late[8:9, :] = late[8:9, :] + jnp.sum(own_grad * unit, axis=0, keepdims=True)
    late[9:10, :] = late[9:10, :] + jnp.sum(own_grad, axis=0, keepdims=True)
    vec(1, 0).start()
    done = uu.at[0]
    xg_copy = pltpu.make_async_copy(mid, xg_ref, loc_sem.at[nblk])

    def aa(stage, a):
        _, _, first, second = route(t0 if a == 0 else 1 - t0)
        view = done.at[a_rows(stage, t0, a), a_lanes(a)]
        dev = (first, second, dev_c)[stage]
        return rcopy(view, view, aa_s.at[stage, a], aa_r.at[stage, a], dev)

    def att_final():
        for a in range(2):
            mine = a_rows(0, t0, a)
            low = CUTS[a][0]
            high = low + CUTS[a][1]
            total = aw[t, mine, low:high].astype(F32)
            for q in range(parts - 1):
                view = rz_a.at[q, :, a_lanes(a)]
                rcopy(view, view, ra_s.at[3, a, q], ra_r.at[3, a, q], (d, t)).wait_recv()
                total = total + rz_a[q, :, low:high].astype(F32)
            done[mine, low:high] = total.astype(BF16)
            aa(0, a).start()

    def att_round(stage):
        for a in range(2):
            aa(stage - 1, a).wait_recv()
            aa(stage, a).start()

    halves = [
        pltpu.make_async_copy(
            done.at[rows(n * 4 * piece, 4 * piece), :],
            oa_ref.at[rows(n * 4 * piece, 4 * piece), :],
            loc_sem.at[nblk + 1 + 3 * i],
        )
        for i, n in enumerate((c, 1 - c))
    ]

    def rows_final():
        ng_copy.wait_recv()
        grad = own_grad + ngr[...].astype(F32)
        mid[...] = mid[...] + norm_back(grad, unit, scale_inv, gain1)
        xg_copy.start()

    def wrap_up():
        for j in range(nblk):
            af(2, j).wait_recv()
            f_out(j, 0).start()
            if j >= 2:
                f_out(j - 2, 1).wait()
            ol[(j % 2) * BLK : (j % 2 + 1) * BLK, :] = fg[t * nblk + j, 1].T
            f_out(j, 1).start()

        for k in range(1, parts):
            zb(k, 0).wait_send()
            zb(k, 1).wait_send()
        x_copy.wait_send()
        ng_copy.wait_send()

        for j in range(nblk):
            for k in range(1, parts):
                left(f_any(1 if j < EARLY_FAR else 0), fz_s.at[(k - 1) * nblk + j])
        for r in range(n_all):
            if r < nblk or (r - nblk) // (parts - 1) >= EARLY_FAR:
                left(f_any(0), f1_s.at[r])

        def drain_all(r, carry):
            left(f_any(2), cf_s.at[r])
            left(f_any(1), f2_s.at[r])
            return carry

        lax.fori_loop(0, n_all, drain_all, 0)

        def drain_own(j, carry):
            for stage in range(3):
                left(f_any(stage), af_s.at[stage, j])
            return carry

        lax.fori_loop(0, nblk, drain_own, 0)
        for q in range(parts):
            for a in range(2):
                for stage in range(3):
                    left(a_any(2 - stage, a), ra_s.at[stage, a, q])
                if q < parts - 1:
                    left(a_any(0, a), ra_s.at[3, a, q])

    vec_stage = 0
    for name, low, high in TAIL:
        if name == "v":
            vec_next(1, vec_stage)
            vec_stage += 1
        elif name == "aa0":
            att_final()
        elif name == "aa1":
            att_round(1)
        elif name == "aa2":
            wrap_up()
            att_round(2)
            halves[0].start()
        elif name == "ng":
            rows_final()
        else:
            repeat(name, low, high)

    for which in range(2):
        rz = e_rz if which == 0 else l_rz
        for k in range(1, parts):
            s = far(k)
            rcopy(
                rz.at[s], rz.at[s], sm_s.at[which, 3], sm_r.at[which, 3 + s], (d, t)
            ).wait_recv()
    early[...] = ((e_rz[0] + e_rz[1]) + e_rz[2]) + e_rz[3]
    late[...] = ((l_rz[0] + l_rz[1]) + l_rz[2]) + l_rz[3]
    osm_ref[0:4, :] = early[0:4, :]
    osm_ref[4:6, :] = late[8:10, :]
    osm_ref[8:9, :] = late[pl.ds(2 * t, 1), :]
    osm_ref[9:10, :] = late[pl.ds(2 * t + 1, 1), :]
    for j in range(nblk):
        osm_ref[16 + j : 17 + j, :] = early[pl.ds(4 + t * nblk + j, 1), :]

    for a in range(2):
        aa(2, a).wait_recv()
    halves[1].start()
    for k in range(1, parts):
        for which in range(2):
            vec_far(which, k).wait_send()
    for j in range(nblk):
        f_out(j, 0).wait()
    for j in range(nblk - 2, nblk):
        f_out(j, 1).wait()

    halves[0].wait()
    halves[1].wait()
    xg_copy.wait()
    for stage in range(3):
        for a in range(2):
            aa(stage, a).wait_send()


def finish(
    lo,
    xg,
    up,
    dn,
    at,
    sm,
    lo_out,
    xg_out,
    up_out,
    dn_out,
    qkv_out,
    out_out,
    g2_out,
    s2_out,
    bo_out,
    bd_out,
    g1_out,
    s1_out,
    qv_out,
    bup_out,
    lo_b,
    xg_b,
    up_b,
    dn_b,
    at_b,
    up_f,
    dn_f,
    at_f,
    in_sem,
    out_sem,
):
    hw = out_out.shape[0]
    qkvw = qkv_out.shape[0]
    jobs = []
    for n, (src, mid_b, wide, dst) in enumerate(
        ((up, up_b, up_f, up_out), (dn, dn_b, dn_f, dn_out), (at, at_b, at_f, None))
    ):
        size = src.shape[0] // CHUNKS
        for i in range(CHUNKS):
            part = pl.ds(i * size, size)
            if dst is not None:
                to = dst.at[part, :]
            elif (i + 1) * size <= qkvw:
                to = qkv_out.at[part, :]
            else:
                to = out_out.at[pl.ds(i * size - qkvw, size), :]
            jobs.append((src.at[part, :], mid_b.at[part, :], wide.at[part, :], to))
    jobs.append((xg, xg_b, None, xg_out))
    jobs.append((lo, lo_b, None, lo_out))
    ins = [
        pltpu.make_async_copy(job[0], job[1], in_sem.at[i]) for i, job in enumerate(jobs)
    ]
    for cp in ins:
        cp.start()
    for i, ref in enumerate((g2_out, s2_out, bo_out, bd_out, g1_out, s1_out)):
        ref[...] = sm[i]
    qv_out[...] = sm[8:10, 0:hw]
    for j in range(bup_out.shape[0] // BLK):
        bup_out[j * BLK : (j + 1) * BLK] = sm[16 + j, 0:BLK]
    outs = []
    for i, (_, got, wide, dst) in enumerate(jobs):
        ins[i].wait()
        if wide is not None:
            wide[...] = got[...].astype(F32)
        outs.append(pltpu.make_async_copy(got if wide is None else wide, dst, out_sem.at[i]))
        outs[-1].start()
    for cp in outs:
        cp.wait()


def local(
    x_in,
    cotangent,
    lengths,
    bucket_ids,
    bucket_weights,
    ln1_gain,
    ln1_bias,
    w_qkv,
    qv_bias,
    w_out,
    b_out,
    ln2_gain,
    ln2_bias,
    w_up,
    b_up,
    w_down,
    b_down,
):
    share, width = x_in.shape
    hw = w_qkv.shape[2]
    heads = hw // HD
    parts = 4
    fw = w_up.shape[1]
    nblk = fw // BLK
    piece = width // GROUP
    keys = 2 * share
    n_all = parts * nblk
    n_far = n_all - nblk
    vm = pl.BlockSpec(memory_space=pltpu.VMEM)
    sm = pl.BlockSpec(memory_space=pltpu.SMEM)
    hbm = pl.BlockSpec(memory_space=pl.ANY)
    dma = pltpu.SemaphoreType.DMA
    scratch = [
        pltpu.VMEM((n_all + nblk, 2, width, BLK), BF16),
        pltpu.VMEM((parts, width, 4 * hw), BF16),
        pltpu.VMEM((SLOTS_C, 2, 4 * piece, BLK), BF16),
        pltpu.VMEM((n_all, 2, 2 * piece, BLK), BF16),
        pltpu.VMEM((n_all, 2, piece, BLK), BF16),
        pltpu.VMEM((n_far, 2, 2 * piece, BLK), BF16),
        pltpu.VMEM((parts, 4 * piece, 4 * hw), BF16),
        pltpu.VMEM((parts, 2 * piece, 4 * hw), BF16),
        pltpu.VMEM((parts, piece, 4 * hw), BF16),
        pltpu.VMEM((parts - 1, piece, 4 * hw), BF16),
        pltpu.VMEM((keys, width), BF16),
        pltpu.VMEM((share, width), BF16),
        pltpu.VMEM((parts, share, 256), BF16),
        pltpu.VMEM((parts, keys, 256), BF16),
        pltpu.VMEM((parts, keys, 256), BF16),
        pltpu.VMEM((parts, share, 256), BF16),
        pltpu.VMEM((parts, share, 256), BF16),
        pltpu.VMEM((parts, share, 128), F32),
        pltpu.VMEM((3 * hw, share), BF16),
        pltpu.VMEM((2, heads, share, share), BF16),
        pltpu.VMEM((share, width), F32),
        pltpu.VMEM((share, width), F32),
        pltpu.VMEM((share, width), F32),
        pltpu.VMEM((parts, width, width), BF16),
        pltpu.VMEM((share, width), BF16),
        pltpu.VMEM((width, share), BF16),
        pltpu.VMEM((share, width), BF16),
        pltpu.VMEM((share, width), BF16),
        pltpu.VMEM((parts, 1, fw), F32),
        pltpu.VMEM((parts, 2, hw), F32),
        pltpu.VMEM((24, width), F32),
        pltpu.VMEM((16, width), F32),
        pltpu.VMEM((3, 24, width), F32),
        pltpu.VMEM((parts, 24, width), F32),
        pltpu.VMEM((3, 16, width), F32),
        pltpu.VMEM((parts, 16, width), F32),
        dma((2 * nblk + 5,)),
        dma((2, heads)),
        dma((2, 3)),
        dma((2, parts)),
        dma((2,)),
        dma((6,)),
        dma((2, parts)),
        dma((3, 2, parts)),
        dma((3, 2, parts)),
        dma((n_far,)),
        dma((n_all,)),
        dma((3, n_all)),
        dma((3, n_all)),
        dma((n_all,)),
        dma((n_all,)),
        dma((n_all,)),
        dma((n_all,)),
        dma((n_all,)),
        dma((n_all,)),
        dma((n_far,)),
        dma((n_far,)),
        dma((3, nblk)),
        dma((3, nblk)),
        dma((4, 2, parts)),
        dma((4, 2, parts)),
        dma((3, 2)),
        dma((3, 2)),
        dma((2, 7)),
        dma((2, 7)),
        dma((2,)),
        pltpu.SemaphoreType.REGULAR,
    ]
    layer_out, x_grad, up, down, att, small, _ = pl.pallas_call(
        kernel,
        out_shape=[
            jax.ShapeDtypeStruct((share, width), BF16),
            jax.ShapeDtypeStruct((share, width), F32),
            jax.ShapeDtypeStruct((width, fw), BF16),
            jax.ShapeDtypeStruct((fw, width), BF16),
            jax.ShapeDtypeStruct((width, width), BF16),
            jax.ShapeDtypeStruct((24, width), F32),
            jax.ShapeDtypeStruct((parts * heads, 2, share, share), BF16),
        ],
        in_specs=[vm, hbm, sm, sm, sm, vm, vm, hbm, vm, hbm, vm, vm, vm, hbm, vm, hbm, vm],
        out_specs=[hbm, hbm, hbm, hbm, hbm, vm, hbm],
        scratch_shapes=scratch,
        compiler_params=pltpu.CompilerParams(
            collective_id=0, has_side_effects=True, vmem_limit_bytes=67043328
        ),
    )(
        x_in,
        cotangent,
        lengths,
        bucket_ids,
        bucket_weights,
        ln1_gain,
        ln1_bias,
        w_qkv.transpose(0, 2, 1),
        qv_bias,
        w_out,
        b_out,
        ln2_gain,
        ln2_bias,
        w_up,
        b_up,
        w_down,
        b_down,
    )
    dp = lax.axis_size("dp")
    if dp > GROUP:
        groups = [[g + GROUP * i for i in range(dp // GROUP)] for g in range(GROUP)]
        sums = lax.psum(
            tuple(g.astype(F32) for g in (up, down, att, small)), "dp", axis_index_groups=groups
        )
        up, down, att = (g.astype(BF16) for g in sums[:3])
        small = sums[3]
    flat = jax.ShapeDtypeStruct((width,), F32)
    outs = pl.pallas_call(
        finish,
        out_shape=[
            jax.ShapeDtypeStruct((share, width), BF16),
            jax.ShapeDtypeStruct((share, width), F32),
            jax.ShapeDtypeStruct((width, fw), F32),
            jax.ShapeDtypeStruct((fw, width), F32),
            jax.ShapeDtypeStruct((3 * hw, width), F32),
            jax.ShapeDtypeStruct((hw, width), F32),
            flat,
            flat,
            flat,
            flat,
            flat,
            flat,
            jax.ShapeDtypeStruct((2, hw), F32),
            jax.ShapeDtypeStruct((fw,), F32),
        ],
        in_specs=[hbm] * 5 + [vm],
        out_specs=[hbm] * 6 + [vm] * 8,
        scratch_shapes=[
            pltpu.VMEM((share, width), BF16),
            pltpu.VMEM((share, width), F32),
            pltpu.VMEM((width, fw), BF16),
            pltpu.VMEM((fw, width), BF16),
            pltpu.VMEM((width, width), BF16),
            pltpu.VMEM((width, fw), F32),
            pltpu.VMEM((fw, width), F32),
            pltpu.VMEM((width, width), F32),
            dma((3 * CHUNKS + 2,)),
            dma((3 * CHUNKS + 2,)),
        ],
    )(layer_out, x_grad, up, down, att, small)
    layer_out, x_grad, g_up, g_down, g_qkv, g_out, g2, s2, bo, bd, g1, s1, g_qv, g_bup = outs
    return (
        layer_out,
        x_grad,
        g1,
        s1,
        g_qkv.reshape(3, hw, width).transpose(0, 2, 1),
        g_qv,
        g_out,
        bo,
        g2,
        s2,
        g_up,
        g_bup,
        g_down,
        bd,
    )


def solution(mesh):
    return jax.shard_map(
        local,
        mesh=mesh,
        in_specs=(
            P(("dp", "tensor"), None),
            P(("dp", "tensor"), None),
            P("dp", None),
            P("dp"),
            P(),
            P(),
            P(),
            P(None, None, "tensor"),
            P(None, "tensor"),
            P("tensor", None),
            P(),
            P(),
            P(),
            P(None, "tensor"),
            P("tensor"),
            P("tensor", None),
            P(),
        ),
        out_specs=(
            P(("dp", "tensor"), None),
            P(("dp", "tensor"), None),
            P(),
            P(),
            P(None, None, "tensor"),
            P(None, "tensor"),
            P("tensor", None),
            P(),
            P(),
            P(),
            P(None, "tensor"),
            P("tensor"),
            P("tensor", None),
            P(),
        ),
        check_vma=False,
    )
```

```python
import functools
import math

import jax
import jax.numpy as jnp
from jax import lax
from jax.experimental import pallas as pl
from jax.experimental.pallas import tpu as pltpu
from jax.sharding import PartitionSpec as P

HD = 32
BUCKET = 256
EPSILON = 1e-05
GROUP = 8
BLK = 256
BIG = 1e30
F32 = jnp.float32
BF16 = jnp.bfloat16
MESH = pl.DeviceIdType.MESH
RSQRT2 = 1.0 / math.sqrt(2.0)
RSQRT2PI = 1.0 / math.sqrt(2.0 * math.pi)
SLOTS_C = 2
X_PLACE = 0
WIDE_FROM = 15
NG_PLACE = 1
EARLY_FAR = 3
CUTS = ((0, 256), (256, 384))
CHUNKS = 4
PLAN = {
    "p0": (
        ("a0", (0, 1)),
        ("a1", (0, 1)),
    ),
    "p1": (
        ("a0", (1, 3)),
        ("a2", (0, 1)),
    ),
    "p2": (
        ("a1", (1, 3)),
        ("a2", (1, 3)),
    ),
    "pj": (
    ),
    "o": (
    ),
    "q": (
        ("g0", (0, 0, 11, 14, 15)),
        ("g1", (0, 0, 0, 0, 8)),
    ),
    "mid": (
        ("g1", (8, 10)),
    ),
    "r": (
        ("g1", (10, 11, 15, 15, 15, 15, 15, 15, 15, 15, 15, 15, 15, 15, 15, 15, 15, 15, 15, 15, 15)),
        ("g2", (0, 0, 3, 3, 5, 8, 9, 9, 9, 11, 13, 15, 15, 15, 15, 15, 15, 15, 15, 15, 15)),
        ("rf", (0, 0, 0, 0, 0, 0, 0, 0, 0, 0, 0, 0, 0, 0, 0, 2, 2, 4, 4, 5, 5)),
        ("r1", (0, 0, 0, 0, 0, 0, 0, 0, 0, 0, 0, 0, 0, 2, 3, 3, 4, 4, 5, 5, 7)),
        ("r2", (0, 0, 0, 0, 0, 0, 0, 1, 2, 3, 4, 4, 4, 6, 8, 8, 10, 11, 12, 13, 14)),
    ),
    "ln": (
        ("rf", (5, 7)),
        ("r2", (14, 16)),
    ),
    "k": (
        ("rf", (7, 7, 8, 8, 9)),
        ("r1", (7, 9, 9, 9, 9)),
        ("r2", (16, 16, 16, 20, 20)),
    ),
    "h": (
        ("rf", (9, 9, 9, 11, 17)),
        ("r1", (9, 14, 16, 17, 17)),
        ("f0", (0, 0, 0, 0, 2)),
    ),
    "w": (
        ("rf", (17, 17, 19, 19, 20)),
        ("r1", (17, 20, 20, 20, 20)),
        ("b3", (0, 0, 0, 0, 2)),
        ("b2", (0, 0, 0, 2, 3)),
        ("b1", (0, 0, 2, 3, 4)),
        ("f0", (2, 2, 3, 3, 5)),
        ("f1", (0, 1, 1, 3, 3)),
        ("f2", (0, 0, 0, 0, 3)),
    ),
}
TAIL = (
    ("b2", 3, 4),
    ("v", 0, 0),
    ("f1", 3, 5),
    ("b3", 2, 4),
    ("v", 0, 0),
    ("aa0", 0, 0),
    ("v", 0, 0),
    ("aa1", 0, 0),
    ("f2", 3, 5),
    ("ng", 0, 0),
    ("aa2", 0, 0),
)


def nn(a, b):
    return lax.dot_general(a, b, (((1,), (0,)), ((), ())), preferred_element_type=F32)


def nt(a, b):
    return lax.dot_general(a, b, (((1,), (1,)), ((), ())), preferred_element_type=F32)


def unit_of(values):
    centre = values - jnp.mean(values, axis=-1, keepdims=True)
    scale_inv = lax.rsqrt(jnp.mean(centre * centre, axis=-1, keepdims=True) + EPSILON)
    return centre * scale_inv, scale_inv


def norm_back(grad, unit, scale_inv, gain):
    scaled = grad * gain
    return scale_inv * (
        scaled
        - jnp.mean(scaled, axis=-1, keepdims=True)
        - unit * jnp.mean(scaled * unit, axis=-1, keepdims=True)
    )


def lanes(shape):
    return lax.broadcasted_iota(jnp.int32, shape, 1)


def kernel(
    x_ref,
    cot_ref,
    len_ref,
    bid_ref,
    bw_ref,
    g1_ref,
    s1_ref,
    wqkv_ref,
    qvb_ref,
    wout_ref,
    bout_ref,
    g2_ref,
    s2_ref,
    wup_ref,
    bup_ref,
    wdn_ref,
    bdn_ref,
    lo_ref,
    xg_ref,
    ou_ref,
    od_ref,
    oa_ref,
    osm_ref,
    ph_ref,
    fg,
    aw,
    rc_f,
    r2_f,
    r1_f,
    rz_f,
    rc_a,
    r2_a,
    r1_a,
    rz_a,
    xn,
    xp,
    qb,
    kb,
    vb,
    mx,
    dmx,
    stat,
    dd,
    pst,
    mid,
    acc0,
    acc1,
    uu,
    ol,
    olt,
    ngs,
    ngr,
    bupa,
    qvba,
    early,
    late,
    e_rx,
    e_rz,
    l_rx,
    l_rz,
    loc_sem,
    ps_sem,
    za_s,
    za_r,
    zx_sem,
    zb_s,
    zb_r,
    ga_s,
    ga_r,
    zf_s,
    zf_r,
    gf_s,
    gf_r,
    cf_s,
    cf_r,
    f2_s,
    f2_r,
    f1_s,
    f1_r,
    fz_s,
    fz_r,
    af_s,
    af_r,
    ra_s,
    ra_r,
    aa_s,
    aa_r,
    sm_s,
    sm_r,
    ng_sem,
    credit,
):
    share, width = x_ref.shape
    hw = wqkv_ref.shape[1]
    heads = hw // HD
    qkvw = 3 * hw
    parts = 4
    nblk = wup_ref.shape[1] // BLK
    piece = width // GROUP
    keys = 2 * share
    factor = HD ** (-0.5)
    q_scale = factor * math.log2(math.e)

    d = lax.axis_index("dp")
    t = lax.axis_index("tensor")
    c = d % 2
    bx = (d // 2) % 2
    by = (d // 4) % 2
    dev_c = (d + 1 - 2 * c, t)
    dx = d + 2 - 4 * bx
    dy = d + 4 - 8 * by
    t0 = t % 2
    t1 = t // 2
    tp = t + 1 - 2 * t0

    def quotient(n, step, limit):
        if isinstance(n, int):
            return n // step
        return sum(jnp.where(n >= i, 1, 0) for i in range(step, limit, step))

    def odd(n, limit):
        return n - 2 * quotient(n, 2, limit)

    def differ(a, b):
        return a + b - 2 * a * b

    def far_bits(k):
        high = quotient(k, 2, parts)
        low = differ(t0, k - 2 * high)
        return low + 2 * differ(t1, high), low

    def far(k):
        return far_bits(k)[0]

    def route(par):
        low = bx + par * (by - bx)
        high = by + par * (bx - by)
        first = (dx + par * (dy - dx), t)
        second = (dy + par * (dx - dy), t)
        return low, high, first, second

    def rcopy(src, dst, ssem, rsem, dev):
        return pltpu.make_async_remote_copy(
            src_ref=src, dst_ref=dst, send_sem=ssem, recv_sem=rsem, device_id=dev, device_id_type=MESH
        )

    def arrived(view, sem):
        rcopy(view, view, sem, sem, (d, t)).wait_recv()

    def left(view, sem):
        rcopy(view, view, sem, sem, (d, t)).wait_send()

    def rows(start, size):
        return pl.ds(pl.multiple_of(start, 16), size)

    barrier = pltpu.get_barrier_semaphore()
    for dev in (dev_c, (dx, t), (dy, t), (d, far(1)), (d, far(2)), (d, far(3))):
        pl.semaphore_signal(barrier, inc=1, device_id=dev, device_id_type=MESH)

    def up_load(j):
        return pltpu.make_async_copy(
            wup_ref.at[:, pl.ds(j * BLK, BLK)], fg.at[t * nblk + j, 0], loc_sem.at[j]
        )

    def dn_load(j):
        return pltpu.make_async_copy(
            wdn_ref.at[pl.ds(j * BLK, BLK), :],
            uu.at[j // 2, pl.ds((j % 2) * BLK, BLK), :],
            loc_sem.at[nblk + j],
        )

    cot_load = pltpu.make_async_copy(cot_ref, ol, loc_sem.at[2 * nblk])

    a_loads = [
        pltpu.make_async_copy(
            wqkv_ref.at[i], aw.at[t, pl.ds(i * hw, hw), :], loc_sem.at[2 * nblk + 1 + i]
        )
        for i in range(3)
    ]
    a_loads.append(
        pltpu.make_async_copy(
            wout_ref, aw.at[t, pl.ds(qkvw, hw), :], loc_sem.at[2 * nblk + 4]
        )
    )
    for cp in a_loads:
        cp.start()
    for j in range(nblk):
        dn_load(j).start()
        up_load(j).start()
    cot_load.start()
    bupa[t] = bup_ref[...][None, :]
    qvba[t] = qvb_ref[...]

    pl.semaphore_wait(barrier, 6)

    def a_rows(stage, parity, a):
        low, high, _, _ = route(parity if a == 0 else 1 - parity)
        if stage == 0:
            return rows((c * 4 + high * 2 + low) * piece, piece)
        if stage == 1:
            return rows((c * 4 + high * 2) * piece, 2 * piece)
        return rows(c * 4 * piece, 4 * piece)

    def a_lanes(a):
        return pl.ds(CUTS[a][0], CUTS[a][1])

    def a_any(stage, a):
        return aw.at[0, 0 : (piece, 2 * piece, 4 * piece)[stage], a_lanes(a)]

    def za(k, a):
        view = aw.at[t, a_rows(0, t0, a), a_lanes(a)]
        return rcopy(view, view, za_s.at[a, k - 1], za_r.at[a, t], (d, far(k)))

    def zb(k, which):
        dst = (bupa if which == 0 else qvba).at[t]
        return rcopy(dst, dst, zb_s.at[2 * (k - 1) + which], zb_r.at[which, t], (d, far(k)))

    def zb_wait(s, which):
        dst = (bupa if which == 0 else qvba).at[s]
        rcopy(dst, dst, zb_s.at[0], zb_r.at[which, s], (d, t)).wait_recv()

    x_copy = rcopy(x_ref, xp, zx_sem.at[0], zx_sem.at[1], (d, tp))

    for cp in a_loads:
        cp.wait()
    for k in range(1, parts):
        for a in range(2):
            za(k, a).start()
        zb(k, 1).start()
    for k in range(1, parts):
        zb(k, 0).start()

    def ga(stage, s, parity, a):
        _, _, first, second = route(parity if a == 0 else 1 - parity)
        view = aw.at[s, a_rows(stage, parity, a), a_lanes(a)]
        dev = (first, second, dev_c)[stage]
        return rcopy(view, view, ga_s.at[stage, a, s], ga_r.at[stage, a, s], dev)

    def step_a(stage, i):
        s, parity = far_bits(i + 1)
        for a in range(2):
            if stage == 0:
                arrived(a_any(0, a), za_r.at[a, s])
            else:
                arrived(a_any(stage - 1, a), ga_r.at[stage - 1, a, s])
            ga(stage, s, parity, a).start()

    n_far = (parts - 1) * nblk

    def far_block(m):
        j = quotient(m, parts - 1, n_far)
        s, parity = far_bits(1 + m - (parts - 1) * j)
        return s, j, s * nblk + j, differ(parity, odd(j, nblk))

    def own_parity(j):
        return differ(t0, odd(j, nblk))

    def gf(stage, m):
        _, _, b, par = far_block(m)
        low, high, first, second = route(par)
        if stage == 0:
            view, dev = fg.at[b, :, rows((c * 4 + high * 2 + low) * piece, piece), :], first
        elif stage == 1:
            view, dev = fg.at[b, :, rows((c * 4 + high * 2) * piece, 2 * piece), :], second
        else:
            view, dev = fg.at[b, :, rows(c * 4 * piece, 4 * piece), :], dev_c
        return rcopy(view, view, gf_s.at[stage, b], gf_r.at[stage, b], dev)

    def f_any(stage):
        return fg.at[0, :, 0 : (piece, 2 * piece, 4 * piece)[stage], :]

    def step_g(stage, m):
        b = far_block(m)[2]
        if WIDE_FROM >= n_far:
            if stage == 0:
                arrived(f_any(0), zf_r.at[b])
            else:
                arrived(f_any(stage - 1), gf_r.at[stage - 1, b])
            gf(stage, m).start()
            return
        if stage == 0:

            @pl.when(m < WIDE_FROM)
            def _():
                arrived(f_any(0), zf_r.at[b])
                gf(0, m).start()

            return
        if stage == 1:

            @pl.when(m < WIDE_FROM)
            def _():
                arrived(f_any(0), gf_r.at[0, b])

            @pl.when(m >= WIDE_FROM)
            def _():
                arrived(f_any(1), zf_r.at[b])

        else:
            arrived(f_any(1), gf_r.at[1, b])
        gf(stage, m).start()

    n_all = parts * nblk

    def block(r):
        own = jnp.where(r < nblk, 1, 0)
        m = r - nblk
        turn_j = quotient(m, parts - 1, n_far)
        k = (1 - own) * (1 + m - (parts - 1) * turn_j)
        j = own * r + (1 - own) * turn_j
        s, parity = far_bits(k)
        home = s * nblk + j
        return k, j, s, home, home + own * (n_all + j - home), differ(parity, odd(j, nblk))

    def rf(stage, r, slot=None):
        k, j, s, _, g, par = block(r)
        low, high, first, second = route(par)
        if stage == 0:
            return rcopy(
                fg.at[g, :, rows((1 - c) * 4 * piece, 4 * piece), :],
                rc_f.at[slot],
                cf_s.at[r],
                cf_r.at[r],
                dev_c,
            )
        if stage == 1:
            return rcopy(
                fg.at[g, :, rows((c * 4 + (1 - high) * 2) * piece, 2 * piece), :],
                r2_f.at[r],
                f2_s.at[r],
                f2_r.at[r],
                second,
            )
        if stage == 2:
            return rcopy(
                fg.at[g, :, rows((c * 4 + high * 2 + 1 - low) * piece, piece), :],
                r1_f.at[r],
                f1_s.at[r],
                f1_r.at[r],
                first,
            )
        z = jnp.maximum((k - 1) * nblk + j, 0)
        if stage == 4:
            return rcopy(
                fg.at[g, :, rows((c * 4 + high * 2) * piece, 2 * piece), :],
                rz_f.at[z],
                fz_s.at[z],
                fz_r.at[z],
                (d, s),
            )
        return rcopy(
            fg.at[g, :, rows((c * 4 + high * 2 + low) * piece, piece), :],
            rz_f.at[z, :, 0:piece, :],
            fz_s.at[z],
            fz_r.at[z],
            (d, s),
        )

    def add_rows(ref, got):
        ref[...] = (ref[...].astype(F32) + got[...].astype(F32)).astype(BF16)

    def rf_core(r, slot):
        g = block(r)[4]
        arrived(rc_f.at[slot], cf_r.at[r])
        add_rows(fg.at[g, :, rows(c * 4 * piece, 4 * piece), :], rc_f.at[slot])

        @pl.when(r < n_all - SLOTS_C)
        def _():
            pl.semaphore_signal(credit, inc=1, device_id=dev_c, device_id_type=MESH)

    def turn(i):
        return i + nblk - n_all * jnp.where(i >= n_all - nblk, 1, 0)

    def rf_first(r):
        _, j, _, _, g, par = block(r)
        _, high, _, _ = route(par)
        both = fg.at[g, :, rows((c * 4 + high * 2) * piece, 2 * piece), :]
        arrived(r2_f.at[r], f2_r.at[r])
        add_rows(both, r2_f.at[r])

        @pl.when((j < EARLY_FAR) & (r >= nblk))
        def _():
            rf(4, r).start()

        @pl.when((j < EARLY_FAR) & (r < nblk))
        def _():
            total = both[...].astype(F32)
            for k in range(1, parts):
                z = (k - 1) * nblk + j
                arrived(rz_f.at[z], fz_r.at[z])
                total = total + rz_f[z].astype(F32)
            both[...] = total.astype(BF16)

        @pl.when((j >= EARLY_FAR) | (r < nblk))
        def _():
            rf(2, r).start()

    def rf_far(r):
        _, j, _, _, g, par = block(r)
        low, high, _, _ = route(par)

        @pl.when((j >= EARLY_FAR) | (r < nblk))
        def _():
            arrived(r1_f.at[r], f1_r.at[r])
            add_rows(fg.at[g, :, rows((c * 4 + high * 2 + low) * piece, piece), :], r1_f.at[r])

        @pl.when((j >= EARLY_FAR) & (r >= nblk))
        def _():
            rf(3, r).start()

    def af(stage, j):
        low, high, first, second = route(own_parity(j))
        b = t * nblk + j
        if stage == 0:
            view, dev = fg.at[b, :, rows((c * 4 + high * 2 + low) * piece, piece), :], first
        elif stage == 1:
            view, dev = fg.at[b, :, rows((c * 4 + high * 2) * piece, 2 * piece), :], second
        else:
            view, dev = fg.at[b, :, rows(c * 4 * piece, 4 * piece), :], dev_c
        return rcopy(view, view, af_s.at[stage, j], af_r.at[stage, j], dev)

    def f_final(j):
        low, high, _, _ = route(own_parity(j))
        mine = rows((c * 4 + high * 2 + low) * piece, piece)

        @pl.when(j < EARLY_FAR)
        def _():
            fg[t * nblk + j, :, mine, :] = fg[n_all + j, :, mine, :]

        @pl.when(j >= EARLY_FAR)
        def _():
            total = fg[n_all + j, :, mine, :].astype(F32)
            for k in range(1, parts):
                z = (k - 1) * nblk + j
                arrived(rz_f.at[z, :, 0:piece, :], fz_r.at[z])
                total = total + rz_f[z, :, 0:piece, :].astype(F32)
            fg[t * nblk + j, :, mine, :] = total.astype(BF16)

        af(0, j).start()

    def f_out(j, which):
        if which == 0:
            return pltpu.make_async_copy(
                fg.at[t * nblk + j, 0], ou_ref.at[:, pl.ds(j * BLK, BLK)], loc_sem.at[j]
            )
        return pltpu.make_async_copy(
            ol.at[pl.ds((j % 2) * BLK, BLK), :],
            od_ref.at[pl.ds(j * BLK, BLK), :],
            loc_sem.at[nblk + 2 + j % 2],
        )

    def f_second(j):
        arrived(f_any(0), af_r.at[0, j])
        af(1, j).start()

    def f_third(j):
        arrived(f_any(1), af_r.at[1, j])
        af(2, j).start()

    def group_bits(it):
        n = it + 1
        return far_bits(n - parts * quotient(n, parts, 2 * parts + 1))

    def group_of(it):
        return group_bits(it)[0]

    def ra(stage, q, a):
        s, parity = group_bits(q)
        low, high, first, second = route(parity if a == 0 else 1 - parity)
        if stage == 0:
            where, buf, dev = rows((1 - c) * 4 * piece, 4 * piece), rc_a, dev_c
        elif stage == 1:
            where, buf, dev = rows((c * 4 + (1 - high) * 2) * piece, 2 * piece), r2_a, second
        elif stage == 2:
            where, buf, dev = rows((c * 4 + high * 2 + 1 - low) * piece, piece), r1_a, first
        else:
            where, buf, dev = rows((c * 4 + high * 2 + low) * piece, piece), rz_a, (d, s)
            q = jnp.minimum(q, parts - 2)
        return rcopy(
            aw.at[s, where, a_lanes(a)],
            buf.at[q, :, a_lanes(a)],
            ra_s.at[stage, a, q],
            ra_r.at[stage, a, q],
            dev,
        )

    def step_b(stage, q):
        s, parity = group_bits(q)
        buf = (rc_a, r2_a, r1_a)[stage - 1]
        for a in range(2):
            view = buf.at[q, :, a_lanes(a)]
            arrived(view, ra_r.at[stage - 1, a, q])
            add_rows(aw.at[s, a_rows(3 - stage, parity, a), a_lanes(a)], view)
            if stage < 3:
                ra(stage, q, a).start()
            else:

                @pl.when(q < parts - 1)
                def _():
                    ra(3, q, a).start()

    steps = {
        "a0": lambda i: step_a(0, i),
        "a1": lambda i: step_a(1, i),
        "a2": lambda i: step_a(2, i),
        "g0": lambda i: step_g(0, i),
        "g1": lambda i: step_g(1, i),
        "g2": lambda i: step_g(2, i),
        "r2": lambda i: rf(1, turn(i)).start(),
        "r1": lambda i: rf_first(turn(i)),
        "rf": lambda i: rf_far(turn(i)),
        "b1": lambda i: step_b(1, i),
        "b2": lambda i: step_b(2, i),
        "b3": lambda i: step_b(3, i),
        "f0": lambda i: f_final(i),
        "f1": lambda i: f_second(i),
        "f2": lambda i: f_third(i),
    }

    def repeat(name, low, high):
        def one(i, carry):
            steps[name](i)
            return carry

        lax.fori_loop(low, high, one, 0)

    def advance(place, idx=None, reached=None):
        after = []
        for n, (name, counts) in enumerate(PLAN[place]):
            low = counts[0] if reached is None else reached[n]
            high = low
            if idx is None:
                high = counts[-1]
            else:
                for i in range(len(counts) - 1):
                    more = counts[i + 1] - counts[i]
                    if more:
                        high = high + jnp.where(idx == i, more, 0)
            repeat(name, low, high)
            after.append(high)
        return tuple(after)

    def begin(place):
        return tuple(jnp.int32(counts[0]) for _, counts in PLAN[place])

    gain1 = g1_ref[...][None, :]
    shift1 = s1_ref[...][None, :]
    unit, _ = unit_of(x_ref[...].astype(F32))
    xn[0:share, :] = (unit * gain1 + shift1).astype(BF16)
    advance("p0")

    def zf(k, j):
        low, high, _, _ = route(own_parity(j))
        where = rows((c * 4 + high * 2 + low) * piece, piece)
        if j * (parts - 1) + k - 1 >= WIDE_FROM:
            where = rows((c * 4 + high * 2) * piece, 2 * piece)
        view = fg.at[t * nblk + j, :, where, :]
        return rcopy(
            view, view, zf_s.at[(k - 1) * nblk + j], zf_r.at[t * nblk + j], (d, far(k))
        )

    for j in range(nblk):
        up_load(j).wait()
        dn_load(j).wait()
        fg[t * nblk + j, 1] = uu[j // 2, (j % 2) * BLK : (j % 2 + 1) * BLK, :].T
    for m in range((parts - 1) * nblk):
        if m == X_PLACE:
            x_copy.start()
        zf(1 + m % (parts - 1), m // (parts - 1)).start()

    advance("p1")

    bucket = bid_ref[0]
    span = jnp.where(bucket == 0, BUCKET, jnp.where(bucket == 1, 2 * BUCKET, 4 * BUCKET))
    weight = jnp.where(bucket == 0, bw_ref[0], jnp.where(bucket == 1, bw_ref[1], bw_ref[2]))

    def slot_info(base, shape):
        place = base + lax.broadcasted_iota(jnp.int32, shape, 0)
        item = jnp.zeros(shape, jnp.int32)
        for j in range(1, len_ref.shape[1]):
            item = item + jnp.where(place >= j * span, 1, 0)
        length = jnp.zeros(shape, jnp.int32)
        for j in range(len_ref.shape[1]):
            length = jnp.where(item == j, len_ref[0, j], length)
        return item, (place - item * span) < length

    wide = (share, 2 * 128)
    lane = lanes(wide)
    slots = len_ref.shape[1]
    in_aux = (lane >= hw) & (lane < hw + slots)
    one_aux = jnp.where(lane >= hw, 1.0, 0.0).astype(BF16)

    own_item, own_live = slot_info(t * share, wide)
    q_aux = jnp.where(in_aux & (own_item == lane - hw), 1.0, 0.0).astype(BF16)
    k_aux0 = jnp.where(in_aux & ~((own_item == lane - hw) & own_live), -BIG, 0.0).astype(BF16)
    pair_item, pair_live = slot_info(tp * share, wide)
    k_aux1 = jnp.where(in_aux & ~((pair_item == lane - hw) & pair_live), -BIG, 0.0).astype(BF16)
    for s in range(parts):
        qb[s] = q_aux
        kb[s, 0:share] = k_aux0
        kb[s, share:keys] = k_aux1
        vb[s, 0:share] = one_aux
        vb[s, share:keys] = one_aux
    _, live1 = slot_info(t * share, (share, 128))
    row_weight = jnp.where(live1, weight, 0.0)[:, 0:1]

    advance("p2")

    def project(s, half, own):
        base = half * share
        first = 0 if own else hw
        out = nt(xn[base : base + share, :], aw[s, first:qkvw, :])
        if own:
            qb[s, :, 0:hw] = ((out[:, 0:hw] + qvba[s, 0:1, :]) * q_scale).astype(BF16)
        at = hw - first
        kb[s, base : base + share, 0:hw] = out[:, at : at + hw].astype(BF16)
        vb[s, base : base + share, 0:hw] = (
            out[:, at + hw : at + 2 * hw] + qvba[s, 1:2, :]
        ).astype(BF16)

    lane_w = lanes((share, 2 * 128))
    lane_n = lanes((share, 128))

    def head_lanes(h):
        return (lane_w >= HD * h) & (lane_w < HD * (h + 1))

    def spread(values, at):
        out = jnp.zeros((share, 2 * 128), F32)
        for h in range(heads):
            out = jnp.where(head_lanes(h), values[:, at + h : at + h + 1], out)
        return out

    def p_out(s, h, half, buf):
        return pltpu.make_async_copy(
            pst.at[buf, h], ph_ref.at[s * heads + h, half], ps_sem.at[buf, h]
        )

    at0 = hw - 128
    at1 = at0 + 32
    at2 = at0 + 64

    def att_forward(k, half):
        s = far(k)
        base = half * share
        buf = odd(k, parts)
        if half == 1:
            for h in range(heads):
                p_out(s, h, half, buf).wait()
        else:

            @pl.when(k >= 2)
            def _():
                for h in range(heads):
                    p_out(s, h, half, buf).wait()

        qg = qb[s]
        kg = kb[s, base : base + share]
        vg = vb[s, base : base + share]
        out = jnp.zeros((share, 2 * 128), F32)
        tops = jnp.zeros((share, 128), F32)
        for h in range(heads):
            head = head_lanes(h)
            qm = jnp.where(head | (lane_w >= hw), qg, jnp.zeros_like(qg))
            scores = nt(qm, kg)
            top = jnp.max(scores, axis=1, keepdims=True)
            probs = jnp.exp2(scores - top).astype(BF16)
            pst[buf, h] = probs
            mixed = nn(probs, vg)
            out = jnp.where(head | (lane_w == hw + h), mixed, out)
            tops = jnp.where(lane_n == at0 + h, top, tops)
        for h in range(heads):
            p_out(s, h, half, buf).start()
        sums = jnp.where((lane_n >= at0) & (lane_n < at0 + heads), out[:, 128:256], 1.0)
        log_sum = tops + jnp.log2(sums)
        if half == 0:
            mx[s] = (out * spread(1.0 / sums, at0)).astype(BF16)
            stat[s] = jnp.where(lane_n < at1, tops, pltpu.roll(log_sum, 32, 1))
        else:
            before = stat[s]
            log_before = pltpu.roll(before, 96, 1)
            upper = jnp.maximum(log_sum, log_before)
            lower = jnp.minimum(log_sum, log_before)
            log_all = upper + jnp.log2(1.0 + jnp.exp2(lower - upper))
            part0 = jnp.exp2(log_before - log_all)
            part1 = jnp.exp2(log_sum - log_all) / sums
            mx[s] = (
                mx[s].astype(F32) * spread(part0, at0) + out * spread(part1, at0)
            ).astype(BF16)
            stat[s] = jnp.where(
                lane_n < at1,
                jnp.exp2(before - log_all),
                pltpu.roll(jnp.exp2(tops - log_all), 32, 1),
            )

    def own_keys(k, carry):
        s = far(k)

        @pl.when(k > 0)
        def _():
            zb_wait(s, 1)
            for a in range(2):
                arrived(a_any(2, a), ga_r.at[2, a, s])

        project(s, 0, True)

        @pl.when(k == 0)
        def _():
            advance("pj")

        att_forward(k, 0)
        return advance("o", k, carry)

    lax.fori_loop(0, parts, own_keys, begin("o"))

    x_copy.wait_recv()
    unit, _ = unit_of(xp[...].astype(F32))
    xn[share:keys, :] = (unit * gain1 + shift1).astype(BF16)

    def pair_keys(k, carry):
        project(far(k), 1, False)
        att_forward(k, 1)
        return advance("q", k, carry)

    lax.fori_loop(0, parts, pair_keys, begin("q"))
    for buf in range(2):
        for h in range(heads):
            p_out(0, h, 1, buf).wait()

    branch = jnp.zeros((share, width), F32)
    for s in range(parts):
        branch = branch + nn(mx[s, :, 0:hw], aw[s, qkvw : 4 * hw, :])
    middle = x_ref[...].astype(F32) + (branch + bout_ref[...][None, :])
    mid[...] = middle
    unit, _ = unit_of(middle)
    normed = (unit * g2_ref[...][None, :] + s2_ref[...][None, :]).astype(BF16)
    n2 = uu.at[0, 0:share, :]
    n2t = uu.at[1, :, 0:share]
    n2[...] = normed
    n2t[...] = normed.T
    cot_load.wait()
    low_grad = (ol[...].astype(F32) * row_weight).astype(BF16)
    early[...] = jnp.zeros_like(early)
    late[...] = jnp.zeros_like(late)
    early[3:4, :] = jnp.sum(low_grad.astype(F32), axis=0, keepdims=True)
    ol[...] = low_grad
    olt[...] = low_grad.T
    acc0[...] = jnp.zeros_like(acc0)
    acc1[...] = jnp.zeros_like(acc1)

    for k in range(1, parts):
        zb_wait(far(k), 0)
    advance("mid")

    def ffn(r, carry):
        k, j, s, home, g, _ = block(r)

        @pl.when(k > 0)
        def _():
            arrived(f_any(2), gf_r.at[2, home])

        wu = fg[home, 0]
        wd = fg[home, 1]
        hidden = nn(n2[...], wu) + bupa[s, :, pl.ds(pl.multiple_of(j * BLK, BLK), BLK)]
        cdf = 0.5 + 0.5 * lax.erf(hidden * RSQRT2)
        slope = cdf + hidden * (jnp.exp(-0.5 * hidden * hidden) * RSQRT2PI)
        active = (hidden * cdf).astype(BF16)
        act_grad = nn(ol[...], wd)
        hid_grad = (slope * act_grad).astype(BF16)
        acc0[...] += nt(active, wd)
        acc1[...] += nt(hid_grad, wu)
        early[pl.ds(4 + home, 1), 0:BLK] = jnp.sum(hid_grad.astype(F32), axis=0, keepdims=True)
        up_grad = nn(n2t[...], hid_grad).astype(BF16)
        dn_grad = nn(olt[...], active).astype(BF16)

        @pl.when(k > 0)
        def _():
            for stage in (1, 2):
                left(f_any(stage), gf_s.at[stage, home])

        @pl.when((k > 0) & (r - nblk < WIDE_FROM))
        def _():
            left(f_any(0), gf_s.at[0, home])

        fg[g, 0] = up_grad
        fg[g, 1] = dn_grad

        @pl.when(r == 3 * nblk - 1)
        def _():
            for m in range(n_far):
                zf(1 + m % (parts - 1), m // (parts - 1)).wait_send()

        @pl.when(r >= SLOTS_C)
        def _():
            pl.semaphore_wait(credit, 1)

        slot = odd(r, n_all)
        rf(0, r, slot).start()

        @pl.when(r > 0)
        def _():
            rf_core(r - 1, 1 - slot)

        return advance("r", r, carry)

    lax.fori_loop(0, n_all, ffn, begin("r"))
    rf_core(n_all - 1, (n_all - 1) % SLOTS_C)

    middle = mid[...]
    ngs[...] = (middle + (acc0[...] + bdn_ref[...][None, :])).astype(BF16)
    lo_copy = pltpu.make_async_copy(ngs, lo_ref, loc_sem.at[2 * nblk])
    lo_copy.start()
    unit, scale_inv = unit_of(middle)
    got = acc1[...]
    early[0:1, :] = jnp.sum(got * unit, axis=0, keepdims=True)
    early[1:2, :] = jnp.sum(got, axis=0, keepdims=True)
    middle_part = norm_back(got, unit, scale_inv, g2_ref[...][None, :])
    reload = pltpu.make_async_copy(cot_ref, ol, loc_sem.at[0])
    reload.start()
    reload.wait()
    out_grad = ol[...].astype(F32) * row_weight
    middle_grad = out_grad + middle_part
    mid[...] = middle_grad
    branch_low = middle_grad.astype(BF16)
    early[2:3, :] = jnp.sum(branch_low.astype(F32), axis=0, keepdims=True)
    ol[...] = branch_low

    for k in range(1, parts):
        for a in range(2):
            za(k, a).wait_send()
            for stage in range(3):
                left(a_any(stage, a), ga_s.at[stage, a, far(k)])
    advance("ln")

    head_row = lax.broadcasted_iota(jnp.int32, (hw, 128), 0)
    head_col = (lax.broadcasted_iota(jnp.int32, (hw, 128), 1) - at2) * HD
    pick = jnp.where((head_row >= head_col) & (head_row < head_col + HD), 1.0, 0.0).astype(BF16)

    def out_back(k, carry):
        s = far(k)
        mixed = mx[s, :, 0:hw]
        mixed_grad = nt(ol[...], aw[s, qkvw : 4 * hw, :]).astype(BF16)
        dmx[s, :, 0:hw] = mixed_grad
        prod = mixed_grad.astype(F32) * mixed.astype(F32)
        coarse = prod.astype(BF16)
        fine = (prod - coarse.astype(F32)).astype(BF16)
        delta = nn(coarse, pick) + nn(fine, pick)
        stat[s] = jnp.where((lane_n >= at2) & (lane_n < at2 + heads), delta, stat[s])
        aw[s, qkvw : 4 * hw, :] = nn(mixed.T, ol[...]).astype(BF16)
        return advance("k", k, carry)

    lax.fori_loop(0, parts, out_back, begin("k"))

    def p_in(s, h, half, buf):
        return pltpu.make_async_copy(
            ph_ref.at[s * heads + h, half], pst.at[buf, h], ps_sem.at[buf, h]
        )

    def fetch(it):
        for h in range(heads):
            p_in(group_of(it), h, 1 - quotient(it, parts, 2 * parts), odd(it, 2 * parts)).start()

    def att_group(it, half):
        s = group_of(it)
        base = half * share
        buf = odd(it, 2 * parts)

        @pl.when(it + 1 < 2 * parts)
        def _():
            fetch(it + 1)

        for h in range(heads):
            p_in(s, h, half, buf).wait()
        known = stat[s]
        wanted = known if half == 0 else pltpu.roll(known, 96, 1)
        delta = -(pltpu.roll(known, 64, 1) * wanted)
        coarse = delta.astype(BF16).astype(F32)
        aux = jnp.where((lane_n >= at0) & (lane_n < at0 + heads), coarse, 0.0)
        aux = jnp.where(
            (lane_n >= at0 + 8) & (lane_n < at0 + 8 + heads), pltpu.roll(delta - coarse, 8, 1), aux
        )
        scaled = dmx[s].astype(F32) * spread(wanted, at0)
        dg = jnp.concatenate(
            [scaled[:, 0:128], jnp.where(lane_n < at0, scaled[:, 128:256], aux)], axis=1
        ).astype(BF16)
        qg = qb[s]
        kg = kb[s, base : base + share]
        vg = vb[s, base : base + share]
        qt = qg[:, 0:hw].T
        dt = dg[:, 0:hw].T
        dq = jnp.zeros((share, 2 * 128), F32)
        dks = []
        dvs = []
        for h in range(heads):
            head = head_lanes(h)
            aux_h = (lane_w == hw + h) | (lane_w == hw + 8 + h)
            dm = jnp.where(head | aux_h, dg, jnp.zeros_like(dg))
            prob_grad = nt(dm, vg)
            probs = pst[buf, h]
            score_grad = (probs.astype(F32) * prob_grad).astype(BF16)
            dq = jnp.where(head, nn(score_grad, kg), dq)
            dks.append(nn(qt[HD * h : HD * (h + 1)], score_grad))
            dvs.append(nn(dt[HD * h : HD * (h + 1)], probs))
        dqt = (dq[:, 0:hw] * factor).T
        dkt = (jnp.concatenate(dks, axis=0) * math.log(2.0)).astype(BF16)
        dvt = jnp.concatenate(dvs, axis=0).astype(BF16)
        return s, dqt, dkt, dvt

    acc0[...] = jnp.zeros_like(acc0)
    acc1[...] = jnp.zeros_like(acc1)
    dmx_pad = jnp.zeros((share, 2 * 128 - hw), BF16)
    for s in range(parts):
        dmx[s, :, hw : 2 * 128] = dmx_pad
    fetch(0)

    def row_sums(values):
        return jnp.sum(values.astype(F32), axis=0, keepdims=True)

    def pair_half(it, carry):
        s, dqt, dkt, dvt = att_group(it, 1)
        uu[s, 0:hw, 0:share] = dqt.astype(BF16)
        uu[s, hw : 2 * hw, 0:share] = dkt
        uu[s, 2 * hw : qkvw, 0:share] = dvt
        back = uu[s, hw:qkvw, 0:share].T
        acc0[...] += nn(back, aw[s, hw:qkvw, :])
        late[pl.ds(2 * s + 1, 1), 0:hw] = row_sums(back[:, hw : 2 * hw])
        return advance("h", it, carry)

    lax.fori_loop(0, parts, pair_half, begin("h"))

    ng_copy = rcopy(ngs, ngr, ng_sem.at[0], ng_sem.at[1], (d, tp))
    pair_grad = acc0[...]
    lo_copy.wait()
    ngs[...] = pair_grad.astype(BF16)
    if NG_PLACE == 0:
        ng_copy.start()
    unit, _ = unit_of(xp[...].astype(F32))
    late[8:9, :] = jnp.sum(pair_grad * unit, axis=0, keepdims=True)
    late[9:10, :] = jnp.sum(pair_grad, axis=0, keepdims=True)

    stages = (dev_c, (dx, t), (dy, t))

    def vec(which, stage):
        buf, rx = (early, e_rx) if which == 0 else (late, l_rx)
        return rcopy(buf, rx.at[stage], sm_s.at[which, stage], sm_r.at[which, stage], stages[stage])

    def vec_far(which, k):
        rz = e_rz if which == 0 else l_rz
        return rcopy(
            rz.at[t], rz.at[t], sm_s.at[which, 2 + k], sm_r.at[which, 3 + t], (d, far(k))
        )

    def vec_next(which, stage):
        buf, rx = (early, e_rx) if which == 0 else (late, l_rx)
        vec(which, stage).wait_recv()
        vec(which, stage).wait_send()
        buf[...] = buf[...] + rx[stage]
        if stage < 2:
            vec(which, stage + 1).start()
        else:
            rz = e_rz if which == 0 else l_rz
            rz[t] = buf[...]
            for k in range(1, parts):
                vec_far(which, k).start()

    vec(0, 0).start()

    def own_half(it, carry):
        q = it - parts
        s, dqt, dkt, dvt = att_group(it, 0)
        dqt = (uu[s, 0:hw, 0:share].astype(F32) + dqt).astype(BF16)
        dd[0:hw, :] = dqt
        dd[hw : 2 * hw, :] = dkt
        dd[2 * hw : qkvw, :] = dvt
        back = dd[...].T
        acc1[...] += nn(back, aw[s, 0:qkvw, :])
        late[pl.ds(2 * s, 1), 0:hw] = row_sums(back[:, 0:hw])
        late[pl.ds(2 * s + 1, 1), 0:hw] = late[pl.ds(2 * s + 1, 1), 0:hw] + row_sums(
            back[:, 2 * hw : qkvw]
        )
        aw[s, 0:hw, :] = nn(dqt, xn[0:share, :]).astype(BF16)
        aw[s, hw:qkvw, :] = (
            nn(dd[hw:qkvw, :], xn[0:share, :]) + nn(uu[s, hw:qkvw, 0:share], xn[share:keys, :])
        ).astype(BF16)
        for a in range(2):
            ra(0, q, a).start()
        carry = advance("w", q, carry)
        if NG_PLACE > 0:

            @pl.when(q == NG_PLACE - 1)
            def _():
                ng_copy.start()

        for stage in range(3):

            @pl.when(q == stage)
            def _():
                vec_next(0, stage)

        return carry

    lax.fori_loop(parts, 2 * parts, own_half, begin("w"))

    own_grad = acc1[...]
    unit, scale_inv = unit_of(x_ref[...].astype(F32))
    late[8:9, :] = late[8:9, :] + jnp.sum(own_grad * unit, axis=0, keepdims=True)
    late[9:10, :] = late[9:10, :] + jnp.sum(own_grad, axis=0, keepdims=True)
    vec(1, 0).start()
    done = uu.at[0]
    xg_copy = pltpu.make_async_copy(mid, xg_ref, loc_sem.at[nblk])

    def aa(stage, a):
        _, _, first, second = route(t0 if a == 0 else 1 - t0)
        view = done.at[a_rows(stage, t0, a), a_lanes(a)]
        dev = (first, second, dev_c)[stage]
        return rcopy(view, view, aa_s.at[stage, a], aa_r.at[stage, a], dev)

    def att_final():
        for a in range(2):
            mine = a_rows(0, t0, a)
            low = CUTS[a][0]
            high = low + CUTS[a][1]
            total = aw[t, mine, low:high].astype(F32)
            for q in range(parts - 1):
                view = rz_a.at[q, :, a_lanes(a)]
                rcopy(view, view, ra_s.at[3, a, q], ra_r.at[3, a, q], (d, t)).wait_recv()
                total = total + rz_a[q, :, low:high].astype(F32)
            done[mine, low:high] = total.astype(BF16)
            aa(0, a).start()

    def att_round(stage):
        for a in range(2):
            aa(stage - 1, a).wait_recv()
            aa(stage, a).start()

    halves = [
        pltpu.make_async_copy(
            done.at[rows(n * 4 * piece, 4 * piece), :],
            oa_ref.at[rows(n * 4 * piece, 4 * piece), :],
            loc_sem.at[nblk + 1 + 3 * i],
        )
        for i, n in enumerate((c, 1 - c))
    ]

    def rows_final():
        ng_copy.wait_recv()
        grad = own_grad + ngr[...].astype(F32)
        mid[...] = mid[...] + norm_back(grad, unit, scale_inv, gain1)
        xg_copy.start()

    def wrap_up():
        for j in range(nblk):
            af(2, j).wait_recv()
            f_out(j, 0).start()
            if j >= 2:
                f_out(j - 2, 1).wait()
            ol[(j % 2) * BLK : (j % 2 + 1) * BLK, :] = fg[t * nblk + j, 1].T
            f_out(j, 1).start()

        for k in range(1, parts):
            zb(k, 0).wait_send()
            zb(k, 1).wait_send()
        x_copy.wait_send()
        ng_copy.wait_send()

        for j in range(nblk):
            for k in range(1, parts):
                left(f_any(1 if j < EARLY_FAR else 0), fz_s.at[(k - 1) * nblk + j])
        for r in range(n_all):
            if r < nblk or (r - nblk) // (parts - 1) >= EARLY_FAR:
                left(f_any(0), f1_s.at[r])

        def drain_all(r, carry):
            left(f_any(2), cf_s.at[r])
            left(f_any(1), f2_s.at[r])
            return carry

        lax.fori_loop(0, n_all, drain_all, 0)

        def drain_own(j, carry):
            for stage in range(3):
                left(f_any(stage), af_s.at[stage, j])
            return carry

        lax.fori_loop(0, nblk, drain_own, 0)
        for q in range(parts):
            for a in range(2):
                for stage in range(3):
                    left(a_any(2 - stage, a), ra_s.at[stage, a, q])
                if q < parts - 1:
                    left(a_any(0, a), ra_s.at[3, a, q])

    vec_stage = 0
    for name, low, high in TAIL:
        if name == "v":
            vec_next(1, vec_stage)
            vec_stage += 1
        elif name == "aa0":
            att_final()
        elif name == "aa1":
            att_round(1)
        elif name == "aa2":
            wrap_up()
            att_round(2)
            halves[0].start()
        elif name == "ng":
            rows_final()
        else:
            repeat(name, low, high)

    for which in range(2):
        rz = e_rz if which == 0 else l_rz
        for k in range(1, parts):
            s = far(k)
            rcopy(
                rz.at[s], rz.at[s], sm_s.at[which, 3], sm_r.at[which, 3 + s], (d, t)
            ).wait_recv()
    early[...] = ((e_rz[0] + e_rz[1]) + e_rz[2]) + e_rz[3]
    late[...] = ((l_rz[0] + l_rz[1]) + l_rz[2]) + l_rz[3]
    osm_ref[0:4, :] = early[0:4, :]
    osm_ref[4:6, :] = late[8:10, :]
    osm_ref[8:9, :] = late[pl.ds(2 * t, 1), :]
    osm_ref[9:10, :] = late[pl.ds(2 * t + 1, 1), :]
    for j in range(nblk):
        osm_ref[16 + j : 17 + j, :] = early[pl.ds(4 + t * nblk + j, 1), :]

    for a in range(2):
        aa(2, a).wait_recv()
    halves[1].start()
    for k in range(1, parts):
        for which in range(2):
            vec_far(which, k).wait_send()
    for j in range(nblk):
        f_out(j, 0).wait()
    for j in range(nblk - 2, nblk):
        f_out(j, 1).wait()

    halves[0].wait()
    halves[1].wait()
    xg_copy.wait()
    for stage in range(3):
        for a in range(2):
            aa(stage, a).wait_send()


def finish(
    lo,
    xg,
    up,
    dn,
    at,
    sm,
    lo_out,
    xg_out,
    up_out,
    dn_out,
    qkv_out,
    out_out,
    g2_out,
    s2_out,
    bo_out,
    bd_out,
    g1_out,
    s1_out,
    qv_out,
    bup_out,
    lo_b,
    xg_b,
    up_b,
    dn_b,
    at_b,
    up_f,
    dn_f,
    at_f,
    in_sem,
    out_sem,
):
    hw = out_out.shape[0]
    qkvw = qkv_out.shape[0]
    jobs = []
    for n, (src, mid_b, wide, dst) in enumerate(
        ((up, up_b, up_f, up_out), (dn, dn_b, dn_f, dn_out), (at, at_b, at_f, None))
    ):
        size = src.shape[0] // CHUNKS
        for i in range(CHUNKS):
            part = pl.ds(i * size, size)
            if dst is not None:
                to = dst.at[part, :]
            elif (i + 1) * size <= qkvw:
                to = qkv_out.at[part, :]
            else:
                to = out_out.at[pl.ds(i * size - qkvw, size), :]
            jobs.append((src.at[part, :], mid_b.at[part, :], wide.at[part, :], to))
    jobs.append((xg, xg_b, None, xg_out))
    jobs.append((lo, lo_b, None, lo_out))
    ins = [
        pltpu.make_async_copy(job[0], job[1], in_sem.at[i]) for i, job in enumerate(jobs)
    ]
    for cp in ins:
        cp.start()
    for i, ref in enumerate((g2_out, s2_out, bo_out, bd_out, g1_out, s1_out)):
        ref[...] = sm[i]
    qv_out[...] = sm[8:10, 0:hw]
    for j in range(bup_out.shape[0] // BLK):
        bup_out[j * BLK : (j + 1) * BLK] = sm[16 + j, 0:BLK]
    outs = []
    for i, (_, got, wide, dst) in enumerate(jobs):
        ins[i].wait()
        if wide is not None:
            wide[...] = got[...].astype(F32)
        outs.append(pltpu.make_async_copy(got if wide is None else wide, dst, out_sem.at[i]))
        outs[-1].start()
    for cp in outs:
        cp.wait()


def local(
    x_in,
    cotangent,
    lengths,
    bucket_ids,
    bucket_weights,
    ln1_gain,
    ln1_bias,
    w_qkv,
    qv_bias,
    w_out,
    b_out,
    ln2_gain,
    ln2_bias,
    w_up,
    b_up,
    w_down,
    b_down,
):
    share, width = x_in.shape
    hw = w_qkv.shape[2]
    heads = hw // HD
    parts = 4
    fw = w_up.shape[1]
    nblk = fw // BLK
    piece = width // GROUP
    keys = 2 * share
    n_all = parts * nblk
    n_far = n_all - nblk
    vm = pl.BlockSpec(memory_space=pltpu.VMEM)
    sm = pl.BlockSpec(memory_space=pltpu.SMEM)
    hbm = pl.BlockSpec(memory_space=pl.ANY)
    dma = pltpu.SemaphoreType.DMA
    scratch = [
        pltpu.VMEM((n_all + nblk, 2, width, BLK), BF16),
        pltpu.VMEM((parts, width, 4 * hw), BF16),
        pltpu.VMEM((SLOTS_C, 2, 4 * piece, BLK), BF16),
        pltpu.VMEM((n_all, 2, 2 * piece, BLK), BF16),
        pltpu.VMEM((n_all, 2, piece, BLK), BF16),
        pltpu.VMEM((n_far, 2, 2 * piece, BLK), BF16),
        pltpu.VMEM((parts, 4 * piece, 4 * hw), BF16),
        pltpu.VMEM((parts, 2 * piece, 4 * hw), BF16),
        pltpu.VMEM((parts, piece, 4 * hw), BF16),
        pltpu.VMEM((parts - 1, piece, 4 * hw), BF16),
        pltpu.VMEM((keys, width), BF16),
        pltpu.VMEM((share, width), BF16),
        pltpu.VMEM((parts, share, 256), BF16),
        pltpu.VMEM((parts, keys, 256), BF16),
        pltpu.VMEM((parts, keys, 256), BF16),
        pltpu.VMEM((parts, share, 256), BF16),
        pltpu.VMEM((parts, share, 256), BF16),
        pltpu.VMEM((parts, share, 128), F32),
        pltpu.VMEM((3 * hw, share), BF16),
        pltpu.VMEM((2, heads, share, share), BF16),
        pltpu.VMEM((share, width), F32),
        pltpu.VMEM((share, width), F32),
        pltpu.VMEM((share, width), F32),
        pltpu.VMEM((parts, width, width), BF16),
        pltpu.VMEM((share, width), BF16),
        pltpu.VMEM((width, share), BF16),
        pltpu.VMEM((share, width), BF16),
        pltpu.VMEM((share, width), BF16),
        pltpu.VMEM((parts, 1, fw), F32),
        pltpu.VMEM((parts, 2, hw), F32),
        pltpu.VMEM((24, width), F32),
        pltpu.VMEM((16, width), F32),
        pltpu.VMEM((3, 24, width), F32),
        pltpu.VMEM((parts, 24, width), F32),
        pltpu.VMEM((3, 16, width), F32),
        pltpu.VMEM((parts, 16, width), F32),
        dma((2 * nblk + 5,)),
        dma((2, heads)),
        dma((2, 3)),
        dma((2, parts)),
        dma((2,)),
        dma((6,)),
        dma((2, parts)),
        dma((3, 2, parts)),
        dma((3, 2, parts)),
        dma((n_far,)),
        dma((n_all,)),
        dma((3, n_all)),
        dma((3, n_all)),
        dma((n_all,)),
        dma((n_all,)),
        dma((n_all,)),
        dma((n_all,)),
        dma((n_all,)),
        dma((n_all,)),
        dma((n_far,)),
        dma((n_far,)),
        dma((3, nblk)),
        dma((3, nblk)),
        dma((4, 2, parts)),
        dma((4, 2, parts)),
        dma((3, 2)),
        dma((3, 2)),
        dma((2, 7)),
        dma((2, 7)),
        dma((2,)),
        pltpu.SemaphoreType.REGULAR,
    ]
    layer_out, x_grad, up, down, att, small, _ = pl.pallas_call(
        kernel,
        out_shape=[
            jax.ShapeDtypeStruct((share, width), BF16),
            jax.ShapeDtypeStruct((share, width), F32),
            jax.ShapeDtypeStruct((width, fw), BF16),
            jax.ShapeDtypeStruct((fw, width), BF16),
            jax.ShapeDtypeStruct((width, width), BF16),
            jax.ShapeDtypeStruct((24, width), F32),
            jax.ShapeDtypeStruct((parts * heads, 2, share, share), BF16),
        ],
        in_specs=[vm, hbm, sm, sm, sm, vm, vm, hbm, vm, hbm, vm, vm, vm, hbm, vm, hbm, vm],
        out_specs=[hbm, hbm, hbm, hbm, hbm, vm, hbm],
        scratch_shapes=scratch,
        compiler_params=pltpu.CompilerParams(
            collective_id=0, has_side_effects=True, vmem_limit_bytes=67043328
        ),
    )(
        x_in,
        cotangent,
        lengths,
        bucket_ids,
        bucket_weights,
        ln1_gain,
        ln1_bias,
        w_qkv.transpose(0, 2, 1),
        qv_bias,
        w_out,
        b_out,
        ln2_gain,
        ln2_bias,
        w_up,
        b_up,
        w_down,
        b_down,
    )
    dp = lax.axis_size("dp")
    if dp > GROUP:
        groups = [[g + GROUP * i for i in range(dp // GROUP)] for g in range(GROUP)]
        sums = lax.psum(
            tuple(g.astype(F32) for g in (up, down, att, small)), "dp", axis_index_groups=groups
        )
        up, down, att = (g.astype(BF16) for g in sums[:3])
        small = sums[3]
    flat = jax.ShapeDtypeStruct((width,), F32)
    outs = pl.pallas_call(
        finish,
        out_shape=[
            jax.ShapeDtypeStruct((share, width), BF16),
            jax.ShapeDtypeStruct((share, width), F32),
            jax.ShapeDtypeStruct((width, fw), F32),
            jax.ShapeDtypeStruct((fw, width), F32),
            jax.ShapeDtypeStruct((3 * hw, width), F32),
            jax.ShapeDtypeStruct((hw, width), F32),
            flat,
            flat,
            flat,
            flat,
            flat,
            flat,
            jax.ShapeDtypeStruct((2, hw), F32),
            jax.ShapeDtypeStruct((fw,), F32),
        ],
        in_specs=[hbm] * 5 + [vm],
        out_specs=[hbm] * 6 + [vm] * 8,
        scratch_shapes=[
            pltpu.VMEM((share, width), BF16),
            pltpu.VMEM((share, width), F32),
            pltpu.VMEM((width, fw), BF16),
            pltpu.VMEM((fw, width), BF16),
            pltpu.VMEM((width, width), BF16),
            pltpu.VMEM((width, fw), F32),
            pltpu.VMEM((fw, width), F32),
            pltpu.VMEM((width, width), F32),
            dma((3 * CHUNKS + 2,)),
            dma((3 * CHUNKS + 2,)),
        ],
    )(layer_out, x_grad, up, down, att, small)
    layer_out, x_grad, g_up, g_down, g_qkv, g_out, g2, s2, bo, bd, g1, s1, g_qv, g_bup = outs
    return (
        layer_out,
        x_grad,
        g1,
        s1,
        g_qkv.reshape(3, hw, width).transpose(0, 2, 1),
        g_qv,
        g_out,
        bo,
        g2,
        s2,
        g_up,
        g_bup,
        g_down,
        bd,
    )


def solution(mesh):
    return jax.shard_map(
        local,
        mesh=mesh,
        in_specs=(
            P(("dp", "tensor"), None),
            P(("dp", "tensor"), None),
            P("dp", None),
            P("dp"),
            P(),
            P(),
            P(),
            P(None, None, "tensor"),
            P(None, "tensor"),
            P("tensor", None),
            P(),
            P(),
            P(),
            P(None, "tensor"),
            P("tensor"),
            P("tensor", None),
            P(),
        ),
        out_specs=(
            P(("dp", "tensor"), None),
            P(("dp", "tensor"), None),
            P(),
            P(),
            P(None, None, "tensor"),
            P(None, "tensor"),
            P("tensor", None),
            P(),
            P(),
            P(),
            P(None, "tensor"),
            P("tensor"),
            P("tensor", None),
            P(),
        ),
        check_vma=False,
    )
```
